256 devices in a mesh: gx: 8 (over z_lo, y), gy: 4 (over x), gz: 8 (over z_hi, core).
Axes of the slice: x: 4, y: 4, z: 8 (z_hi: 4, z_lo: 2; z = z_hi * 2 + z_lo), core: 2. Of those that a mesh axis runs over, the one named last changes fastest.
Arguments:
- coordinates: float32 [8, 4, 8, 3, 16, 128], P('gx', 'gy', 'gz'), may hold values from -8 to 168
- neighbours: int32 [8, 4, 8, 16, 128], P('gx', 'gy', 'gz'), may hold values from 0 to 991, as said below
- pair_index: int32 [8, 4, 8, 4, 15360], P('gx', 'gy', 'gz'), may hold values from 0 to 127, as said below
- pair_live: int32 [8, 4, 8, 15360], P('gx', 'gy', 'gz'), may hold values 0 or 1
- basis: bfloat16 [8, 4, 8, 128, 1536], P('gx', 'gy', 'gz'), may hold values from -50 to 50
Outputs:
- next_basis: float32 [8, 4, 8, 128, 1536], P('gx', 'gy', 'gz')
- ritz_matrix: float32 [256, 256], replicated
The draws below stay inside these ranges and needn't reach their ends.
Inputs may be any that keep to these rules, and one draw needn't show every extreme that they name: neighbours[x, y, z, 0, f] = 864 + f. Any other entry c < 864 names frame c % 32 of the domain offset by (c // 32 // 9 - 1, c // 32 // 3 % 3 - 1, c // 32 % 3 - 1), which lies in the grid and is not the domain itself; an entry c >= 864 names the domain's own frame c - 864, never the row's frame f. `pair_index`: row 0 holds a frame f < 128, row 1 a slot 1 to 15, rows 2 and 3 atoms below 16.
All inputs are finite; a program needn't handle non-finite values. No bound on the sum of `pair_live` on one device may be relied on, other than what follows from the above.
Results may differ from the reference program's by a relative error of at most 0.0003.
Values may be sent and summed in bfloat16 or wider, within the bound.
A program may use at most 128 MiB of HBM per device.

```python
import jax
import jax.numpy as jnp
from jax import lax

K = 256
F_DEV = 128
APF = 16
NBR = 16
BND = 32
PAIRS = 15360
GRID_X = 8
GRID_Y = 4
GRID_Z = 8
NROWS = 196608


def draw_coordinates(key, part):
    centre_key = jax.random.fold_in(key, 11)
    offset_key = jax.random.fold_in(key, 12)
    anchor = jnp.stack(jnp.meshgrid(jnp.arange(GRID_X), jnp.arange(GRID_Y), jnp.arange(GRID_Z), indexing='ij'), axis=3).astype(jnp.float32)
    centres = (anchor[:, :, :, :, None, None] + jax.random.uniform(centre_key, (GRID_X, GRID_Y, GRID_Z, 3, 1, F_DEV))) * 20.0
    offsets = 2.0 * jnp.clip(jax.random.normal(offset_key, (GRID_X, GRID_Y, GRID_Z, 3, APF, F_DEV)), -4.0, 4.0)
    return centres + offsets


def draw_neighbours(key, part):
    full_shape = (GRID_X, GRID_Y, GRID_Z, NBR, F_DEV)
    step_x = jax.random.randint(jax.random.fold_in(key, 21), full_shape, -1, 2)
    step_y = jax.random.randint(jax.random.fold_in(key, 22), full_shape, -1, 2)
    step_z = jax.random.randint(jax.random.fold_in(key, 23), full_shape, -1, 2)
    grid_x = jnp.arange(GRID_X, dtype=jnp.int32)[:, None, None, None, None]
    grid_y = jnp.arange(GRID_Y, dtype=jnp.int32)[None, :, None, None, None]
    grid_z = jnp.arange(GRID_Z, dtype=jnp.int32)[None, None, :, None, None]
    inside = (grid_x + step_x >= 0) & (grid_x + step_x < GRID_X)
    inside = inside & (grid_y + step_y >= 0) & (grid_y + step_y < GRID_Y)
    inside = inside & (grid_z + step_z >= 0) & (grid_z + step_z < GRID_Z)
    inside = inside & ((step_x != 0) | (step_y != 0) | (step_z != 0))
    ghost_frame = jax.random.randint(jax.random.fold_in(key, 24), full_shape, 0, BND)
    ghost_column = ((step_x + 1) * 9 + (step_y + 1) * 3 + (step_z + 1)) * BND + ghost_frame
    frame_ids = jnp.arange(F_DEV, dtype=jnp.int32)[None, None, None, None, :]
    other_frame = jax.random.randint(jax.random.fold_in(key, 25), full_shape, 1, F_DEV)
    local_column = 27 * BND + (frame_ids + other_frame) % F_DEV
    choose = jax.random.randint(jax.random.fold_in(key, 26), full_shape, 0, 2) == 0
    picked = jnp.where(choose & inside, ghost_column, local_column)
    slot_ids = jnp.arange(NBR, dtype=jnp.int32)[None, None, None, :, None]
    own_column = 27 * BND + frame_ids + jnp.zeros(full_shape, jnp.int32)
    return jnp.where(slot_ids == 0, own_column, picked).astype(jnp.int32)


def draw_pair_index(key, part):
    full_shape = (GRID_X, GRID_Y, GRID_Z, PAIRS)
    own_frame = jax.random.randint(jax.random.fold_in(key, 31), full_shape, 0, F_DEV)
    slot_of = jax.random.randint(jax.random.fold_in(key, 32), full_shape, 1, NBR)
    atom_a = jax.random.randint(jax.random.fold_in(key, 33), full_shape, 0, APF)
    atom_b = jax.random.randint(jax.random.fold_in(key, 34), full_shape, 0, APF)
    return jnp.stack([own_frame, slot_of, atom_a, atom_b], axis=3).astype(jnp.int32)


def draw_basis(key, part):
    scale_key = jax.random.fold_in(key, 41)
    value_key = jax.random.fold_in(key, 42)
    column_scale = jnp.exp(jax.random.uniform(scale_key, (GRID_X, GRID_Y, GRID_Z, 1, 6, K), minval=0.0, maxval=2.302585))
    values = column_scale * jnp.clip(jax.random.normal(value_key, (GRID_X, GRID_Y, GRID_Z, F_DEV, 6, K)), -4.0, 4.0)
    return values.reshape(GRID_X, GRID_Y, GRID_Z, F_DEV, 6 * K).astype(jnp.bfloat16)


def set_ends(entries, rng, smallest, largest):
    extent = entries.shape
    place = [jax.random.randint(jax.random.fold_in(rng, axis), (), 0, extent[axis]) for axis in range(len(extent))]
    entries = entries.at[tuple(place)].set(smallest)
    longest = extent.index(max(extent))
    place[longest] = (place[longest] + 1) % extent[longest]
    return entries.at[tuple(place)].set(largest)


def setup_inputs(seed: int = 0) -> dict:
    keys = jax.random.split(jax.random.key(seed), 6)
    return {
        "coordinates": draw_coordinates(jax.random.fold_in(keys[5], 71), 0),
        "neighbours": draw_neighbours(jax.random.fold_in(keys[5], 71), 0),
        "pair_index": draw_pair_index(jax.random.fold_in(keys[5], 71), 0),
        "pair_live": set_ends((jax.random.randint(keys[3], (GRID_X, GRID_Y, GRID_Z, PAIRS), 0, 4) < 3).astype(jnp.int32), jax.random.fold_in(keys[3], 1), 0, 1),
        "basis": draw_basis(jax.random.fold_in(keys[5], 71), 0),
    }


stiffness = 0.01

def cross_product(left, right):
    return jnp.stack([left[1] * right[2] - left[2] * right[1], left[2] * right[0] - left[0] * right[2], left[0] * right[1] - left[1] * right[0]])

def assemble(visible, neighbours, pair_index, pair_live):
    columns = visible.shape[2]
    frames = neighbours.shape[1]
    slots = neighbours.shape[0]
    centres = jnp.mean(visible, axis=1)
    own_frame = pair_index[0]
    slot_of = pair_index[1]
    atom_a = pair_index[2]
    atom_b = pair_index[3]
    self_column = own_frame + (columns - frames)
    partner = jnp.take(neighbours.reshape(-1), slot_of * frames + own_frame, axis=0)
    flat_coords = visible.reshape(3, -1)
    pos_a = jnp.take(flat_coords, atom_a * columns + self_column, axis=1)
    pos_b = jnp.take(flat_coords, atom_b * columns + partner, axis=1)
    arm_a = pos_a - jnp.take(centres, self_column, axis=1)
    arm_b = pos_b - jnp.take(centres, partner, axis=1)
    spring = pos_a - pos_b
    length_sq = jnp.maximum(jnp.sum(spring * spring, axis=0), 1.0)
    weight = stiffness * pair_live.astype(jnp.float32) / length_sq
    left_vec = jnp.concatenate([spring, cross_product(arm_a, spring)], axis=0)
    right_vec = jnp.concatenate([spring, cross_product(arm_b, spring)], axis=0)
    off_terms = -(weight * left_vec)[:, None, :] * right_vec[None, :, :]
    self_terms = (weight * left_vec)[:, None, :] * left_vec[None, :, :]
    values = jnp.concatenate([off_terms.reshape(36, -1).T, self_terms.reshape(36, -1).T], axis=0)
    row_keys = jnp.concatenate([slot_of * frames + own_frame, own_frame], axis=0).astype(jnp.int32)
    blocks = jnp.zeros((slots * frames, 36), jnp.float32).at[row_keys].add(values)
    return blocks.reshape(slots, frames, 36).transpose(0, 2, 1)

def apply_blocks(blocks, neighbours, vector_table):
    frames = neighbours.shape[1]
    vector_count = vector_table.shape[1] // 6

    def add_slot(slot_index, accumulated):
        gathered = jnp.take(vector_table, neighbours[slot_index], axis=0).reshape(frames, 6, vector_count)
        coeffs = blocks[slot_index].reshape(6, 6, frames)
        for inner_dof in range(6):
            accumulated = accumulated + coeffs[:, inner_dof, :].T[:, :, None] * gathered[:, None, inner_dof, :].astype(jnp.float32)
        return accumulated
    start = jnp.zeros((frames, 6, vector_count), jnp.float32)
    accumulated = lax.fori_loop(0, neighbours.shape[0], add_slot, start)
    return accumulated.reshape(frames, 6 * vector_count)

def gram_matrix(left, right):
    return lax.dot_general(left.astype(jnp.float32), right.astype(jnp.float32), (((0,), (0,)), ((), ())), preferred_element_type=jnp.float32)

def rayleigh_ritz(basis_gram, cross_gram, image_gram, image_rows, total_rows):
    factor = jnp.linalg.cholesky(basis_gram / total_rows)
    sym_cross = (cross_gram + cross_gram.T) / (2.0 * total_rows)
    half_solved = lax.linalg.triangular_solve(factor, sym_cross, left_side=True, lower=True)
    ritz_matrix = lax.linalg.triangular_solve(factor, half_solved.T, left_side=True, lower=True)
    image_factor = jnp.linalg.cholesky(image_gram / total_rows)
    next_rows = lax.linalg.triangular_solve(image_factor, image_rows, left_side=False, lower=True, transpose_a=True)
    return (ritz_matrix, next_rows)

def reference(coordinates, neighbours, pair_index, pair_live, basis):
    rim_coords = jnp.pad(coordinates[:, :, :, :, :, :BND], ((1, 1), (1, 1), (1, 1), (0, 0), (0, 0), (0, 0)))
    rim_basis = jnp.pad(basis[:, :, :, :BND, :], ((1, 1), (1, 1), (1, 1), (0, 0), (0, 0)))

    def one_domain(flat_index):
        dom_x = flat_index // (GRID_Y * GRID_Z)
        dom_y = flat_index // GRID_Z % GRID_Y
        dom_z = flat_index % GRID_Z
        zero_index = jnp.zeros((), jnp.int32)
        near_coords = lax.dynamic_slice(rim_coords, (dom_x, dom_y, dom_z, zero_index, zero_index, zero_index), (3, 3, 3, 3, APF, BND))
        near_basis = lax.dynamic_slice(rim_basis, (dom_x, dom_y, dom_z, zero_index, zero_index), (3, 3, 3, BND, 6 * K))
        own_coords = coordinates[dom_x, dom_y, dom_z]
        own_basis = basis[dom_x, dom_y, dom_z]
        own_lists = neighbours[dom_x, dom_y, dom_z]
        visible = jnp.concatenate([near_coords.reshape(27, 3, APF, BND).transpose(1, 2, 0, 3).reshape(3, APF, 27 * BND), own_coords], axis=2)
        vector_table = jnp.concatenate([near_basis.reshape(27 * BND, 6 * K), own_basis], axis=0)
        blocks = assemble(visible, own_lists, pair_index[dom_x, dom_y, dom_z], pair_live[dom_x, dom_y, dom_z])
        image_rows = apply_blocks(blocks, own_lists, vector_table)
        rounded = image_rows.astype(jnp.bfloat16).reshape(F_DEV * 6, K)
        flat_basis = own_basis.reshape(F_DEV * 6, K)
        grams = (gram_matrix(flat_basis, flat_basis), gram_matrix(flat_basis, rounded), gram_matrix(rounded, rounded))
        return (image_rows, grams)
    domain_ids = jnp.arange(GRID_X * GRID_Y * GRID_Z, dtype=jnp.int32)
    images, grams = lax.map(one_domain, domain_ids)
    basis_gram = jnp.sum(grams[0], axis=0)
    cross_gram = jnp.sum(grams[1], axis=0)
    image_gram = jnp.sum(grams[2], axis=0)
    ritz_matrix, next_rows = rayleigh_ritz(basis_gram, cross_gram, image_gram, images.reshape(-1, K), NROWS)
    next_basis = next_rows.reshape(GRID_X, GRID_Y, GRID_Z, F_DEV, 6 * K)
    return (next_basis, ritz_matrix)
```

```python
import functools
import jax
import jax.numpy as jnp
from jax import lax
from jax.experimental import pallas as pl
from jax.experimental.pallas import tpu as pltpu
from jax.sharding import PartitionSpec as P

VM = pl.BlockSpec(memory_space=pltpu.VMEM)
BIG = 60 * 1024 * 1024
F = 128
K = 256
NB = 16
PB = 4096.0
CHUNK = 3840
STEP = 768


def count_body(pairs_ref, live_ref, hist_ref, acc_ref):
    rows = lax.broadcasted_iota(jnp.int32, (256, STEP), 0)
    zero = jnp.zeros((256, STEP), jnp.float32)

    def chunk(c, first):
        def step(t, carry):
            at = pl.ds(pl.multiple_of(c * CHUNK + t * STEP, 128), STEP)
            f = pairs_ref[0:1, at]
            s = pairs_ref[1:2, at]
            a = pairs_ref[2:3, at]
            b = pairs_ref[3:4, at]
            live = live_ref[0:1, at]
            value = (live * jnp.where(a >= 8, int(PB), 1)).astype(jnp.float32)
            col = ((a >> 2) & 1) * 128 + f
            right = jnp.where(rows == col, jnp.broadcast_to(value, (256, STEP)), zero).astype(jnp.bfloat16)
            hot = rows == (b * 16 + s)
            low = a & 3
            for part in range(4):
                mark = jnp.broadcast_to((low == part).astype(jnp.float32), (256, STEP))
                left = jnp.where(hot, mark, zero).astype(jnp.bfloat16)
                got = lax.dot_general(left, right, (((1,), (1,)), ((), ())), preferred_element_type=jnp.float32)
                here = pl.ds(part * 256, 256)
                acc_ref[here, :] = acc_ref[here, :] + got
            return carry

        acc_ref[...] = jnp.zeros_like(acc_ref)
        lax.fori_loop(0, CHUNK // STEP, step, 0)
        for part in range(4):
            got = acc_ref[part * 256 : (part + 1) * 256, :]
            high = jnp.floor(got * (1.0 / PB))
            lower = got - PB * high
            for mid in range(2):
                lanes = slice(mid * 128, (mid + 1) * 128)
                for top, val in ((0, lower), (1, high)):
                    a = top * 8 + mid * 4 + part
                    here = slice(a * 256, (a + 1) * 256)
                    if first:
                        hist_ref[here, :] = val[:, lanes]
                    else:
                        hist_ref[here, :] = hist_ref[here, :] + val[:, lanes]

    chunk(0, True)

    def more(c, carry):
        chunk(c, False)
        return carry

    lax.fori_loop(1, pairs_ref.shape[1] // CHUNK, more, 0)


def count_pairs(pairs, live):
    return pl.pallas_call(
        count_body,
        out_shape=jax.ShapeDtypeStruct((4096, 128), jnp.float32),
        in_specs=[VM, VM],
        out_specs=VM,
        scratch_shapes=[pltpu.VMEM((1024, 256), jnp.float32)],
        compiler_params=pltpu.CompilerParams(vmem_limit_bytes=BIG),
        cost_estimate=pl.CostEstimate(flops=8 * 10**9, bytes_accessed=3 * 10**6, transcendentals=0),
        name="count_pairs",
    )(pairs, live)


def cross(p, q):
    return [
        p[1] * q[2] - p[2] * q[1],
        p[2] * q[0] - p[0] * q[2],
        p[0] * q[1] - p[1] * q[0],
    ]


SYM = ((0, 0), (0, 1), (0, 2), (1, 1), (1, 2), (2, 2))


def symmetric(six):
    return [[six[0], six[1], six[2]], [six[1], six[3], six[4]], [six[2], six[4], six[5]]]


def moments(hist_ref, coords_ref, q_ref, blk_ref, rr_ref):
    blk_ref[...] = jnp.zeros_like(blk_ref)
    rr_ref[...] = jnp.zeros_like(rr_ref)
    own = [jnp.sum(coords_ref[16 * c : 16 * c + 16, :], axis=0, keepdims=True) * (1.0 / 16.0) for c in range(3)]
    for half in range(2):
        def tile(c, b):
            return q_ref[(c * 16 + b) * 16 + half * 8 : (c * 16 + b) * 16 + half * 8 + 8, :]

        centre = []
        for c in range(3):
            total = tile(c, 0)
            for b in range(1, 16):
                total = total + tile(c, b)
            centre.append(total * (1.0 / 16.0))

        def atom(a, carry):
            r = [jnp.broadcast_to(coords_ref[pl.ds(c * 16 + a, 1), :], (8, F)) for c in range(3)]
            arm = [r[c] - jnp.broadcast_to(own[c], (8, F)) for c in range(3)]
            m = [None] * 6
            n = [[None] * 3 for _ in range(3)]
            for b in range(16):
                q = [tile(c, b) for c in range(3)]
                d = [r[c] - q[c] for c in range(3)]
                count = hist_ref[pl.ds(pl.multiple_of(a * 256 + b * 16 + half * 8, 8), 8), :]
                w = (0.01 * count) / jnp.maximum(d[0] * d[0] + d[1] * d[1] + d[2] * d[2], 1.0)
                wd = [w * d[c] for c in range(3)]
                turn = cross([q[c] - centre[c] for c in range(3)], d)
                for k, (j, i) in enumerate(SYM):
                    t = wd[j] * d[i]
                    m[k] = t if m[k] is None else m[k] + t
                for j in range(3):
                    for i in range(3):
                        t = wd[j] * turn[i]
                        n[j][i] = t if n[j][i] is None else n[j][i] + t
            m = symmetric(m)
            rt = [cross(arm, [m[j][i] for j in range(3)]) for i in range(3)]
            rn = [cross(arm, [n[j][i] for j in range(3)]) for i in range(3)]
            for j in range(3):
                for i in range(3):
                    for jj, ii, val in ((j, i, m[j][i]), (j, 3 + i, n[j][i]), (3 + j, i, rt[i][j]), (3 + j, 3 + i, rn[i][j])):
                        here = pl.ds((jj * 6 + ii) * 16 + half * 8, 8)
                        blk_ref[here, :] = blk_ref[here, :] - val
            for j in range(3):
                rr = cross(arm, [rt[i][j] for i in range(3)])
                for i in range(3):
                    here = pl.ds((j * 3 + i) * 8, 8)
                    rr_ref[here, :] = rr_ref[here, :] + rr[i]
            return carry

        lax.fori_loop(0, 16, atom, 0)
    for j in range(3):
        for i in range(3):
            tt = jnp.sum(blk_ref[pl.ds((j * 6 + i) * 16, 16), :], axis=0, keepdims=True)
            rt = jnp.sum(blk_ref[pl.ds(((3 + j) * 6 + i) * 16, 16), :], axis=0, keepdims=True)
            rr = jnp.sum(rr_ref[pl.ds((j * 3 + i) * 8, 8), :], axis=0, keepdims=True)
            for jj, ii, val in ((j, i, -tt), (3 + j, i, -rt), (i, 3 + j, -rt), (3 + j, 3 + i, rr)):
                here = pl.ds((jj * 6 + ii) * 16, 1)
                rr_ref[72 + jj * 6 + ii : 73 + jj * 6 + ii, :] = val
    for ji in range(36):
        here = pl.ds(ji * 16, 1)
        blk_ref[here, :] = blk_ref[here, :] + rr_ref[72 + ji : 73 + ji, :]


KC = 32


def apply_body(hist_ref, table_ref, lists_ref, coords_ref, image_ref, gram_ref, hot_ref, q_ref, g_ref, blk_ref, rr_ref, it_ref, x_ref, y_ref):
    cols = table_ref.shape[0]
    for s in range(NB):
        near = jnp.broadcast_to(lists_ref[s : s + 1, :], (cols, F))
        hot = lax.broadcasted_iota(jnp.int32, (cols, F), 0) == near
        hot_ref[:, s * F : (s + 1) * F] = jnp.where(hot, 1.0, 0.0).astype(jnp.bfloat16)

    def gather(lo, hi):
        return lax.dot_general(table_ref[:, lo:hi], hot_ref[...], (((0,), (0,)), ((), ())), preferred_element_type=jnp.float32)

    got = gather(6 * K, 6 * K + 256)
    pos = got[0:48] + got[48:96] + got[96:144]
    for s in range(NB):
        for t in range(6):
            q_ref[pl.ds(t * 128 + s, 8, stride=16), :] = pos[t * 8 : t * 8 + 8, s * F : (s + 1) * F]
    moments(hist_ref, coords_ref, q_ref, blk_ref, rr_ref)
    for i in range(6):
        g_ref[i * K : (i + 1) * K, :] = gather(i * K, (i + 1) * K)

    def piece(kc, carry):
        start = pl.multiple_of(kc * KC, KC)
        totals = [jnp.zeros((KC, F), jnp.float32) for _ in range(6)]
        for s in range(NB):
            for i in range(6):
                g = g_ref[pl.ds(i * K + start, KC), s * F : (s + 1) * F]
                for j in range(6):
                    row = (j * 6 + i) * 16 + s
                    totals[j] = totals[j] + jnp.broadcast_to(blk_ref[row : row + 1, :], (KC, F)) * g
        for j in range(6):
            it_ref[pl.ds(j * K + start, KC), :] = totals[j]
        return carry

    lax.fori_loop(0, K // KC, piece, 0)
    own = cols - F
    for j in range(6):
        y = jnp.transpose(it_ref[j * K : (j + 1) * K, :])
        image_ref[j * F : (j + 1) * F, :] = y
        y_ref[j * F : (j + 1) * F, :] = y.astype(jnp.bfloat16)
        x_ref[j * F : (j + 1) * F, :] = table_ref[own:cols, j * K : (j + 1) * K]
    for n, (p, q) in enumerate(((x_ref, x_ref), (x_ref, y_ref), (y_ref, y_ref))):
        gram = lax.dot_general(p[...], q[...], (((0,), (0,)), ((), ())), preferred_element_type=jnp.float32)
        gram_ref[n * K : (n + 1) * K, :] = gram


def apply_pairs(hist, table, lists, coords):
    cols = table.shape[0]
    return pl.pallas_call(
        apply_body,
        out_shape=(jax.ShapeDtypeStruct((6 * F, K), jnp.float32), jax.ShapeDtypeStruct((3 * K, K), jnp.float32)),
        in_specs=[VM] * 4,
        out_specs=(VM, VM),
        scratch_shapes=[
            pltpu.VMEM((cols, NB * F), jnp.bfloat16),
            pltpu.VMEM((768, F), jnp.float32),
            pltpu.VMEM((6 * K, NB * F), jnp.float32),
            pltpu.VMEM((576, F), jnp.float32),
            pltpu.VMEM((112, F), jnp.float32),
            pltpu.VMEM((6 * K, F), jnp.float32),
            pltpu.VMEM((6 * F, K), jnp.bfloat16),
            pltpu.VMEM((6 * F, K), jnp.bfloat16),
        ],
        compiler_params=pltpu.CompilerParams(vmem_limit_bytes=BIG),
        cost_estimate=pl.CostEstimate(flops=8 * 10**9, bytes_accessed=8 * 10**6, transcendentals=0),
        name="apply_pairs",
    )(hist, table, lists, coords)


def three_parts(rows):
    def cut(x):
        return lax.reduce_precision(x, 8, 7)

    high = cut(rows)
    mid = cut(rows - high)
    low = rows - high - mid
    return jnp.concatenate([high.astype(jnp.bfloat16), mid.astype(jnp.bfloat16), low.astype(jnp.bfloat16)], axis=1)


def extended(basis, coords):
    frames = basis.shape[0]
    flat = coords.reshape(48, frames).T
    parts = three_parts(flat)
    return jnp.concatenate([basis, parts, jnp.zeros((frames, 256 - 144), jnp.bfloat16)], axis=1)

MESH = pl.DeviceIdType.MESH


def place():
    gx, gy, gz = lax.axis_index("gx"), lax.axis_index("gy"), lax.axis_index("gz")
    y, z = lax.rem(gx, 4), lax.div(gz, 2) * 2 + lax.div(gx, 4)
    return gy, y, z, lax.rem(gz, 2)


def device(x, y, z, core):
    return {"gx": lax.rem(z, 2) * 4 + y, "gy": x, "gz": lax.div(z, 2) * 2 + core}


def total_body(gram_ref, out_ref, tail_ref, data, half_in, half, y_in, part, x_in, z_in, t1, t2, t3, t4, send, recv):
    x, y, z, core = place()
    across = [device(x, y, z, 1 - core)]
    along_y = [device(x, lax.rem(y + d, 4), z, core) for d in range(1, 4)]
    along_x = [device(lax.rem(x + d, 4), y, z, core) for d in range(1, 4)]
    along_z = [device(x, y, lax.rem(z + d, 8), core) for d in range(1, 8)]
    barrier = pltpu.get_barrier_semaphore()
    for peer in across + along_y + along_x + along_z:
        pl.semaphore_signal(barrier, inc=1, device_id=peer, device_id_type=MESH)

    lower = lax.broadcasted_iota(jnp.int32, (F, F), 0) >= lax.broadcasted_iota(jnp.int32, (F, F), 1)
    eye = lax.broadcasted_iota(jnp.int32, (F, F), 0) == lax.broadcasted_iota(jnp.int32, (F, F), 1)
    t1[0] = jnp.zeros((8, F), jnp.float32)
    for m in range(3):
        b11 = gram_ref[m * K : m * K + F, 0:F]
        b21 = gram_ref[m * K + F : m * K + K, 0:F]
        b22 = gram_ref[m * K + F : m * K + K, F:K]
        if m == 1:
            b11 = b11 + b11.T
            b21 = b21 + gram_ref[m * K : m * K + F, F:K].T
            b22 = b22 + b22.T
        data[m * 32 : m * 32 + 16] = b21.reshape(16, 8, F)
        data[m * 32 + 16 : m * 32 + 32] = jnp.where(lower, b11, b22).reshape(16, 8, F)
        t1[0, m : m + 1, :] = jnp.sum(jnp.where(eye, b22, 0.0), axis=0, keepdims=True)
    pl.semaphore_wait(barrier, 14)

    count = [0]

    def copy(src, dst, peer):
        n = count[0]
        count[0] += 1
        return pltpu.make_async_remote_copy(src_ref=src, dst_ref=dst, send_sem=send.at[n], recv_sem=recv.at[n], device_id=peer, device_id_type=MESH)

    def run(copies):
        for c in copies:
            c.start()
        for c in copies:
            c.wait()

    run([
        copy(data.at[pl.ds((1 - core) * 48, 48)], half_in, across[0]),
        copy(t1.at[0], t1.at[1], across[0]),
    ])
    half[...] = data[pl.ds(core * 48, 48)] + half_in[...]
    t2[y] = t1[0] + t1[1]
    run(
        [copy(half.at[pl.ds(lax.rem(y + d, 4) * 12, 12)], y_in.at[d - 1], along_y[d - 1]) for d in range(1, 4)]
        + [copy(t2.at[y], t2.at[y], along_y[d - 1]) for d in range(1, 4)]
    )
    part[...] = half[pl.ds(y * 12, 12)] + y_in[0] + y_in[1] + y_in[2]
    t3[x] = t2[0] + t2[1] + t2[2] + t2[3]
    run(
        [copy(part.at[pl.ds(lax.rem(x + d, 4) * 3, 3)], x_in.at[d - 1], along_x[d - 1]) for d in range(1, 4)]
        + [copy(t3.at[x], t3.at[x], along_x[d - 1]) for d in range(1, 4)]
    )
    z_in[z] = part[pl.ds(x * 3, 3)] + x_in[0] + x_in[1] + x_in[2]
    t4[z] = t3[0] + t3[1] + t3[2] + t3[3]
    run(
        [copy(z_in.at[z], z_in.at[z], along_z[d - 1]) for d in range(1, 8)]
        + [copy(t4.at[z], t4.at[z], along_z[d - 1]) for d in range(1, 8)]
    )
    total, tail = z_in[0], t4[0]
    for n in range(1, 8):
        total = total + z_in[n]
        tail = tail + t4[n]
    tail_ref[...] = tail
    mine = core * 48 + y * 12 + x * 3
    out_ref[pl.ds(mine, 3)] = total
    run([copy(out_ref.at[pl.ds(mine, 3)], out_ref.at[pl.ds(mine, 3)], along_x[d - 1]) for d in range(1, 4)])
    mine = core * 48 + y * 12
    run([copy(out_ref.at[pl.ds(mine, 12)], out_ref.at[pl.ds(mine, 12)], along_y[d - 1]) for d in range(1, 4)])
    mine = core * 48
    run([copy(out_ref.at[pl.ds(mine, 48)], out_ref.at[pl.ds(mine, 48)], across[0])])


def total_grams(gram):
    def buf(*shape):
        return pltpu.VMEM((*shape, 8, F), jnp.float32)

    return pl.pallas_call(
        total_body,
        out_shape=(jax.ShapeDtypeStruct((96, 8, F), jnp.float32), jax.ShapeDtypeStruct((8, F), jnp.float32)),
        in_specs=[VM],
        out_specs=(VM, VM),
        scratch_shapes=[
            buf(96), buf(48), buf(48), buf(3, 12), buf(12), buf(3, 3), buf(8, 3), buf(2), buf(4), buf(4), buf(8),
            pltpu.SemaphoreType.DMA((35,)), pltpu.SemaphoreType.DMA((35,)),
        ],
        compiler_params=pltpu.CompilerParams(collective_id=1, has_side_effects=True, vmem_limit_bytes=16 * 1024 * 1024),
        cost_estimate=pl.CostEstimate(flops=10**6, bytes_accessed=2 * 10**6, transcendentals=0),
        name="total_grams",
    )(gram)


def dot32(p, q, dims):
    return lax.dot_general(p, q, (dims, ((), ())), precision=lax.Precision.HIGHEST, preferred_element_type=jnp.float32)


NT = ((1,), (1,))
NN = ((1,), (0,))


def eliminate(mats):
    sub = lax.broadcasted_iota(jnp.int32, (8, F), 0)
    lane = lax.broadcasted_iota(jnp.int32, (8, F), 1)
    tiles = [[m[8 * t : 8 * t + 8, :] for t in range(16)] for m in mats]
    for j in range(F):
        t, r = divmod(j, 8)
        at = lane == j
        for rows in tiles:
            pivot = rows[t]
            inv = 1.0 / jnp.broadcast_to(pivot[r : r + 1, j : j + 1], (8, F))
            scaled = jnp.where(at, 1.0, jnp.broadcast_to(pivot[r : r + 1, :], (8, F))) * inv
            for u in range(t, 16):
                col = jnp.broadcast_to(rows[u][:, j : j + 1], (8, F))
                if u == t:
                    if r == 7:
                        continue
                    below = sub > r
                    rows[u] = jnp.where(at & below, 0.0, rows[u]) - jnp.where(below, col, 0.0) * scaled
                else:
                    rows[u] = jnp.where(at, 0.0, rows[u]) - col * scaled
    out = []
    for rows in tiles:
        full = []
        for t in range(16):
            diag = lane == sub + 8 * t
            d = jnp.sum(jnp.where(diag, rows[t], 0.0), axis=1, keepdims=True)
            keep = jnp.where(lane < sub + 8 * t, rows[t], jnp.where(diag, 1.0, 0.0))
            full.append(keep * jnp.broadcast_to(1.0 / jnp.sqrt(d), (8, F)))
        out.append(jnp.concatenate(full, axis=0))
    return out


def solve_body(sum_ref, tail_ref, image_ref, next_ref, ritz_ref, mat_ref, inv_ref, *, total_rows):
    scale = 1.0 / total_rows
    sub = lax.broadcasted_iota(jnp.int32, (F, F), 0)
    lane = lax.broadcasted_iota(jnp.int32, (F, F), 1)

    def unpack(m, half):
        b21 = sum_ref[m * 32 : m * 32 + 16].reshape(F, F) * half
        both = sum_ref[m * 32 + 16 : m * 32 + 32].reshape(F, F) * half
        flip = both.T
        b11 = jnp.where(sub >= lane, both, flip)
        diag = jnp.broadcast_to(tail_ref[m : m + 1, :] * half, (F, F))
        b22 = jnp.where(sub < lane, both, jnp.where(sub == lane, diag, flip))
        return b11, b21, b22

    s11, s21, s22 = unpack(0, scale)
    w11, w21, w22 = unpack(2, scale)
    mat_ref[0] = s11
    mat_ref[1] = w11
    for n, (b21, b22) in enumerate(((s21, s22), (w21, w22))):
        mat_ref[2 + 2 * n] = b21
        mat_ref[3 + 2 * n] = b22

    def half_step(step, carry):
        s, w = eliminate([mat_ref[0], mat_ref[1]])
        for n, top in enumerate((s, w)):
            inv_ref[2 * step + n] = top

        @pl.when(step == 0)
        def _():
            for n, top in enumerate((s, w)):
                left = dot32(mat_ref[2 + 2 * n], top, NT)
                mat_ref[n] = mat_ref[3 + 2 * n] - dot32(left, left, NT)
                mat_ref[2 + 2 * n] = left

        return carry

    lax.fori_loop(0, 2, half_step, 0)

    def whole(n):
        top, low = inv_ref[n], inv_ref[2 + n]
        corner = -dot32(low, dot32(mat_ref[2 + 2 * n], top, NN), NN)
        return jnp.concatenate(
            [jnp.concatenate([top, jnp.zeros((F, F), jnp.float32)], axis=1), jnp.concatenate([corner, low], axis=1)], axis=0
        )

    q11, q21, q22 = unpack(1, 0.5 * scale)
    cross_sum = jnp.concatenate([jnp.concatenate([q11, q21.T], axis=1), jnp.concatenate([q21, q22], axis=1)], axis=0)
    s_inv = whole(0)
    ritz_ref[...] = dot32(dot32(s_inv, cross_sum, NN), s_inv, NT)
    w_inv = whole(1)
    for j in range(6):
        next_ref[:, j * K : (j + 1) * K] = dot32(image_ref[j * F : (j + 1) * F, :], w_inv, NT)


def solve(sums, tail, image, total_rows):
    return pl.pallas_call(
        functools.partial(solve_body, total_rows=total_rows),
        out_shape=(jax.ShapeDtypeStruct((F, 6 * K), jnp.float32), jax.ShapeDtypeStruct((K, K), jnp.float32)),
        in_specs=[VM] * 3,
        out_specs=(VM, VM),
        scratch_shapes=[pltpu.VMEM((6, F, F), jnp.float32), pltpu.VMEM((4, F, F), jnp.float32)],
        compiler_params=pltpu.CompilerParams(vmem_limit_bytes=BIG),
        name="solve",
    )(sums, tail, image)


def padded(cells, sides):
    for axis, dim in sides:
        count = lax.axis_size(axis)
        ring = [(i, (i + 1) % count) for i in range(count)]
        last = cells.shape[dim] - 1
        head = lax.slice_in_dim(cells, 0, 1, axis=dim)
        tail = lax.slice_in_dim(cells, last, last + 1, axis=dim)
        cells = jnp.concatenate(
            [lax.ppermute(tail, axis, ring), cells, lax.ppermute(head, axis, [(j, i) for i, j in ring])], axis=dim
        )
    return cells


def per_device(coordinates, neighbours, pair_index, pair_live, basis):
    own = coordinates[0, 0, 0].reshape(48, F)
    rows = extended(basis[0, 0, 0], own)
    near = padded(rows[None, None, None, :32], (("gz", 2), ("gy", 1), ("gx", 0)))
    hist = count_pairs(pair_index[0, 0, 0], pair_live[0, 0, 0].reshape(1, -1))
    table = jnp.concatenate([near.reshape(27 * 32, rows.shape[1]), rows], axis=0)
    image, gram = apply_pairs(hist, table, neighbours[0, 0, 0], own)
    sums, tail = total_grams(gram)
    next_rows, ritz = solve(sums, tail, image, 6.0 * F * 256)
    return next_rows.reshape(1, 1, 1, F, 6 * K), ritz


def solution(mesh):
    cells = [P("gx", "gy", "gz", *([None] * n)) for n in (3, 2, 2, 1, 2)]
    return jax.shard_map(per_device, mesh=mesh, in_specs=tuple(cells), out_specs=(cells[4], P()), check_vma=False)
```

```python
import functools
import jax
import jax.numpy as jnp
from jax import lax
from jax.experimental import pallas as pl
from jax.experimental.pallas import tpu as pltpu
from jax.sharding import PartitionSpec as P

VM = pl.BlockSpec(memory_space=pltpu.VMEM)
BIG = 60 * 1024 * 1024
F = 128
K = 256
NB = 16
PB = 4096.0
CHUNK = 3840
STEP = 768


def counter(pairs_ref, live_ref, hist_ref, acc_ref):
    rows = lax.broadcasted_iota(jnp.int32, (256, STEP), 0)
    zero = jnp.zeros((256, STEP), jnp.float32)

    def step(at, carry):
        at = pl.ds(pl.multiple_of(at * STEP, 128), STEP)
        f = pairs_ref[0:1, at]
        s = pairs_ref[1:2, at]
        a = pairs_ref[2:3, at]
        b = pairs_ref[3:4, at]
        live = live_ref[0:1, at]
        value = (live * jnp.where(a >= 8, int(PB), 1)).astype(jnp.float32)
        col = ((a >> 2) & 1) * 128 + f
        right = jnp.where(rows == col, jnp.broadcast_to(value, (256, STEP)), zero).astype(jnp.bfloat16)
        hot = rows == (b * 16 + s)
        low = a & 3
        for part in range(4):
            mark = jnp.broadcast_to((low == part).astype(jnp.float32), (256, STEP))
            left = jnp.where(hot, mark, zero).astype(jnp.bfloat16)
            got = lax.dot_general(left, right, (((1,), (1,)), ((), ())), preferred_element_type=jnp.float32)
            here = pl.ds(part * 256, 256)
            acc_ref[here, :] = acc_ref[here, :] + got
        return carry

    def chunk(c):
        acc_ref[...] = jnp.zeros_like(acc_ref)
        steps = CHUNK // STEP
        lax.fori_loop(c * steps, (c + 1) * steps, step, 0)
        for part in range(4):
            got = acc_ref[part * 256 : (part + 1) * 256, :]
            high = jnp.floor(got * (1.0 / PB))
            lower = got - PB * high
            for mid in range(2):
                lanes = slice(mid * 128, (mid + 1) * 128)
                for top, val in ((0, lower), (1, high)):
                    a = top * 8 + mid * 4 + part
                    here = slice(a * 256, (a + 1) * 256)
                    if c == 0:
                        hist_ref[here, :] = val[:, lanes]
                    else:
                        hist_ref[here, :] = hist_ref[here, :] + val[:, lanes]

    return chunk


def cross(p, q):
    return [
        p[1] * q[2] - p[2] * q[1],
        p[2] * q[0] - p[0] * q[2],
        p[0] * q[1] - p[1] * q[0],
    ]


SYM = ((0, 0), (0, 1), (0, 2), (1, 1), (1, 2), (2, 2))


def symmetric(six):
    return [[six[0], six[1], six[2]], [six[1], six[3], six[4]], [six[2], six[4], six[5]]]


def moments(hist_ref, coords_ref, q_ref, blk_ref, rr_ref):
    blk_ref[...] = jnp.zeros_like(blk_ref)
    rr_ref[...] = jnp.zeros_like(rr_ref)
    own = [jnp.sum(coords_ref[16 * c : 16 * c + 16, :], axis=0, keepdims=True) * (1.0 / 16.0) for c in range(3)]
    for half in range(2):
        def tile(c, b):
            return q_ref[(c * 16 + b) * 16 + half * 8 : (c * 16 + b) * 16 + half * 8 + 8, :]

        centre = []
        for c in range(3):
            total = tile(c, 0)
            for b in range(1, 16):
                total = total + tile(c, b)
            centre.append(total * (1.0 / 16.0))

        def atom(a, carry):
            r = [jnp.broadcast_to(coords_ref[pl.ds(c * 16 + a, 1), :], (8, F)) for c in range(3)]
            arm = [r[c] - jnp.broadcast_to(own[c], (8, F)) for c in range(3)]
            m = [None] * 6
            n = [[None] * 3 for _ in range(3)]
            for b in range(16):
                q = [tile(c, b) for c in range(3)]
                d = [r[c] - q[c] for c in range(3)]
                count = hist_ref[pl.ds(pl.multiple_of(a * 256 + b * 16 + half * 8, 8), 8), :]
                w = (0.01 * count) / jnp.maximum(d[0] * d[0] + d[1] * d[1] + d[2] * d[2], 1.0)
                wd = [w * d[c] for c in range(3)]
                turn = cross([q[c] - centre[c] for c in range(3)], d)
                for k, (j, i) in enumerate(SYM):
                    t = wd[j] * d[i]
                    m[k] = t if m[k] is None else m[k] + t
                for j in range(3):
                    for i in range(3):
                        t = wd[j] * turn[i]
                        n[j][i] = t if n[j][i] is None else n[j][i] + t
            m = symmetric(m)
            rt = [cross(arm, [m[j][i] for j in range(3)]) for i in range(3)]
            rn = [cross(arm, [n[j][i] for j in range(3)]) for i in range(3)]
            for j in range(3):
                for i in range(3):
                    for jj, ii, val in ((j, i, m[j][i]), (j, 3 + i, n[j][i]), (3 + j, i, rt[i][j]), (3 + j, 3 + i, rn[i][j])):
                        here = pl.ds((jj * 6 + ii) * 16 + half * 8, 8)
                        blk_ref[here, :] = blk_ref[here, :] - val
            for j in range(3):
                rr = cross(arm, [rt[i][j] for i in range(3)])
                for i in range(3):
                    here = pl.ds((j * 3 + i) * 8, 8)
                    rr_ref[here, :] = rr_ref[here, :] + rr[i]
            return carry

        lax.fori_loop(0, 16, atom, 0)
    for j in range(3):
        for i in range(3):
            tt = jnp.sum(blk_ref[pl.ds((j * 6 + i) * 16, 16), :], axis=0, keepdims=True)
            rt = jnp.sum(blk_ref[pl.ds(((3 + j) * 6 + i) * 16, 16), :], axis=0, keepdims=True)
            rr = jnp.sum(rr_ref[pl.ds((j * 3 + i) * 8, 8), :], axis=0, keepdims=True)
            for jj, ii, val in ((j, i, -tt), (3 + j, i, -rt), (i, 3 + j, -rt), (3 + j, 3 + i, rr)):
                here = pl.ds((jj * 6 + ii) * 16, 1)
                rr_ref[72 + jj * 6 + ii : 73 + jj * 6 + ii, :] = val
    for ji in range(36):
        here = pl.ds(ji * 16, 1)
        blk_ref[here, :] = blk_ref[here, :] + rr_ref[72 + ji : 73 + ji, :]


KC = 32


def apply_body(hist_ref, table_ref, lists_ref, coords_ref, image_ref, gram_ref, hot_ref, q_ref, g_ref, blk_ref, rr_ref, it_ref, x_ref, y_ref):
    cols = table_ref.shape[0]
    for s in range(NB):
        near = jnp.broadcast_to(lists_ref[s : s + 1, :], (cols, F))
        hot = lax.broadcasted_iota(jnp.int32, (cols, F), 0) == near
        hot_ref[:, s * F : (s + 1) * F] = jnp.where(hot, 1.0, 0.0).astype(jnp.bfloat16)

    def gather(lo, hi):
        return lax.dot_general(table_ref[:, lo:hi], hot_ref[...], (((0,), (0,)), ((), ())), preferred_element_type=jnp.float32)

    got = gather(6 * K, 6 * K + 256)
    pos = got[0:48] + got[48:96] + got[96:144]
    for s in range(NB):
        for t in range(6):
            q_ref[pl.ds(t * 128 + s, 8, stride=16), :] = pos[t * 8 : t * 8 + 8, s * F : (s + 1) * F]
    moments(hist_ref, coords_ref, q_ref, blk_ref, rr_ref)
    for i in range(6):
        g_ref[i * K : (i + 1) * K, :] = gather(i * K, (i + 1) * K)

    def piece(kc, carry):
        start = pl.multiple_of(kc * KC, KC)
        totals = [jnp.zeros((KC, F), jnp.float32) for _ in range(6)]
        for s in range(NB):
            for i in range(6):
                g = g_ref[pl.ds(i * K + start, KC), s * F : (s + 1) * F]
                for j in range(6):
                    row = (j * 6 + i) * 16 + s
                    totals[j] = totals[j] + jnp.broadcast_to(blk_ref[row : row + 1, :], (KC, F)) * g
        for j in range(6):
            it_ref[pl.ds(j * K + start, KC), :] = totals[j]
        return carry

    lax.fori_loop(0, K // KC, piece, 0)
    own = cols - F
    for j in range(6):
        y = jnp.transpose(it_ref[j * K : (j + 1) * K, :])
        image_ref[j * F : (j + 1) * F, :] = y
        y_ref[j * F : (j + 1) * F, :] = y.astype(jnp.bfloat16)
        x_ref[j * F : (j + 1) * F, :] = table_ref[own:cols, j * K : (j + 1) * K]
    for n, (p, q) in enumerate(((x_ref, x_ref), (x_ref, y_ref), (y_ref, y_ref))):
        gram = lax.dot_general(p[...], q[...], (((0,), (0,)), ((), ())), preferred_element_type=jnp.float32)
        gram_ref[n * K : (n + 1) * K, :] = gram


def apply_pairs(hist, table, lists, coords):
    cols = table.shape[0]
    return pl.pallas_call(
        apply_body,
        out_shape=(jax.ShapeDtypeStruct((6 * F, K), jnp.float32), jax.ShapeDtypeStruct((3 * K, K), jnp.float32)),
        in_specs=[VM] * 4,
        out_specs=(VM, VM),
        scratch_shapes=[
            pltpu.VMEM((cols, NB * F), jnp.bfloat16),
            pltpu.VMEM((768, F), jnp.float32),
            pltpu.VMEM((6 * K, NB * F), jnp.float32),
            pltpu.VMEM((576, F), jnp.float32),
            pltpu.VMEM((112, F), jnp.float32),
            pltpu.VMEM((6 * K, F), jnp.float32),
            pltpu.VMEM((6 * F, K), jnp.bfloat16),
            pltpu.VMEM((6 * F, K), jnp.bfloat16),
        ],
        compiler_params=pltpu.CompilerParams(vmem_limit_bytes=BIG),
        cost_estimate=pl.CostEstimate(flops=8 * 10**9, bytes_accessed=8 * 10**6, transcendentals=0),
        name="apply_pairs",
    )(hist, table, lists, coords)


MESH = pl.DeviceIdType.MESH


def place():
    gx, gy, gz = lax.axis_index("gx"), lax.axis_index("gy"), lax.axis_index("gz")
    y, z = lax.rem(gx, 4), lax.div(gz, 2) * 2 + lax.div(gx, 4)
    return gy, y, z, lax.rem(gz, 2)


def device(x, y, z, core):
    return {"gx": lax.rem(z, 2) * 4 + y, "gy": x, "gz": lax.div(z, 2) * 2 + core}


def total_body(gram_ref, out_ref, tail_ref, data, half_in, half, y_in, part, x_in, z_in, t1, t2, t3, t4, send, recv):
    x, y, z, core = place()
    across = [device(x, y, z, 1 - core)]
    along_y = [device(x, lax.rem(y + d, 4), z, core) for d in range(1, 4)]
    along_x = [device(lax.rem(x + d, 4), y, z, core) for d in range(1, 4)]
    along_z = [device(x, y, lax.rem(z + d, 8), core) for d in range(1, 8)]
    barrier = pltpu.get_barrier_semaphore()
    for peer in across + along_y + along_x + along_z:
        pl.semaphore_signal(barrier, inc=1, device_id=peer, device_id_type=MESH)

    lower = lax.broadcasted_iota(jnp.int32, (F, F), 0) >= lax.broadcasted_iota(jnp.int32, (F, F), 1)
    eye = lax.broadcasted_iota(jnp.int32, (F, F), 0) == lax.broadcasted_iota(jnp.int32, (F, F), 1)
    t1[0] = jnp.zeros((8, F), jnp.float32)
    for m in range(3):
        b11 = gram_ref[m * K : m * K + F, 0:F]
        b21 = gram_ref[m * K + F : m * K + K, 0:F]
        b22 = gram_ref[m * K + F : m * K + K, F:K]
        if m == 1:
            b11 = b11 + b11.T
            b21 = b21 + gram_ref[m * K : m * K + F, F:K].T
            b22 = b22 + b22.T
        data[m * 32 : m * 32 + 16] = b21.reshape(16, 8, F)
        data[m * 32 + 16 : m * 32 + 32] = jnp.where(lower, b11, b22).reshape(16, 8, F)
        t1[0, m : m + 1, :] = jnp.sum(jnp.where(eye, b22, 0.0), axis=0, keepdims=True)
    pl.semaphore_wait(barrier, 14)

    count = [0]

    def copy(src, dst, peer):
        n = count[0]
        count[0] += 1
        return pltpu.make_async_remote_copy(src_ref=src, dst_ref=dst, send_sem=send.at[n], recv_sem=recv.at[n], device_id=peer, device_id_type=MESH)

    def run(copies):
        for c in copies:
            c.start()
        for c in copies:
            c.wait()

    run([
        copy(data.at[pl.ds((1 - core) * 48, 48)], half_in, across[0]),
        copy(t1.at[0], t1.at[1], across[0]),
    ])
    half[...] = data[pl.ds(core * 48, 48)] + half_in[...]
    t2[y] = t1[0] + t1[1]
    run(
        [copy(half.at[pl.ds(lax.rem(y + d, 4) * 12, 12)], y_in.at[d - 1], along_y[d - 1]) for d in range(1, 4)]
        + [copy(t2.at[y], t2.at[y], along_y[d - 1]) for d in range(1, 4)]
    )
    part[...] = half[pl.ds(y * 12, 12)] + y_in[0] + y_in[1] + y_in[2]
    t3[x] = t2[0] + t2[1] + t2[2] + t2[3]
    run(
        [copy(part.at[pl.ds(lax.rem(x + d, 4) * 3, 3)], x_in.at[d - 1], along_x[d - 1]) for d in range(1, 4)]
        + [copy(t3.at[x], t3.at[x], along_x[d - 1]) for d in range(1, 4)]
    )
    z_in[z] = part[pl.ds(x * 3, 3)] + x_in[0] + x_in[1] + x_in[2]
    t4[z] = t3[0] + t3[1] + t3[2] + t3[3]
    run(
        [copy(z_in.at[z], z_in.at[z], along_z[d - 1]) for d in range(1, 8)]
        + [copy(t4.at[z], t4.at[z], along_z[d - 1]) for d in range(1, 8)]
    )
    total, tail = z_in[0], t4[0]
    for n in range(1, 8):
        total = total + z_in[n]
        tail = tail + t4[n]
    tail_ref[...] = tail
    mine = core * 48 + y * 12 + x * 3
    out_ref[pl.ds(mine, 3)] = total
    run([copy(out_ref.at[pl.ds(mine, 3)], out_ref.at[pl.ds(mine, 3)], along_x[d - 1]) for d in range(1, 4)])
    mine = core * 48 + y * 12
    run([copy(out_ref.at[pl.ds(mine, 12)], out_ref.at[pl.ds(mine, 12)], along_y[d - 1]) for d in range(1, 4)])
    mine = core * 48
    run([copy(out_ref.at[pl.ds(mine, 48)], out_ref.at[pl.ds(mine, 48)], across[0])])


def total_grams(gram):
    def buf(*shape):
        return pltpu.VMEM((*shape, 8, F), jnp.float32)

    return pl.pallas_call(
        total_body,
        out_shape=(jax.ShapeDtypeStruct((96, 8, F), jnp.float32), jax.ShapeDtypeStruct((8, F), jnp.float32)),
        in_specs=[VM],
        out_specs=(VM, VM),
        scratch_shapes=[
            buf(96), buf(48), buf(48), buf(3, 12), buf(12), buf(3, 3), buf(8, 3), buf(2), buf(4), buf(4), buf(8),
            pltpu.SemaphoreType.DMA((35,)), pltpu.SemaphoreType.DMA((35,)),
        ],
        compiler_params=pltpu.CompilerParams(collective_id=1, has_side_effects=True, vmem_limit_bytes=16 * 1024 * 1024),
        cost_estimate=pl.CostEstimate(flops=10**6, bytes_accessed=2 * 10**6, transcendentals=0),
        name="total_grams",
    )(gram)


def near_body(pairs_ref, live_ref, basis_ref, coords_ref, hist_ref, table_ref, acc_ref, send, recv):
    gx, gy, gz = lax.axis_index("gx"), lax.axis_index("gy"), lax.axis_index("gz")
    core = lax.rem(gz, 2)
    far = 2 * core
    partner = {"gz": gz + 1 - 2 * core}
    beyond = {"gz": lax.rem(gz + 7 + 2 * core, 8)}
    up_x, down_x = {"gy": lax.rem(gy + 1, 4)}, {"gy": lax.rem(gy + 3, 4)}
    up_y, down_y = {"gx": lax.rem(gx + 1, 8)}, {"gx": lax.rem(gx + 7, 8)}
    barrier = pltpu.get_barrier_semaphore()
    for peer in (partner, beyond, up_x, down_x, up_y, down_y):
        pl.semaphore_signal(barrier, inc=1, device_id=peer, device_id_type=MESH)

    own = 27 * 32
    flat = coords_ref[...]
    high = flat.astype(jnp.bfloat16).astype(jnp.float32)
    mid = (flat - high).astype(jnp.bfloat16).astype(jnp.float32)
    parts = jnp.concatenate([high, mid, flat - high - mid, jnp.zeros((112, F), jnp.float32)], axis=0)
    table_ref[own : own + F, 0 : 6 * K] = basis_ref[...]
    table_ref[own : own + F, 6 * K : 7 * K] = jnp.transpose(parts).astype(jnp.bfloat16)
    table_ref[13 * 32 : 14 * 32, :] = table_ref[own : own + 32, :]
    pl.semaphore_wait(barrier, 6)

    count = [0]

    def slab(a, b, e):
        return table_ref.at[pl.ds(pl.multiple_of((9 * a + 3 * b + e) * 32, 32), 32)]

    def copy(src, dst, peer):
        n = count[0]
        count[0] += 1
        c = pltpu.make_async_remote_copy(src_ref=src, dst_ref=dst, send_sem=send.at[n], recv_sem=recv.at[n], device_id=peer, device_id_type=MESH)
        c.start()
        return c

    def first_hops(e):
        return [
            copy(slab(1, 1, e), slab(1, 0, e), up_x),
            copy(slab(1, 1, e), slab(1, 2, e), down_x),
            copy(slab(1, 1, e), slab(0, 1, e), up_y),
            copy(slab(1, 1, e), slab(2, 1, e), down_y),
        ]

    def second_hops(e):
        return [
            copy(slab(1, 0, e), slab(0, 0, e), up_y),
            copy(slab(1, 2, e), slab(2, 2, e), down_y),
            copy(slab(0, 1, e), slab(0, 2, e), down_x),
            copy(slab(2, 1, e), slab(2, 0, e), up_x),
        ]

    def forward(places):
        return [copy(slab(a, b, 1), slab(a, b, far), partner) for a, b in places]

    edges, corners = ((1, 0), (1, 2), (0, 1), (2, 1)), ((0, 0), (2, 2), (0, 2), (2, 0))
    z_far = copy(slab(1, 1, 1), slab(1, 1, 2 - far), beyond)
    z_near = copy(slab(1, 1, 1), slab(1, 1, far), partner)
    own_first = first_hops(1)
    chunk = counter(pairs_ref, live_ref, hist_ref, acc_ref)
    chunk(0)
    for c in [z_far] + own_first:
        c.wait_recv()
    far_first = first_hops(far)
    own_second = second_hops(1)
    sent = forward(edges)
    chunk(1)
    for c in own_second + far_first:
        c.wait_recv()
    far_second = second_hops(far)
    sent = sent + forward(corners)
    chunk(2)
    chunk(3)
    for c in [z_near] + far_second + sent:
        c.wait_recv()
    for c in [z_far, z_near] + own_first + far_first + own_second + far_second + sent:
        c.wait_send()


def near_and_counts(pairs, live, basis, coords):
    return pl.pallas_call(
        near_body,
        out_shape=(jax.ShapeDtypeStruct((4096, F), jnp.float32), jax.ShapeDtypeStruct((27 * 32 + F, 7 * K), jnp.bfloat16)),
        in_specs=[VM] * 4,
        out_specs=(VM, VM),
        scratch_shapes=[pltpu.VMEM((1024, 256), jnp.float32), pltpu.SemaphoreType.DMA((26,)), pltpu.SemaphoreType.DMA((26,))],
        compiler_params=pltpu.CompilerParams(collective_id=2, has_side_effects=True, vmem_limit_bytes=BIG),
        cost_estimate=pl.CostEstimate(flops=8 * 10**9, bytes_accessed=3 * 10**6, transcendentals=0),
        name="near_and_counts",
    )(pairs, live, basis, coords)


def dot32(p, q, dims):
    return lax.dot_general(p, q, (dims, ((), ())), precision=lax.Precision.HIGHEST, preferred_element_type=jnp.float32)


NT = ((1,), (1,))
NN = ((1,), (0,))


def eliminate(mats):
    sub = lax.broadcasted_iota(jnp.int32, (8, F), 0)
    lane = lax.broadcasted_iota(jnp.int32, (8, F), 1)
    tiles = [[m[8 * t : 8 * t + 8, :] for t in range(16)] for m in mats]
    for j in range(F):
        t, r = divmod(j, 8)
        at = lane == j
        for rows in tiles:
            pivot = rows[t]
            inv = 1.0 / jnp.broadcast_to(pivot[r : r + 1, j : j + 1], (8, F))
            scaled = jnp.where(at, 1.0, jnp.broadcast_to(pivot[r : r + 1, :], (8, F))) * inv
            for u in range(t, 16):
                col = jnp.broadcast_to(rows[u][:, j : j + 1], (8, F))
                if u == t:
                    if r == 7:
                        continue
                    below = sub > r
                    rows[u] = jnp.where(at & below, 0.0, rows[u]) - jnp.where(below, col, 0.0) * scaled
                else:
                    rows[u] = jnp.where(at, 0.0, rows[u]) - col * scaled
    out = []
    for rows in tiles:
        full = []
        for t in range(16):
            diag = lane == sub + 8 * t
            d = jnp.sum(jnp.where(diag, rows[t], 0.0), axis=1, keepdims=True)
            keep = jnp.where(lane < sub + 8 * t, rows[t], jnp.where(diag, 1.0, 0.0))
            full.append(keep * jnp.broadcast_to(1.0 / jnp.sqrt(d), (8, F)))
        out.append(jnp.concatenate(full, axis=0))
    return out


def solve_body(sum_ref, tail_ref, image_ref, next_ref, ritz_ref, mat_ref, inv_ref, *, total_rows):
    scale = 1.0 / total_rows
    sub = lax.broadcasted_iota(jnp.int32, (F, F), 0)
    lane = lax.broadcasted_iota(jnp.int32, (F, F), 1)

    def unpack(m, half):
        b21 = sum_ref[m * 32 : m * 32 + 16].reshape(F, F) * half
        both = sum_ref[m * 32 + 16 : m * 32 + 32].reshape(F, F) * half
        flip = both.T
        b11 = jnp.where(sub >= lane, both, flip)
        diag = jnp.broadcast_to(tail_ref[m : m + 1, :] * half, (F, F))
        b22 = jnp.where(sub < lane, both, jnp.where(sub == lane, diag, flip))
        return b11, b21, b22

    s11, s21, s22 = unpack(0, scale)
    w11, w21, w22 = unpack(2, scale)
    mat_ref[0] = s11
    mat_ref[1] = w11
    for n, (b21, b22) in enumerate(((s21, s22), (w21, w22))):
        mat_ref[2 + 2 * n] = b21
        mat_ref[3 + 2 * n] = b22

    def half_step(step, carry):
        s, w = eliminate([mat_ref[0], mat_ref[1]])
        for n, top in enumerate((s, w)):
            inv_ref[2 * step + n] = top

        @pl.when(step == 0)
        def _():
            for n, top in enumerate((s, w)):
                left = dot32(mat_ref[2 + 2 * n], top, NT)
                mat_ref[n] = mat_ref[3 + 2 * n] - dot32(left, left, NT)
                mat_ref[2 + 2 * n] = left

        return carry

    lax.fori_loop(0, 2, half_step, 0)

    def whole(n):
        top, low = inv_ref[n], inv_ref[2 + n]
        corner = -dot32(low, dot32(mat_ref[2 + 2 * n], top, NN), NN)
        return jnp.concatenate(
            [jnp.concatenate([top, jnp.zeros((F, F), jnp.float32)], axis=1), jnp.concatenate([corner, low], axis=1)], axis=0
        )

    q11, q21, q22 = unpack(1, 0.5 * scale)
    cross_sum = jnp.concatenate([jnp.concatenate([q11, q21.T], axis=1), jnp.concatenate([q21, q22], axis=1)], axis=0)
    s_inv = whole(0)
    ritz_ref[...] = dot32(dot32(s_inv, cross_sum, NN), s_inv, NT)
    w_inv = whole(1)
    for j in range(6):
        next_ref[:, j * K : (j + 1) * K] = dot32(image_ref[j * F : (j + 1) * F, :], w_inv, NT)


def solve(sums, tail, image, total_rows):
    return pl.pallas_call(
        functools.partial(solve_body, total_rows=total_rows),
        out_shape=(jax.ShapeDtypeStruct((F, 6 * K), jnp.float32), jax.ShapeDtypeStruct((K, K), jnp.float32)),
        in_specs=[VM] * 3,
        out_specs=(VM, VM),
        scratch_shapes=[pltpu.VMEM((6, F, F), jnp.float32), pltpu.VMEM((4, F, F), jnp.float32)],
        compiler_params=pltpu.CompilerParams(vmem_limit_bytes=BIG),
        name="solve",
    )(sums, tail, image)


def per_device(coordinates, neighbours, pair_index, pair_live, basis):
    own = coordinates[0, 0, 0].reshape(48, F)
    hist, table = near_and_counts(pair_index[0, 0, 0], pair_live[0, 0, 0].reshape(1, -1), basis[0, 0, 0], own)
    image, gram = apply_pairs(hist, table, neighbours[0, 0, 0], own)
    sums, tail = total_grams(gram)
    next_rows, ritz = solve(sums, tail, image, 6.0 * F * 256)
    return next_rows.reshape(1, 1, 1, F, 6 * K), ritz


def solution(mesh):
    cells = [P("gx", "gy", "gz", *([None] * n)) for n in (3, 2, 2, 1, 2)]
    return jax.shard_map(per_device, mesh=mesh, in_specs=tuple(cells), out_specs=(cells[4], P()), check_vma=False)
```

```python
import functools
import jax
import jax.numpy as jnp
from jax import lax
from jax.experimental import pallas as pl
from jax.experimental.pallas import tpu as pltpu
from jax.sharding import PartitionSpec as P

VM = pl.BlockSpec(memory_space=pltpu.VMEM)
F = 128
K = 256
NB = 16
PB = 4096.0
CHUNK = 3840
STEP = 768


def counter(pairs_ref, live_ref, hist_ref, acc_ref):
    rows = lax.broadcasted_iota(jnp.int32, (256, STEP), 0)
    zero = jnp.zeros((256, STEP), jnp.float32)

    def step(at, carry):
        at = pl.ds(pl.multiple_of(at * STEP, 128), STEP)
        f = pairs_ref[0:1, at]
        s = pairs_ref[1:2, at]
        a = pairs_ref[2:3, at]
        b = pairs_ref[3:4, at]
        live = live_ref[0:1, at]
        value = (live * jnp.where(a >= 8, int(PB), 1)).astype(jnp.float32)
        col = ((a >> 2) & 1) * 128 + f
        right = jnp.where(rows == col, jnp.broadcast_to(value, (256, STEP)), zero).astype(jnp.bfloat16)
        hot = rows == (b * 16 + s)
        low = a & 3
        for part in range(4):
            mark = jnp.broadcast_to((low == part).astype(jnp.float32), (256, STEP))
            left = jnp.where(hot, mark, zero).astype(jnp.bfloat16)
            got = lax.dot_general(left, right, (((1,), (1,)), ((), ())), preferred_element_type=jnp.float32)
            here = pl.ds(part * 256, 256)
            acc_ref[here, :] = acc_ref[here, :] + got
        return carry

    def chunk(c):
        acc_ref[...] = jnp.zeros_like(acc_ref)
        steps = CHUNK // STEP
        lax.fori_loop(c * steps, (c + 1) * steps, step, 0)
        for part in range(4):
            got = acc_ref[part * 256 : (part + 1) * 256, :]
            high = jnp.floor(got * (1.0 / PB))
            lower = got - PB * high
            for mid in range(2):
                lanes = slice(mid * 128, (mid + 1) * 128)
                for top, val in ((0, lower), (1, high)):
                    a = top * 8 + mid * 4 + part
                    here = slice(a * 256, (a + 1) * 256)
                    if c == 0:
                        hist_ref[here, :] = val[:, lanes]
                    else:
                        hist_ref[here, :] = hist_ref[here, :] + val[:, lanes]

    return chunk


def cross(p, q):
    return [
        p[1] * q[2] - p[2] * q[1],
        p[2] * q[0] - p[0] * q[2],
        p[0] * q[1] - p[1] * q[0],
    ]


SYM = ((0, 0), (0, 1), (0, 2), (1, 1), (1, 2), (2, 2))


def symmetric(six):
    return [[six[0], six[1], six[2]], [six[1], six[3], six[4]], [six[2], six[4], six[5]]]


def moments(hist_ref, coords_ref, q_ref, blk_ref, rr_ref):
    blk_ref[...] = jnp.zeros_like(blk_ref)
    rr_ref[...] = jnp.zeros_like(rr_ref)
    own = [jnp.sum(coords_ref[16 * c : 16 * c + 16, :], axis=0, keepdims=True) * (1.0 / 16.0) for c in range(3)]
    for half in range(2):
        def tile(c, b):
            return q_ref[(c * 16 + b) * 16 + half * 8 : (c * 16 + b) * 16 + half * 8 + 8, :]

        centre = []
        for c in range(3):
            total = tile(c, 0)
            for b in range(1, 16):
                total = total + tile(c, b)
            centre.append(total * (1.0 / 16.0))

        def atom(a, carry):
            r = [jnp.broadcast_to(coords_ref[pl.ds(c * 16 + a, 1), :], (8, F)) for c in range(3)]
            arm = [r[c] - jnp.broadcast_to(own[c], (8, F)) for c in range(3)]
            m = [None] * 6
            n = [[None] * 3 for _ in range(3)]
            for b in range(16):
                q = [tile(c, b) for c in range(3)]
                d = [r[c] - q[c] for c in range(3)]
                count = hist_ref[pl.ds(pl.multiple_of(a * 256 + b * 16 + half * 8, 8), 8), :]
                w = (0.01 * count) / jnp.maximum(d[0] * d[0] + d[1] * d[1] + d[2] * d[2], 1.0)
                wd = [w * d[c] for c in range(3)]
                turn = cross([q[c] - centre[c] for c in range(3)], d)
                for k, (j, i) in enumerate(SYM):
                    t = wd[j] * d[i]
                    m[k] = t if m[k] is None else m[k] + t
                for j in range(3):
                    for i in range(3):
                        t = wd[j] * turn[i]
                        n[j][i] = t if n[j][i] is None else n[j][i] + t
            m = symmetric(m)
            rt = [cross(arm, [m[j][i] for j in range(3)]) for i in range(3)]
            rn = [cross(arm, [n[j][i] for j in range(3)]) for i in range(3)]
            for j in range(3):
                for i in range(3):
                    for jj, ii, val in ((j, i, m[j][i]), (j, 3 + i, n[j][i]), (3 + j, i, rt[i][j]), (3 + j, 3 + i, rn[i][j])):
                        here = pl.ds((jj * 6 + ii) * 16 + half * 8, 8)
                        blk_ref[here, :] = blk_ref[here, :] - val
            for j in range(3):
                rr = cross(arm, [rt[i][j] for i in range(3)])
                for i in range(3):
                    here = pl.ds((j * 3 + i) * 8, 8)
                    rr_ref[here, :] = rr_ref[here, :] + rr[i]
            return carry

        lax.fori_loop(0, 16, atom, 0)
    for j in range(3):
        for i in range(3):
            tt = jnp.sum(blk_ref[pl.ds((j * 6 + i) * 16, 16), :], axis=0, keepdims=True)
            rt = jnp.sum(blk_ref[pl.ds(((3 + j) * 6 + i) * 16, 16), :], axis=0, keepdims=True)
            rr = jnp.sum(rr_ref[pl.ds((j * 3 + i) * 8, 8), :], axis=0, keepdims=True)
            for jj, ii, val in ((j, i, -tt), (3 + j, i, -rt), (i, 3 + j, -rt), (3 + j, 3 + i, rr)):
                here = pl.ds((jj * 6 + ii) * 16, 1)
                rr_ref[72 + jj * 6 + ii : 73 + jj * 6 + ii, :] = val
    for ji in range(36):
        here = pl.ds(ji * 16, 1)
        blk_ref[here, :] = blk_ref[here, :] + rr_ref[72 + ji : 73 + ji, :]


KC = 32


def apply_body(hist_ref, table_ref, lists_ref, coords_ref, image_ref, gram_ref, hot_ref, q_ref, g_ref, blk_ref, rr_ref, it_ref, x_ref, y_ref):
    cols = table_ref.shape[0]
    for s in range(NB):
        near = jnp.broadcast_to(lists_ref[s : s + 1, :], (cols, F))
        hot = lax.broadcasted_iota(jnp.int32, (cols, F), 0) == near
        hot_ref[:, s * F : (s + 1) * F] = jnp.where(hot, 1.0, 0.0).astype(jnp.bfloat16)

    def gather(lo, hi):
        return lax.dot_general(table_ref[:, lo:hi], hot_ref[...], (((0,), (0,)), ((), ())), preferred_element_type=jnp.float32)

    got = gather(6 * K, 6 * K + 256)
    pos = got[0:48] + got[48:96] + got[96:144]
    for s in range(NB):
        for t in range(6):
            q_ref[pl.ds(t * 128 + s, 8, stride=16), :] = pos[t * 8 : t * 8 + 8, s * F : (s + 1) * F]
    moments(hist_ref, coords_ref, q_ref, blk_ref, rr_ref)
    for i in range(6):
        g_ref[i * K : (i + 1) * K, :] = gather(i * K, (i + 1) * K)

    def piece(kc, carry):
        start = pl.multiple_of(kc * KC, KC)
        totals = [jnp.zeros((KC, F), jnp.float32) for _ in range(6)]
        for s in range(NB):
            for i in range(6):
                g = g_ref[pl.ds(i * K + start, KC), s * F : (s + 1) * F]
                for j in range(6):
                    row = (j * 6 + i) * 16 + s
                    totals[j] = totals[j] + jnp.broadcast_to(blk_ref[row : row + 1, :], (KC, F)) * g
        for j in range(6):
            it_ref[pl.ds(j * K + start, KC), :] = totals[j]
        return carry

    lax.fori_loop(0, K // KC, piece, 0)
    own = cols - F
    for j in range(6):
        y = jnp.transpose(it_ref[j * K : (j + 1) * K, :])
        image_ref[j * F : (j + 1) * F, :] = y
        y_ref[j * F : (j + 1) * F, :] = y.astype(jnp.bfloat16)
        x_ref[j * F : (j + 1) * F, :] = table_ref[own:cols, j * K : (j + 1) * K]
    for n, (p, q) in enumerate(((x_ref, x_ref), (x_ref, y_ref), (y_ref, y_ref))):
        gram = lax.dot_general(p[...], q[...], (((0,), (0,)), ((), ())), preferred_element_type=jnp.float32)
        gram_ref[n * K : (n + 1) * K, :] = gram


def apply_pairs(hist, table, lists, coords):
    cols = table.shape[0]
    return pl.pallas_call(
        apply_body,
        out_shape=(jax.ShapeDtypeStruct((6 * F, K), jnp.float32), jax.ShapeDtypeStruct((3 * K, K), jnp.float32)),
        in_specs=[VM] * 4,
        out_specs=(VM, VM),
        scratch_shapes=[
            pltpu.VMEM((cols, NB * F), jnp.bfloat16),
            pltpu.VMEM((768, F), jnp.float32),
            pltpu.VMEM((6 * K, NB * F), jnp.float32),
            pltpu.VMEM((576, F), jnp.float32),
            pltpu.VMEM((112, F), jnp.float32),
            pltpu.VMEM((6 * K, F), jnp.float32),
            pltpu.VMEM((6 * F, K), jnp.bfloat16),
            pltpu.VMEM((6 * F, K), jnp.bfloat16),
        ],
        compiler_params=pltpu.CompilerParams(vmem_limit_bytes=36 * 1024 * 1024),
        cost_estimate=pl.CostEstimate(flops=8 * 10**9, bytes_accessed=8 * 10**6, transcendentals=0),
        name="apply_pairs",
    )(hist, table, lists, coords)


MESH = pl.DeviceIdType.MESH


def place():
    gx, gy, gz = lax.axis_index("gx"), lax.axis_index("gy"), lax.axis_index("gz")
    y, z = lax.rem(gx, 4), lax.div(gz, 2) * 2 + lax.div(gx, 4)
    return gy, y, z, lax.rem(gz, 2)


def device(x, y, z, core):
    return {"gx": lax.rem(z, 2) * 4 + y, "gy": x, "gz": lax.div(z, 2) * 2 + core}


PLANE = [(dx, dy) for dx in (2, 1, 3, 0) for dy in (2, 1, 3, 0)][:15]


def total_body(gram_ref, out_ref, tail_ref, data, half_in, half, plane_in, z_in, t1, t3, t4, send, recv):
    x, y, z, core = place()
    partner = device(x, y, z, 1 - core)
    plane = [device(lax.rem(x + dx, 4), lax.rem(y + dy, 4), z, core) for dx, dy in PLANE]
    along_z = [device(x, y, lax.rem(z + d, 8), core) for d in range(1, 8)]
    barrier = pltpu.get_barrier_semaphore()
    for peer in [partner] + plane + along_z:
        pl.semaphore_signal(barrier, inc=1, device_id=peer, device_id_type=MESH)

    lower = lax.broadcasted_iota(jnp.int32, (F, F), 0) >= lax.broadcasted_iota(jnp.int32, (F, F), 1)
    eye = lax.broadcasted_iota(jnp.int32, (F, F), 0) == lax.broadcasted_iota(jnp.int32, (F, F), 1)
    t1[0] = jnp.zeros((4, F), jnp.float32)
    for m in range(3):
        b11 = gram_ref[m * K : m * K + F, 0:F]
        b21 = gram_ref[m * K + F : m * K + K, 0:F]
        b22 = gram_ref[m * K + F : m * K + K, F:K]
        if m == 1:
            b11 = b11 + b11.T
            b21 = b21 + gram_ref[m * K : m * K + F, F:K].T
            b22 = b22 + b22.T
        data[m * 32 : m * 32 + 16] = b21.reshape(16, 8, F)
        data[m * 32 + 16 : m * 32 + 32] = jnp.where(lower, b11, b22).reshape(16, 8, F)
        t1[0, m : m + 1, :] = jnp.sum(jnp.where(eye, b22, 0.0), axis=0, keepdims=True)
    pl.semaphore_wait(barrier, 23)

    count = [0]
    started = []

    def copy(src, dst, peer):
        n = count[0]
        count[0] += 1
        c = pltpu.make_async_remote_copy(src_ref=src, dst_ref=dst, send_sem=send.at[n], recv_sem=recv.at[n], device_id=peer, device_id_type=MESH)
        c.start()
        started.append(c)
        return c

    first = []
    for dx in (2, 1, 3, 0):
        at = lax.rem(x + dx, 4) * 12
        first.append(copy(data.at[pl.ds((1 - core) * 48 + at, 12)], half_in.at[pl.ds(at, 12)], partner))
    small = copy(t1.at[0], t1.at[1], partner)
    arriving = []
    for n, dx in enumerate((2, 1, 3, 0)):
        at = lax.rem(x + dx, 4) * 12
        first[n].wait_recv()
        half[pl.ds(at, 12)] = data[pl.ds(core * 48 + at, 12)] + half_in[pl.ds(at, 12)]
        for slot, (px, py) in enumerate(PLANE):
            if px == dx:
                piece = at + lax.rem(y + py, 4) * 3
                arriving.append(copy(half.at[pl.ds(piece, 3)], plane_in.at[slot], plane[slot]))
    small.wait_recv()
    here = x * 4 + y
    t3[here] = t1[0] + t1[1]
    tails = [copy(t3.at[here], t3.at[here], plane[slot]) for slot in range(15)]
    total = half[pl.ds(here * 3, 3)]
    for slot in range(15):
        arriving[slot].wait_recv()
        total = total + plane_in[slot]
    z_in[z] = total
    arriving = [copy(z_in.at[z], z_in.at[z], along_z[d - 1]) for d in range(1, 8)]
    for c in tails:
        c.wait_recv()
    tail = t3[0]
    for n in range(1, 16):
        tail = tail + t3[n]
    t4[z] = tail
    tails = [copy(t4.at[z], t4.at[z], along_z[d - 1]) for d in range(1, 8)]
    for c in arriving:
        c.wait_recv()
    total = z_in[0]
    for n in range(1, 8):
        total = total + z_in[n]
    mine = core * 48 + here * 3
    out_ref[pl.ds(mine, 3)] = total
    arriving = [copy(out_ref.at[pl.ds(mine, 3)], out_ref.at[pl.ds(mine, 3)], plane[slot]) for slot in range(15)]
    onward = [copy(out_ref.at[pl.ds(mine, 3)], out_ref.at[pl.ds(mine, 3)], partner)]
    for c in tails:
        c.wait_recv()
    tail = t4[0]
    for n in range(1, 8):
        tail = tail + t4[n]
    tail_ref[0:4, :] = tail
    tail_ref[4:8, :] = tail
    for slot in reversed(range(15)):
        dx, dy = PLANE[slot]
        theirs = core * 48 + (lax.rem(x + 4 - dx, 4) * 4 + lax.rem(y + 4 - dy, 4)) * 3
        arriving[slot].wait_recv()
        onward.append(copy(out_ref.at[pl.ds(theirs, 3)], out_ref.at[pl.ds(theirs, 3)], partner))
    for c in onward:
        c.wait_recv()
    for c in started:
        c.wait_send()


def total_grams(gram):
    def buf(*shape):
        return pltpu.VMEM((*shape, 8, F), jnp.float32)

    def low(n):
        return pltpu.VMEM((n, 4, F), jnp.float32)

    return pl.pallas_call(
        total_body,
        out_shape=(jax.ShapeDtypeStruct((96, 8, F), jnp.float32), jax.ShapeDtypeStruct((8, F), jnp.float32)),
        in_specs=[VM],
        out_specs=(VM, VM),
        scratch_shapes=[
            buf(96), buf(48), buf(48), buf(15, 3), buf(8, 3), low(2), low(16), low(8),
            pltpu.SemaphoreType.DMA((80,)), pltpu.SemaphoreType.DMA((80,)),
        ],
        compiler_params=pltpu.CompilerParams(collective_id=1, has_side_effects=True, vmem_limit_bytes=12 * 1024 * 1024),
        cost_estimate=pl.CostEstimate(flops=10**6, bytes_accessed=2 * 10**6, transcendentals=0),
        name="total_grams",
    )(gram)


def near_body(pairs_ref, live_ref, basis_ref, coords_ref, hist_ref, table_ref, acc_ref, send, recv):
    gx, gy, gz = lax.axis_index("gx"), lax.axis_index("gy"), lax.axis_index("gz")
    core = lax.rem(gz, 2)
    far = 2 * core
    partner = {"gz": gz + 1 - 2 * core}
    beyond = {"gz": lax.rem(gz + 7 + 2 * core, 8)}
    up_x, down_x = {"gy": lax.rem(gy + 1, 4)}, {"gy": lax.rem(gy + 3, 4)}
    up_y, down_y = {"gx": lax.rem(gx + 1, 8)}, {"gx": lax.rem(gx + 7, 8)}
    barrier = pltpu.get_barrier_semaphore()
    for peer in (partner, beyond, up_x, down_x, up_y, down_y):
        pl.semaphore_signal(barrier, inc=1, device_id=peer, device_id_type=MESH)

    own = 27 * 32
    flat = coords_ref[...]
    high = flat.astype(jnp.bfloat16).astype(jnp.float32)
    mid = (flat - high).astype(jnp.bfloat16).astype(jnp.float32)
    parts = jnp.concatenate([high, mid, flat - high - mid, jnp.zeros((112, F), jnp.float32)], axis=0)
    table_ref[own : own + F, 0 : 6 * K] = basis_ref[...]
    table_ref[own : own + F, 6 * K : 7 * K] = jnp.transpose(parts).astype(jnp.bfloat16)
    table_ref[13 * 32 : 14 * 32, :] = table_ref[own : own + 32, :]
    pl.semaphore_wait(barrier, 6)

    count = [0]

    def slab(a, b, e):
        return table_ref.at[pl.ds(pl.multiple_of((9 * a + 3 * b + e) * 32, 32), 32)]

    def copy(src, dst, peer):
        n = count[0]
        count[0] += 1
        c = pltpu.make_async_remote_copy(src_ref=src, dst_ref=dst, send_sem=send.at[n], recv_sem=recv.at[n], device_id=peer, device_id_type=MESH)
        c.start()
        return c

    def first_hops(e):
        return [
            copy(slab(1, 1, e), slab(1, 0, e), up_x),
            copy(slab(1, 1, e), slab(1, 2, e), down_x),
            copy(slab(1, 1, e), slab(0, 1, e), up_y),
            copy(slab(1, 1, e), slab(2, 1, e), down_y),
        ]

    def second_hops(e):
        return [
            copy(slab(1, 0, e), slab(0, 0, e), up_y),
            copy(slab(1, 2, e), slab(2, 2, e), down_y),
            copy(slab(0, 1, e), slab(0, 2, e), down_x),
            copy(slab(2, 1, e), slab(2, 0, e), up_x),
        ]

    def forward(places):
        return [copy(slab(a, b, 1), slab(a, b, far), partner) for a, b in places]

    edges, corners = ((1, 0), (1, 2), (0, 1), (2, 1)), ((0, 0), (2, 2), (0, 2), (2, 0))
    z_far = copy(slab(1, 1, 1), slab(1, 1, 2 - far), beyond)
    z_near = copy(slab(1, 1, 1), slab(1, 1, far), partner)
    own_first = first_hops(1)
    chunk = counter(pairs_ref, live_ref, hist_ref, acc_ref)
    chunk(0)
    for c in [z_far] + own_first:
        c.wait_recv()
    far_first = first_hops(far)
    own_second = second_hops(1)
    sent = forward(edges)
    chunk(1)
    chunk(2)
    for c in own_second + far_first:
        c.wait_recv()
    far_second = second_hops(far)
    sent = sent + forward(corners)
    chunk(3)
    for c in [z_near] + far_second + sent:
        c.wait_recv()
    for c in [z_far, z_near] + own_first + far_first + own_second + far_second + sent:
        c.wait_send()


def near_and_counts(pairs, live, basis, coords):
    return pl.pallas_call(
        near_body,
        out_shape=(jax.ShapeDtypeStruct((4096, F), jnp.float32), jax.ShapeDtypeStruct((27 * 32 + F, 7 * K), jnp.bfloat16)),
        in_specs=[VM] * 4,
        out_specs=(VM, VM),
        scratch_shapes=[pltpu.VMEM((1024, 256), jnp.float32), pltpu.SemaphoreType.DMA((26,)), pltpu.SemaphoreType.DMA((26,))],
        compiler_params=pltpu.CompilerParams(collective_id=2, has_side_effects=True, vmem_limit_bytes=16 * 1024 * 1024),
        cost_estimate=pl.CostEstimate(flops=8 * 10**9, bytes_accessed=3 * 10**6, transcendentals=0),
        name="near_and_counts",
    )(pairs, live, basis, coords)


def dot32(p, q, dims):
    return lax.dot_general(p, q, (dims, ((), ())), precision=lax.Precision.HIGHEST, preferred_element_type=jnp.float32)


NT = ((1,), (1,))
NN = ((1,), (0,))


def cut(x):
    high = x.astype(jnp.bfloat16)
    rest = x - high.astype(jnp.float32)
    mid = rest.astype(jnp.bfloat16)
    return high, mid, (rest - mid.astype(jnp.float32)).astype(jnp.bfloat16)


def outer(p, q):
    ph, pm, pl_ = cut(p)
    qh, qm, ql = cut(q)
    left = jnp.concatenate([ph, ph, pm, ph, pl_, pm], axis=0)
    right = jnp.concatenate([qh, qm, qh, ql, qh, qm], axis=0)
    return lax.dot_general(left, right, (((0,), (0,)), ((), ())), preferred_element_type=jnp.float32)


def eliminate(mats):
    sub = lax.broadcasted_iota(jnp.int32, (8, F), 0)
    lane = lax.broadcasted_iota(jnp.int32, (8, F), 1)
    tiles = [[m[8 * t : 8 * t + 8, :] for t in range(16)] for m in mats]

    def columns(tile, t):
        return [jnp.broadcast_to(tile[:, 8 * t + k : 8 * t + k + 1], (8, F)) for k in range(8)]

    def spread(tile, r):
        return jnp.broadcast_to(tile[r : r + 1, :], (8, F))

    for t in range(16):
        inside = (lane >= 8 * t) & (lane < 8 * t + 8)
        for rows in tiles:
            top = rows[t]
            c = columns(top, t)
            lead = t + 1 < 16
            if lead:
                after = rows[t + 1]
                ca = columns(after, t)
            scaled = []
            for j in range(8):
                at = lane == 8 * t + j
                pivot = [spread(c[k], j) for k in range(j, 8)]
                inv = 1.0 / pivot[0]
                row = jnp.where(at, 1.0, spread(top, j))
                scaled.append(row * inv)
                if j < 7:
                    f = jnp.where(sub > j, c[j] * inv, 0.0)
                    for k in range(j + 1, 8):
                        c[k] = c[k] - f * pivot[k - j]
                    top = jnp.where(at & (sub > j), 0.0, top) - f * row
                if lead:
                    fa = ca[j] * inv
                    for k in range(j + 1, 8):
                        ca[k] = ca[k] - fa * pivot[k - j]
                    after = jnp.where(at, 0.0, after) - fa * row
            rows[t] = top
            if lead:
                rows[t + 1] = after
            if t + 2 < 16:
                packed = jnp.concatenate([s[0:1, :] for s in scaled], axis=0)
                plain = jnp.where(lane == sub + 8 * t, 1.0, jnp.where(inside & (lane > sub + 8 * t), 0.0, top))
                taken = outer(packed, plain)
                for u in range(t + 2, 16):
                    rows[u] = jnp.where(inside, 0.0, rows[u]) - taken[8 * u : 8 * u + 8, :]
    out = []
    for rows in tiles:
        full = []
        for t in range(16):
            diag = lane == sub + 8 * t
            d = jnp.sum(jnp.where(diag, rows[t], 0.0), axis=1, keepdims=True)
            keep = jnp.where(lane < sub + 8 * t, rows[t], jnp.where(diag, 1.0, 0.0))
            full.append(keep * jnp.broadcast_to(1.0 / jnp.sqrt(d), (8, F)))
        out.append(jnp.concatenate(full, axis=0))
    return out


def solve_body(sum_ref, tail_ref, image_ref, next_ref, ritz_ref, mat_ref, inv_ref, *, total_rows):
    scale = 1.0 / total_rows
    sub = lax.broadcasted_iota(jnp.int32, (F, F), 0)
    lane = lax.broadcasted_iota(jnp.int32, (F, F), 1)

    def unpack(m, half):
        b21 = sum_ref[m * 32 : m * 32 + 16].reshape(F, F) * half
        both = sum_ref[m * 32 + 16 : m * 32 + 32].reshape(F, F) * half
        flip = both.T
        b11 = jnp.where(sub >= lane, both, flip)
        diag = jnp.broadcast_to(tail_ref[m : m + 1, :] * half, (F, F))
        b22 = jnp.where(sub < lane, both, jnp.where(sub == lane, diag, flip))
        return b11, b21, b22

    s11, s21, s22 = unpack(0, scale)
    w11, w21, w22 = unpack(2, scale)
    mat_ref[0] = s11
    mat_ref[1] = w11
    for n, (b21, b22) in enumerate(((s21, s22), (w21, w22))):
        mat_ref[2 + 2 * n] = b21
        mat_ref[3 + 2 * n] = b22

    def half_step(step, carry):
        s, w = eliminate([mat_ref[0], mat_ref[1]])
        for n, top in enumerate((s, w)):
            inv_ref[2 * step + n] = top

        @pl.when(step == 0)
        def _():
            for n, top in enumerate((s, w)):
                left = dot32(mat_ref[2 + 2 * n], top, NT)
                mat_ref[n] = mat_ref[3 + 2 * n] - dot32(left, left, NT)
                mat_ref[2 + 2 * n] = left

        return carry

    lax.fori_loop(0, 2, half_step, 0)

    def whole(n):
        top, low = inv_ref[n], inv_ref[2 + n]
        corner = -dot32(low, dot32(mat_ref[2 + 2 * n], top, NN), NN)
        return jnp.concatenate(
            [jnp.concatenate([top, jnp.zeros((F, F), jnp.float32)], axis=1), jnp.concatenate([corner, low], axis=1)], axis=0
        )

    q11, q21, q22 = unpack(1, 0.5 * scale)
    cross_sum = jnp.concatenate([jnp.concatenate([q11, q21.T], axis=1), jnp.concatenate([q21, q22], axis=1)], axis=0)
    s_inv = whole(0)
    ritz_ref[...] = dot32(dot32(s_inv, cross_sum, NN), s_inv, NT)
    w_inv = whole(1)
    for j in range(6):
        next_ref[:, j * K : (j + 1) * K] = dot32(image_ref[j * F : (j + 1) * F, :], w_inv, NT)


def solve(sums, tail, image, total_rows):
    return pl.pallas_call(
        functools.partial(solve_body, total_rows=total_rows),
        out_shape=(jax.ShapeDtypeStruct((F, 6 * K), jnp.float32), jax.ShapeDtypeStruct((K, K), jnp.float32)),
        in_specs=[VM] * 3,
        out_specs=(VM, VM),
        scratch_shapes=[pltpu.VMEM((6, F, F), jnp.float32), pltpu.VMEM((4, F, F), jnp.float32)],
        compiler_params=pltpu.CompilerParams(vmem_limit_bytes=12 * 1024 * 1024),
        name="solve",
    )(sums, tail, image)


def per_device(coordinates, neighbours, pair_index, pair_live, basis):
    own = coordinates[0, 0, 0].reshape(48, F)
    hist, table = near_and_counts(pair_index[0, 0, 0], pair_live[0, 0, 0].reshape(1, -1), basis[0, 0, 0], own)
    image, gram = apply_pairs(hist, table, neighbours[0, 0, 0], own)
    sums, tail = total_grams(gram)
    next_rows, ritz = solve(sums, tail, image, 6.0 * F * 256)
    return next_rows.reshape(1, 1, 1, F, 6 * K), ritz


def solution(mesh):
    cells = [P("gx", "gy", "gz", *([None] * n)) for n in (3, 2, 2, 1, 2)]
    return jax.shard_map(per_device, mesh=mesh, in_specs=tuple(cells), out_specs=(cells[4], P()), check_vma=False)
```

```python
import functools
import jax
import jax.numpy as jnp
from jax import lax
from jax.experimental import pallas as pl
from jax.experimental.pallas import tpu as pltpu
from jax.sharding import PartitionSpec as P

VM = pl.BlockSpec(memory_space=pltpu.VMEM)
F = 128
K = 256
NB = 16
PB = 4096.0
CHUNK = 3840


def counter(pairs_ref, live_ref, hist_ref):
    rows = lax.broadcasted_iota(jnp.int32, (256, CHUNK), 0)
    zero = jnp.zeros((256, CHUNK), jnp.float32)

    def chunk(c):
        at = slice(c * CHUNK, (c + 1) * CHUNK)
        f = pairs_ref[0:1, at]
        s = pairs_ref[1:2, at]
        a = pairs_ref[2:3, at]
        b = pairs_ref[3:4, at]
        live = live_ref[0:1, at]
        value = (live * jnp.where(a >= 8, int(PB), 1)).astype(jnp.float32)
        col = ((a >> 2) & 1) * 128 + f
        right = jnp.where(rows == col, jnp.broadcast_to(value, (256, CHUNK)), zero).astype(jnp.bfloat16)
        hot = rows == (b * 16 + s)
        low = a & 3
        for part in range(4):
            mark = jnp.broadcast_to((low == part).astype(jnp.float32), (256, CHUNK))
            left = jnp.where(hot, mark, zero).astype(jnp.bfloat16)
            got = lax.dot_general(left, right, (((1,), (1,)), ((), ())), preferred_element_type=jnp.float32)
            high = jnp.floor(got * (1.0 / PB))
            lower = got - PB * high
            for mid in range(2):
                lanes = slice(mid * 128, (mid + 1) * 128)
                for top, val in ((0, lower), (1, high)):
                    a = top * 8 + mid * 4 + part
                    here = slice(a * 256, (a + 1) * 256)
                    if c == 0:
                        hist_ref[here, :] = val[:, lanes]
                    else:
                        hist_ref[here, :] = hist_ref[here, :] + val[:, lanes]

    return chunk


def cross(p, q):
    return [
        p[1] * q[2] - p[2] * q[1],
        p[2] * q[0] - p[0] * q[2],
        p[0] * q[1] - p[1] * q[0],
    ]


SYM = ((0, 0), (0, 1), (0, 2), (1, 1), (1, 2), (2, 2))


def symmetric(six):
    return [[six[0], six[1], six[2]], [six[1], six[3], six[4]], [six[2], six[4], six[5]]]


def moments(hist_ref, coords_ref, q_ref, blk_ref, rr_ref, gather):
    blk_ref[...] = jnp.zeros_like(blk_ref)
    rr_ref[...] = jnp.zeros_like(rr_ref)
    own = [jnp.sum(coords_ref[16 * c : 16 * c + 16, :], axis=0, keepdims=True) * (1.0 / 16.0) for c in range(3)]

    def tile(c, b, half):
        return q_ref[(c * 16 + b) * 16 + half * 8 : (c * 16 + b) * 16 + half * 8 + 8, :]

    centres = []
    for half in range(2):
        centre = []
        for c in range(3):
            total = tile(c, 0, half)
            for b in range(1, 16):
                total = total + tile(c, b, half)
            centre.append(total * (1.0 / 16.0))
        centres.append(centre)

    def atom(a, half):
        centre = centres[half]
        r = [jnp.broadcast_to(coords_ref[pl.ds(c * 16 + a, 1), :], (8, F)) for c in range(3)]
        arm = [r[c] - jnp.broadcast_to(own[c], (8, F)) for c in range(3)]
        m = [None] * 6
        n = [[None] * 3 for _ in range(3)]
        for b in range(16):
            q = [tile(c, b, half) for c in range(3)]
            d = [r[c] - q[c] for c in range(3)]
            count = hist_ref[pl.ds(pl.multiple_of(a * 256 + b * 16 + half * 8, 8), 8), :]
            w = (0.01 * count) / jnp.maximum(d[0] * d[0] + d[1] * d[1] + d[2] * d[2], 1.0)
            wd = [w * d[c] for c in range(3)]
            turn = cross([q[c] - centre[c] for c in range(3)], d)
            for k, (j, i) in enumerate(SYM):
                t = wd[j] * d[i]
                m[k] = t if m[k] is None else m[k] + t
            for j in range(3):
                for i in range(3):
                    t = wd[j] * turn[i]
                    n[j][i] = t if n[j][i] is None else n[j][i] + t
        m = symmetric(m)
        rt = [cross(arm, [m[j][i] for j in range(3)]) for i in range(3)]
        rn = [cross(arm, [n[j][i] for j in range(3)]) for i in range(3)]
        for j in range(3):
            for i in range(3):
                for jj, ii, val in ((j, i, m[j][i]), (j, 3 + i, n[j][i]), (3 + j, i, rt[i][j]), (3 + j, 3 + i, rn[i][j])):
                    here = pl.ds((jj * 6 + ii) * 16 + half * 8, 8)
                    blk_ref[here, :] = blk_ref[here, :] - val
        for j in range(3):
            rr = cross(arm, [rt[i][j] for i in range(3)])
            for i in range(3):
                here = pl.ds((j * 3 + i) * 8, 8)
                rr_ref[here, :] = rr_ref[here, :] + rr[i]

    def quarter(part, carry):
        gather(part)
        for n in range(4):
            for half in range(2):
                atom(part * 4 + n, half)
        return carry

    lax.fori_loop(0, 4, quarter, 0)
    for j in range(3):
        for i in range(3):
            tt = jnp.sum(blk_ref[pl.ds((j * 6 + i) * 16, 16), :], axis=0, keepdims=True)
            rt = jnp.sum(blk_ref[pl.ds(((3 + j) * 6 + i) * 16, 16), :], axis=0, keepdims=True)
            rr = jnp.sum(rr_ref[pl.ds((j * 3 + i) * 8, 8), :], axis=0, keepdims=True)
            for jj, ii, val in ((j, i, -tt), (3 + j, i, -rt), (i, 3 + j, -rt), (3 + j, 3 + i, rr)):
                here = pl.ds((jj * 6 + ii) * 16, 1)
                rr_ref[72 + jj * 6 + ii : 73 + jj * 6 + ii, :] = val
    for ji in range(36):
        here = pl.ds(ji * 16, 1)
        blk_ref[here, :] = blk_ref[here, :] + rr_ref[72 + ji : 73 + ji, :]


KC = 32


def apply_blocks(hist_ref, table_ref, hot_ref, coords_ref, image_ref, q_ref, g_ref, blk_ref, rr_ref, it_ref):
    def gathered(columns):
        return lax.dot_general(table_ref[:, columns], hot_ref[...], (((0,), (0,)), ((), ())), preferred_element_type=jnp.float32)

    got = gathered(slice(6 * K, 7 * K))
    pos = got[0:48] + got[48:96] + got[96:144]
    for s in range(NB):
        for t in range(6):
            q_ref[pl.ds(t * 128 + s, 8, stride=16), :] = pos[t * 8 : t * 8 + 8, s * F : (s + 1) * F]

    def gather(part):
        at = pl.ds(pl.multiple_of(part * 384, 384), 384)
        g_ref[at, :] = gathered(at)

    moments(hist_ref, coords_ref, q_ref, blk_ref, rr_ref, gather)

    def piece(kc, carry):
        start = pl.multiple_of(kc * KC, KC)
        totals = [jnp.zeros((KC, F), jnp.float32) for _ in range(6)]
        for s in range(NB):
            for i in range(6):
                g = g_ref[pl.ds(i * K + start, KC), s * F : (s + 1) * F]
                for j in range(6):
                    row = (j * 6 + i) * 16 + s
                    totals[j] = totals[j] + jnp.broadcast_to(blk_ref[row : row + 1, :], (KC, F)) * g
        for j in range(6):
            it_ref[pl.ds(j * K + start, KC), :] = totals[j]
        return carry

    lax.fori_loop(0, K // KC, piece, 0)
    for j in range(6):
        image_ref[j * F : (j + 1) * F, :] = jnp.transpose(it_ref[j * K : (j + 1) * K, :])


MESH = pl.DeviceIdType.MESH


def place():
    gx, gy, gz = lax.axis_index("gx"), lax.axis_index("gy"), lax.axis_index("gz")
    y, z = lax.rem(gx, 4), lax.div(gz, 2) * 2 + lax.div(gx, 4)
    return gy, y, z, lax.rem(gz, 2)


def device(x, y, z, core):
    return {"gx": lax.rem(z, 2) * 4 + y, "gy": x, "gz": lax.div(z, 2) * 2 + core}


PLANE = [(dx, dy) for dx in (2, 1, 3, 0) for dy in (2, 1, 3, 0)][:15]


def total_body(image_ref, basis_ref, out_ref, tail_ref, x_ref, y_ref, data, half_in, half, plane_in, z_in, t1, t3, t4, send, recv):
    x, y, z, core = place()
    partner = device(x, y, z, 1 - core)
    plane = [device(lax.rem(x + dx, 4), lax.rem(y + dy, 4), z, core) for dx, dy in PLANE]
    along_z = [device(x, y, lax.rem(z + d, 8), core) for d in range(1, 8)]
    barrier = pltpu.get_barrier_semaphore()
    for peer in [partner] + plane + along_z:
        pl.semaphore_signal(barrier, inc=1, device_id=peer, device_id_type=MESH)

    for j in range(6):
        x_ref[j * F : (j + 1) * F, :] = basis_ref[:, j * K : (j + 1) * K]
    y_ref[...] = image_ref[...].astype(jnp.bfloat16)

    def gram(left, right):
        return lax.dot_general(left[...], right[...], (((0,), (0,)), ((), ())), preferred_element_type=jnp.float32)

    lower = lax.broadcasted_iota(jnp.int32, (F, F), 0) >= lax.broadcasted_iota(jnp.int32, (F, F), 1)
    eye = lax.broadcasted_iota(jnp.int32, (F, F), 0) == lax.broadcasted_iota(jnp.int32, (F, F), 1)
    t1[0] = jnp.zeros((4, F), jnp.float32)
    for m in range(3):
        both = gram(x_ref if m < 2 else y_ref, x_ref if m < 1 else y_ref)
        b11, b21, b22 = both[:F, :F], both[F:, :F], both[F:, F:]
        if m == 1:
            b11 = b11 + b11.T
            b21 = b21 + both[:F, F:].T
            b22 = b22 + b22.T
        data[m * 32 : m * 32 + 16] = b21.reshape(16, 8, F)
        data[m * 32 + 16 : m * 32 + 32] = jnp.where(lower, b11, b22).reshape(16, 8, F)
        t1[0, m : m + 1, :] = jnp.sum(jnp.where(eye, b22, 0.0), axis=0, keepdims=True)
    pl.semaphore_wait(barrier, 23)

    count = [0]
    started = []

    def copy(src, dst, peer):
        n = count[0]
        count[0] += 1
        c = pltpu.make_async_remote_copy(src_ref=src, dst_ref=dst, send_sem=send.at[n], recv_sem=recv.at[n], device_id=peer, device_id_type=MESH)
        c.start()
        started.append(c)
        return c

    first = []
    for dx in (2, 1, 3, 0):
        at = lax.rem(x + dx, 4) * 12
        first.append(copy(data.at[pl.ds((1 - core) * 48 + at, 12)], half_in.at[pl.ds(at, 12)], partner))
    small = copy(t1.at[0], t1.at[1], partner)
    arriving = []
    for n, dx in enumerate((2, 1, 3, 0)):
        at = lax.rem(x + dx, 4) * 12
        first[n].wait_recv()
        half[pl.ds(at, 12)] = data[pl.ds(core * 48 + at, 12)] + half_in[pl.ds(at, 12)]
        for slot, (px, py) in enumerate(PLANE):
            if px == dx:
                piece = at + lax.rem(y + py, 4) * 3
                arriving.append(copy(half.at[pl.ds(piece, 3)], plane_in.at[slot], plane[slot]))
    small.wait_recv()
    here = x * 4 + y
    t3[here] = t1[0] + t1[1]
    tails = [copy(t3.at[here], t3.at[here], plane[slot]) for slot in range(15)]
    total = half[pl.ds(here * 3, 3)]
    for slot in range(15):
        arriving[slot].wait_recv()
        total = total + plane_in[slot]
    z_in[z] = total
    arriving = [copy(z_in.at[z], z_in.at[z], along_z[d - 1]) for d in range(1, 8)]
    for c in tails:
        c.wait_recv()
    tail = t3[0]
    for n in range(1, 16):
        tail = tail + t3[n]
    t4[z] = tail
    tails = [copy(t4.at[z], t4.at[z], along_z[d - 1]) for d in range(1, 8)]
    for c in arriving:
        c.wait_recv()
    total = z_in[0]
    for n in range(1, 8):
        total = total + z_in[n]
    mine = core * 48 + here * 3
    out_ref[pl.ds(mine, 3)] = total
    arriving = [copy(out_ref.at[pl.ds(mine, 3)], out_ref.at[pl.ds(mine, 3)], plane[slot]) for slot in range(15)]
    onward = [copy(out_ref.at[pl.ds(mine, 3)], out_ref.at[pl.ds(mine, 3)], partner)]
    for c in tails:
        c.wait_recv()
    tail = t4[0]
    for n in range(1, 8):
        tail = tail + t4[n]
    tail_ref[0:4, :] = tail
    tail_ref[4:8, :] = tail
    for slot in reversed(range(15)):
        dx, dy = PLANE[slot]
        theirs = core * 48 + (lax.rem(x + 4 - dx, 4) * 4 + lax.rem(y + 4 - dy, 4)) * 3
        arriving[slot].wait_recv()
        onward.append(copy(out_ref.at[pl.ds(theirs, 3)], out_ref.at[pl.ds(theirs, 3)], partner))
    for c in onward:
        c.wait_recv()
    for c in started:
        c.wait_send()


def total_grams(image, basis):
    def buf(*shape):
        return pltpu.VMEM((*shape, 8, F), jnp.float32)

    def low(n):
        return pltpu.VMEM((n, 4, F), jnp.float32)

    return pl.pallas_call(
        total_body,
        out_shape=(jax.ShapeDtypeStruct((96, 8, F), jnp.float32), jax.ShapeDtypeStruct((8, F), jnp.float32)),
        in_specs=[VM, VM],
        out_specs=(VM, VM),
        scratch_shapes=[
            pltpu.VMEM((6 * F, K), jnp.bfloat16), pltpu.VMEM((6 * F, K), jnp.bfloat16),
            buf(96), buf(48), buf(48), buf(15, 3), buf(8, 3), low(2), low(16), low(8),
            pltpu.SemaphoreType.DMA((80,)), pltpu.SemaphoreType.DMA((80,)),
        ],
        compiler_params=pltpu.CompilerParams(collective_id=1, has_side_effects=True, vmem_limit_bytes=12 * 1024 * 1024),
        cost_estimate=pl.CostEstimate(flops=10**6, bytes_accessed=2 * 10**6, transcendentals=0),
        name="total_grams",
    )(image, basis)


def image_body(
    pairs_hbm, live_hbm, basis_hbm, coords_hbm, lists_hbm, image_ref,
    pairs_ref, live_ref, coords_ref, lists_ref, hist_ref, table_ref, hot_ref, q_ref, g_ref, blk_ref, rr_ref, it_ref,
    loaded, send, recv,
):
    own = 27 * 32
    loads = [
        pltpu.make_async_copy(src, dst, loaded.at[n])
        for n, (src, dst) in enumerate(
            (
                (coords_hbm, coords_ref),
                (basis_hbm, table_ref.at[pl.ds(own, F), pl.ds(0, 6 * K)]),
                (pairs_hbm, pairs_ref),
                (live_hbm, live_ref),
                (lists_hbm, lists_ref),
            )
        )
    ]
    for c in loads:
        c.start()
    gx, gy, gz = lax.axis_index("gx"), lax.axis_index("gy"), lax.axis_index("gz")
    core = lax.rem(gz, 2)
    far = 2 * core
    partner = {"gz": gz + 1 - 2 * core}
    beyond = {"gz": lax.rem(gz + 7 + 2 * core, 8)}
    up_x, down_x = {"gy": lax.rem(gy + 1, 4)}, {"gy": lax.rem(gy + 3, 4)}
    up_y, down_y = {"gx": lax.rem(gx + 1, 8)}, {"gx": lax.rem(gx + 7, 8)}
    barrier = pltpu.get_barrier_semaphore()
    for peer in (partner, beyond, up_x, down_x, up_y, down_y):
        pl.semaphore_signal(barrier, inc=1, device_id=peer, device_id_type=MESH)

    loads[0].wait()
    flat = coords_ref[...]
    high = flat.astype(jnp.bfloat16).astype(jnp.float32)
    mid = (flat - high).astype(jnp.bfloat16).astype(jnp.float32)
    parts = jnp.concatenate([high, mid, flat - high - mid, jnp.zeros((112, F), jnp.float32)], axis=0)
    table_ref[own : own + F, 6 * K : 7 * K] = jnp.transpose(parts).astype(jnp.bfloat16)
    loads[1].wait()
    table_ref[13 * 32 : 14 * 32, :] = table_ref[own : own + 32, :]
    pl.semaphore_wait(barrier, 6)

    count = [0]

    def slab(a, b, e):
        return table_ref.at[pl.ds(pl.multiple_of((9 * a + 3 * b + e) * 32, 32), 32)]

    def copy(src, dst, peer):
        n = count[0]
        count[0] += 1
        c = pltpu.make_async_remote_copy(src_ref=src, dst_ref=dst, send_sem=send.at[n], recv_sem=recv.at[n], device_id=peer, device_id_type=MESH)
        c.start()
        return c

    def first_hops(e):
        return [
            copy(slab(1, 1, e), slab(1, 0, e), up_x),
            copy(slab(1, 1, e), slab(1, 2, e), down_x),
            copy(slab(1, 1, e), slab(0, 1, e), up_y),
            copy(slab(1, 1, e), slab(2, 1, e), down_y),
        ]

    def second_hops(e):
        return [
            copy(slab(1, 0, e), slab(0, 0, e), up_y),
            copy(slab(1, 2, e), slab(2, 2, e), down_y),
            copy(slab(0, 1, e), slab(0, 2, e), down_x),
            copy(slab(2, 1, e), slab(2, 0, e), up_x),
        ]

    def forward(places):
        return [copy(slab(a, b, 1), slab(a, b, far), partner) for a, b in places]

    edges, corners = ((1, 0), (1, 2), (0, 1), (2, 1)), ((0, 0), (2, 2), (0, 2), (2, 0))
    z_far = copy(slab(1, 1, 1), slab(1, 1, 2 - far), beyond)
    z_near = copy(slab(1, 1, 1), slab(1, 1, far), partner)
    own_first = first_hops(1)
    chunk = counter(pairs_ref, live_ref, hist_ref)
    loads[2].wait()
    loads[3].wait()
    chunk(0)
    for c in [z_far] + own_first:
        c.wait_recv()
    far_first = first_hops(far)
    own_second = second_hops(1)
    sent = forward(edges)
    chunk(1)
    loads[4].wait()
    for s in range(NB):
        near = jnp.broadcast_to(lists_ref[s : s + 1, :], (own + F, F))
        hot = lax.broadcasted_iota(jnp.int32, (own + F, F), 0) == near
        hot_ref[:, s * F : (s + 1) * F] = jnp.where(hot, 1.0, 0.0).astype(jnp.bfloat16)
    chunk(2)
    for c in own_second + far_first:
        c.wait_recv()
    far_second = second_hops(far)
    sent = sent + forward(corners)
    chunk(3)
    for c in [z_near] + far_second + sent:
        c.wait_recv()
    for c in [z_far, z_near] + own_first + far_first + own_second + far_second + sent:
        c.wait_send()
    apply_blocks(hist_ref, table_ref, hot_ref, coords_ref, image_ref, q_ref, g_ref, blk_ref, rr_ref, it_ref)


def images(pairs, live, basis, coords, lists):
    rows = 27 * 32 + F
    return pl.pallas_call(
        image_body,
        out_shape=jax.ShapeDtypeStruct((6 * F, K), jnp.float32),
        in_specs=[pl.BlockSpec(memory_space=pltpu.MemorySpace.HBM)] * 5,
        out_specs=VM,
        scratch_shapes=[
            pltpu.VMEM(pairs.shape, jnp.int32),
            pltpu.VMEM(live.shape, jnp.int32),
            pltpu.VMEM((48, F), jnp.float32),
            pltpu.VMEM((NB, F), jnp.int32),
            pltpu.VMEM((4096, F), jnp.float32),
            pltpu.VMEM((rows, 7 * K), jnp.bfloat16),
            pltpu.VMEM((rows, NB * F), jnp.bfloat16),
            pltpu.VMEM((768, F), jnp.float32),
            pltpu.VMEM((6 * K, NB * F), jnp.float32),
            pltpu.VMEM((576, F), jnp.float32),
            pltpu.VMEM((112, F), jnp.float32),
            pltpu.VMEM((6 * K, F), jnp.float32),
            pltpu.SemaphoreType.DMA((5,)),
            pltpu.SemaphoreType.DMA((26,)),
            pltpu.SemaphoreType.DMA((26,)),
        ],
        compiler_params=pltpu.CompilerParams(collective_id=2, has_side_effects=True, vmem_limit_bytes=66_000_000),
        cost_estimate=pl.CostEstimate(flops=16 * 10**9, bytes_accessed=3 * 10**6, transcendentals=0),
        name="images",
    )(pairs, live, basis, coords, lists)


def dot32(p, q, dims):
    return lax.dot_general(p, q, (dims, ((), ())), precision=lax.Precision.HIGHEST, preferred_element_type=jnp.float32)


NT = ((1,), (1,))
NN = ((1,), (0,))


def cut(x):
    high = x.astype(jnp.bfloat16)
    rest = x - high.astype(jnp.float32)
    mid = rest.astype(jnp.bfloat16)
    return high, mid, (rest - mid.astype(jnp.float32)).astype(jnp.bfloat16)


def outer(p, q):
    ph, pm, pl_ = cut(p)
    qh, qm, ql = cut(q)
    left = jnp.concatenate([ph, ph, pm, ph, pl_, pm], axis=0)
    right = jnp.concatenate([qh, qm, qh, ql, qh, qm], axis=0)
    return lax.dot_general(left, right, (((0,), (0,)), ((), ())), preferred_element_type=jnp.float32)


def eliminate(mats):
    sub = lax.broadcasted_iota(jnp.int32, (8, F), 0)
    lane = lax.broadcasted_iota(jnp.int32, (8, F), 1)
    tiles = [[m[8 * t : 8 * t + 8, :] for t in range(16)] for m in mats]

    def columns(tile, t):
        return [jnp.broadcast_to(tile[:, 8 * t + k : 8 * t + k + 1], (8, F)) for k in range(8)]

    def spread(tile, r):
        return jnp.broadcast_to(tile[r : r + 1, :], (8, F))

    for t in range(16):
        inside = (lane >= 8 * t) & (lane < 8 * t + 8)
        for rows in tiles:
            top = rows[t]
            c = columns(top, t)
            lead = t + 1 < 16
            if lead:
                after = rows[t + 1]
                ca = columns(after, t)
            scaled = []
            for j in range(8):
                at = lane == 8 * t + j
                pivot = [spread(c[k], j) for k in range(j, 8)]
                inv = 1.0 / pivot[0]
                row = jnp.where(at, 1.0, spread(top, j))
                scaled.append(row * inv)
                if j < 7:
                    f = jnp.where(sub > j, c[j] * inv, 0.0)
                    for k in range(j + 1, 8):
                        c[k] = c[k] - f * pivot[k - j]
                    top = jnp.where(at & (sub > j), 0.0, top) - f * row
                if lead:
                    fa = ca[j] * inv
                    for k in range(j + 1, 8):
                        ca[k] = ca[k] - fa * pivot[k - j]
                    after = jnp.where(at, 0.0, after) - fa * row
            rows[t] = top
            if lead:
                rows[t + 1] = after
            if t + 2 < 16:
                packed = jnp.concatenate([s[0:1, :] for s in scaled], axis=0)
                plain = jnp.where(lane == sub + 8 * t, 1.0, jnp.where(inside & (lane > sub + 8 * t), 0.0, top))
                taken = outer(packed, plain)
                for u in range(t + 2, 16):
                    rows[u] = jnp.where(inside, 0.0, rows[u]) - taken[8 * u : 8 * u + 8, :]
    out = []
    for rows in tiles:
        full = []
        for t in range(16):
            diag = lane == sub + 8 * t
            d = jnp.sum(jnp.where(diag, rows[t], 0.0), axis=1, keepdims=True)
            keep = jnp.where(lane < sub + 8 * t, rows[t], jnp.where(diag, 1.0, 0.0))
            full.append(keep * jnp.broadcast_to(1.0 / jnp.sqrt(d), (8, F)))
        out.append(jnp.concatenate(full, axis=0))
    return out


def solve_body(sum_ref, tail_ref, image_ref, next_ref, ritz_ref, mat_ref, inv_ref, *, total_rows):
    scale = 1.0 / total_rows
    sub = lax.broadcasted_iota(jnp.int32, (F, F), 0)
    lane = lax.broadcasted_iota(jnp.int32, (F, F), 1)

    def unpack(m, half):
        b21 = sum_ref[m * 32 : m * 32 + 16].reshape(F, F) * half
        both = sum_ref[m * 32 + 16 : m * 32 + 32].reshape(F, F) * half
        flip = both.T
        b11 = jnp.where(sub >= lane, both, flip)
        diag = jnp.broadcast_to(tail_ref[m : m + 1, :] * half, (F, F))
        b22 = jnp.where(sub < lane, both, jnp.where(sub == lane, diag, flip))
        return b11, b21, b22

    s11, s21, s22 = unpack(0, scale)
    w11, w21, w22 = unpack(2, scale)
    mat_ref[0] = s11
    mat_ref[1] = w11
    for n, (b21, b22) in enumerate(((s21, s22), (w21, w22))):
        mat_ref[2 + 2 * n] = b21
        mat_ref[3 + 2 * n] = b22

    def half_step(step, carry):
        s, w = eliminate([mat_ref[0], mat_ref[1]])
        for n, top in enumerate((s, w)):
            inv_ref[2 * step + n] = top

        @pl.when(step == 0)
        def _():
            for n, top in enumerate((s, w)):
                left = dot32(mat_ref[2 + 2 * n], top, NT)
                mat_ref[n] = mat_ref[3 + 2 * n] - dot32(left, left, NT)
                mat_ref[2 + 2 * n] = left

        return carry

    lax.fori_loop(0, 2, half_step, 0)

    def whole(n):
        top, low = inv_ref[n], inv_ref[2 + n]
        corner = -dot32(low, dot32(mat_ref[2 + 2 * n], top, NN), NN)
        return jnp.concatenate(
            [jnp.concatenate([top, jnp.zeros((F, F), jnp.float32)], axis=1), jnp.concatenate([corner, low], axis=1)], axis=0
        )

    q11, q21, q22 = unpack(1, 0.5 * scale)
    cross_sum = jnp.concatenate([jnp.concatenate([q11, q21.T], axis=1), jnp.concatenate([q21, q22], axis=1)], axis=0)
    s_inv = whole(0)
    ritz_ref[...] = dot32(dot32(s_inv, cross_sum, NN), s_inv, NT)
    w_inv = whole(1)
    for j in range(6):
        next_ref[:, j * K : (j + 1) * K] = dot32(image_ref[j * F : (j + 1) * F, :], w_inv, NT)


def solve(sums, tail, image, total_rows):
    return pl.pallas_call(
        functools.partial(solve_body, total_rows=total_rows),
        out_shape=(jax.ShapeDtypeStruct((F, 6 * K), jnp.float32), jax.ShapeDtypeStruct((K, K), jnp.float32)),
        in_specs=[VM] * 3,
        out_specs=(VM, VM),
        scratch_shapes=[pltpu.VMEM((6, F, F), jnp.float32), pltpu.VMEM((4, F, F), jnp.float32)],
        compiler_params=pltpu.CompilerParams(vmem_limit_bytes=12 * 1024 * 1024),
        name="solve",
    )(sums, tail, image)


def per_device(coordinates, neighbours, pair_index, pair_live, basis):
    own = coordinates[0, 0, 0].reshape(48, F)
    rows = basis[0, 0, 0]
    image = images(pair_index[0, 0, 0], pair_live[0, 0, 0].reshape(1, -1), rows, own, neighbours[0, 0, 0])
    sums, tail = total_grams(image, rows)
    next_rows, ritz = solve(sums, tail, image, 6.0 * F * 256)
    return next_rows.reshape(1, 1, 1, F, 6 * K), ritz


def solution(mesh):
    cells = [P("gx", "gy", "gz", *([None] * n)) for n in (3, 2, 2, 1, 2)]
    return jax.shard_map(per_device, mesh=mesh, in_specs=tuple(cells), out_specs=(cells[4], P()), check_vma=False)
```

```python
import functools
import jax
import jax.numpy as jnp
from jax import lax
from jax.experimental import pallas as pl
from jax.experimental.pallas import tpu as pltpu
from jax.sharding import PartitionSpec as P

VM = pl.BlockSpec(memory_space=pltpu.VMEM)
F = 128
K = 256
NB = 16
PB = 4096.0
CHUNK = 3840


def counter(pairs_ref, live_ref, hist_ref):
    rows = lax.broadcasted_iota(jnp.int32, (256, CHUNK), 0)
    zero = jnp.zeros((256, CHUNK), jnp.float32)

    def chunk(c):
        at = slice(c * CHUNK, (c + 1) * CHUNK)
        f = pairs_ref[0:1, at]
        s = pairs_ref[1:2, at]
        a = pairs_ref[2:3, at]
        b = pairs_ref[3:4, at]
        live = live_ref[0:1, at]
        value = (live * jnp.where(a >= 8, int(PB), 1)).astype(jnp.float32)
        col = ((a >> 2) & 1) * 128 + f
        right = jnp.where(rows == col, jnp.broadcast_to(value, (256, CHUNK)), zero).astype(jnp.bfloat16)
        hot = rows == (b * 16 + s)
        low = a & 3
        for part in range(4):
            mark = jnp.broadcast_to((low == part).astype(jnp.float32), (256, CHUNK))
            left = jnp.where(hot, mark, zero).astype(jnp.bfloat16)
            got = lax.dot_general(left, right, (((1,), (1,)), ((), ())), preferred_element_type=jnp.float32)
            high = jnp.floor(got * (1.0 / PB))
            lower = got - PB * high
            for mid in range(2):
                lanes = slice(mid * 128, (mid + 1) * 128)
                for top, val in ((0, lower), (1, high)):
                    a = top * 8 + mid * 4 + part
                    here = slice(a * 256, (a + 1) * 256)
                    if c == 0:
                        hist_ref[here, :] = val[:, lanes]
                    else:
                        hist_ref[here, :] = hist_ref[here, :] + val[:, lanes]

    return chunk


def cross(p, q):
    return [
        p[1] * q[2] - p[2] * q[1],
        p[2] * q[0] - p[0] * q[2],
        p[0] * q[1] - p[1] * q[0],
    ]


SYM = ((0, 0), (0, 1), (0, 2), (1, 1), (1, 2), (2, 2))


def symmetric(six):
    return [[six[0], six[1], six[2]], [six[1], six[3], six[4]], [six[2], six[4], six[5]]]


def moments(hist_ref, coords_ref, q_ref, blk_ref, rr_ref):
    blk_ref[...] = jnp.zeros_like(blk_ref)
    rr_ref[...] = jnp.zeros_like(rr_ref)
    own = [jnp.sum(coords_ref[16 * c : 16 * c + 16, :], axis=0, keepdims=True) * (1.0 / 16.0) for c in range(3)]

    def tile(c, b, half):
        return q_ref[(c * 16 + b) * 16 + half * 8 : (c * 16 + b) * 16 + half * 8 + 8, :]

    centres = []
    for half in range(2):
        centre = []
        for c in range(3):
            total = tile(c, 0, half)
            for b in range(1, 16):
                total = total + tile(c, b, half)
            centre.append(total * (1.0 / 16.0))
        centres.append(centre)

    def atom(a, half):
        centre = centres[half]
        r = [jnp.broadcast_to(coords_ref[pl.ds(c * 16 + a, 1), :], (8, F)) for c in range(3)]
        arm = [r[c] - jnp.broadcast_to(own[c], (8, F)) for c in range(3)]
        m = [None] * 6
        n = [[None] * 3 for _ in range(3)]
        for b in range(16):
            q = [tile(c, b, half) for c in range(3)]
            d = [r[c] - q[c] for c in range(3)]
            count = hist_ref[pl.ds(pl.multiple_of(a * 256 + b * 16 + half * 8, 8), 8), :]
            w = (0.01 * count) / jnp.maximum(d[0] * d[0] + d[1] * d[1] + d[2] * d[2], 1.0)
            wd = [w * d[c] for c in range(3)]
            turn = cross([q[c] - centre[c] for c in range(3)], d)
            for k, (j, i) in enumerate(SYM):
                t = wd[j] * d[i]
                m[k] = t if m[k] is None else m[k] + t
            for j in range(3):
                for i in range(3):
                    t = wd[j] * turn[i]
                    n[j][i] = t if n[j][i] is None else n[j][i] + t
        m = symmetric(m)
        rt = [cross(arm, [m[j][i] for j in range(3)]) for i in range(3)]
        rn = [cross(arm, [n[j][i] for j in range(3)]) for i in range(3)]
        for j in range(3):
            for i in range(3):
                for jj, ii, val in ((j, i, m[j][i]), (j, 3 + i, n[j][i]), (3 + j, i, rt[i][j]), (3 + j, 3 + i, rn[i][j])):
                    here = pl.ds((jj * 6 + ii) * 16 + half * 8, 8)
                    blk_ref[here, :] = blk_ref[here, :] - val
        for j in range(3):
            rr = cross(arm, [rt[i][j] for i in range(3)])
            for i in range(3):
                here = pl.ds((j * 3 + i) * 8, 8)
                rr_ref[here, :] = rr_ref[here, :] + rr[i]

    def both(a, carry):
        for half in range(2):
            atom(a, half)
        return carry

    lax.fori_loop(0, 16, both, 0)
    for j in range(3):
        for i in range(3):
            tt = jnp.sum(blk_ref[pl.ds((j * 6 + i) * 16, 16), :], axis=0, keepdims=True)
            rt = jnp.sum(blk_ref[pl.ds(((3 + j) * 6 + i) * 16, 16), :], axis=0, keepdims=True)
            rr = jnp.sum(rr_ref[pl.ds((j * 3 + i) * 8, 8), :], axis=0, keepdims=True)
            for jj, ii, val in ((j, i, -tt), (3 + j, i, -rt), (i, 3 + j, -rt), (3 + j, 3 + i, rr)):
                here = pl.ds((jj * 6 + ii) * 16, 1)
                rr_ref[72 + jj * 6 + ii : 73 + jj * 6 + ii, :] = val
    for ji in range(36):
        here = pl.ds(ji * 16, 1)
        blk_ref[here, :] = blk_ref[here, :] + rr_ref[72 + ji : 73 + ji, :]


KC = 32


def chosen(table_ref, columns, hot_ref):
    return lax.dot_general(table_ref[:, columns], hot_ref[...], (((0,), (0,)), ((), ())), preferred_element_type=jnp.float32)


def place_partners(ctab_ref, hot_ref, q_ref):
    got = chosen(ctab_ref, slice(0, 256), hot_ref)
    pos = got[0:48] + got[48:96] + got[96:144]
    for s in range(NB):
        for t in range(6):
            q_ref[pl.ds(t * 128 + s, 8, stride=16), :] = pos[t * 8 : t * 8 + 8, s * F : (s + 1) * F]


def apply_blocks(table_ref, hot_ref, image_ref, g_ref, blk_ref, it_ref):
    for part in range(6):
        at = slice(part * K, (part + 1) * K)
        g_ref[at, :] = chosen(table_ref, at, hot_ref)

    def piece(kc, carry):
        start = pl.multiple_of(kc * KC, KC)

        def slot(s, totals):
            totals = list(totals)
            lanes = pl.ds(pl.multiple_of(s * F, F), F)
            for i in range(6):
                g = g_ref[pl.ds(i * K + start, KC), lanes]
                for j in range(6):
                    row = blk_ref[pl.ds((j * 6 + i) * 16 + s, 1), :]
                    totals[j] = totals[j] + jnp.broadcast_to(row, (KC, F)) * g
            return tuple(totals)

        totals = lax.fori_loop(0, NB, slot, tuple(jnp.zeros((KC, F), jnp.float32) for _ in range(6)))
        for j in range(6):
            it_ref[pl.ds(j * K + start, KC), :] = totals[j]
        return carry

    lax.fori_loop(0, K // KC, piece, 0)
    for j in range(6):
        image_ref[j * F : (j + 1) * F, :] = jnp.transpose(it_ref[j * K : (j + 1) * K, :])


MESH = pl.DeviceIdType.MESH


def place():
    gx, gy, gz = lax.axis_index("gx"), lax.axis_index("gy"), lax.axis_index("gz")
    y, z = lax.rem(gx, 4), lax.div(gz, 2) * 2 + lax.div(gx, 4)
    return gy, y, z, lax.rem(gz, 2)


def device(x, y, z, core):
    return {"gx": lax.rem(z, 2) * 4 + y, "gy": x, "gz": lax.div(z, 2) * 2 + core}


PLANE = [(dx, dy) for dx in (2, 1, 3, 0) for dy in (2, 1, 3, 0)][:15]


def sum_peers():
    x, y, z, core = place()
    plane = [device(lax.rem(x + dx, 4), lax.rem(y + dy, 4), z, core) for dx, dy in PLANE]
    along_z = [device(x, y, lax.rem(z + d, 8), core) for d in range(1, 8)]
    return device(x, y, z, 1 - core), plane, along_z


def total_grams(image_ref, basis_ref, out_ref, tail_ref, x_ref, y_ref, data, half_in, half, plane_in, z_in, t1, t3, t4, send, recv):
    x, y, z, core = place()
    partner, plane, along_z = sum_peers()
    for j in range(6):
        x_ref[j * F : (j + 1) * F, :] = basis_ref[:, j * K : (j + 1) * K]
    y_ref[...] = image_ref[...].astype(jnp.bfloat16)

    def gram(left, right):
        return lax.dot_general(left[...], right[...], (((0,), (0,)), ((), ())), preferred_element_type=jnp.float32)

    lower = lax.broadcasted_iota(jnp.int32, (F, F), 0) >= lax.broadcasted_iota(jnp.int32, (F, F), 1)
    eye = lax.broadcasted_iota(jnp.int32, (F, F), 0) == lax.broadcasted_iota(jnp.int32, (F, F), 1)
    t1[0] = jnp.zeros((4, F), jnp.float32)
    for m in range(3):
        both = gram(x_ref if m < 2 else y_ref, x_ref if m < 1 else y_ref)
        b11, b21, b22 = both[:F, :F], both[F:, :F], both[F:, F:]
        if m == 1:
            b11 = b11 + b11.T
            b21 = b21 + both[:F, F:].T
            b22 = b22 + b22.T
        data[m * 32 : m * 32 + 16] = b21.reshape(16, 8, F)
        data[m * 32 + 16 : m * 32 + 32] = jnp.where(lower, b11, b22).reshape(16, 8, F)
        t1[0, m : m + 1, :] = jnp.sum(jnp.where(eye, b22, 0.0), axis=0, keepdims=True)
    count = [0]
    started = []

    def copy(src, dst, peer):
        n = count[0]
        count[0] += 1
        c = pltpu.make_async_remote_copy(src_ref=src, dst_ref=dst, send_sem=send.at[n], recv_sem=recv.at[n], device_id=peer, device_id_type=MESH)
        c.start()
        started.append(c)
        return c

    first = []
    for dx in (2, 1, 3, 0):
        at = lax.rem(x + dx, 4) * 12
        first.append(copy(data.at[pl.ds((1 - core) * 48 + at, 12)], half_in.at[pl.ds(at, 12)], partner))
    small = copy(t1.at[0], t1.at[1], partner)
    arriving = []
    for n, dx in enumerate((2, 1, 3, 0)):
        at = lax.rem(x + dx, 4) * 12
        first[n].wait_recv()
        half[pl.ds(at, 12)] = data[pl.ds(core * 48 + at, 12)] + half_in[pl.ds(at, 12)]
        for slot, (px, py) in enumerate(PLANE):
            if px == dx:
                piece = at + lax.rem(y + py, 4) * 3
                arriving.append(copy(half.at[pl.ds(piece, 3)], plane_in.at[slot], plane[slot]))
    small.wait_recv()
    here = x * 4 + y
    t3[here] = t1[0] + t1[1]
    tails = [copy(t3.at[here], t3.at[here], plane[slot]) for slot in range(15)]
    total = half[pl.ds(here * 3, 3)]
    for slot in range(15):
        arriving[slot].wait_recv()
        total = total + plane_in[slot]
    z_in[z] = total
    arriving = [copy(z_in.at[z], z_in.at[z], along_z[d - 1]) for d in range(1, 8)]
    for c in tails:
        c.wait_recv()
    tail = t3[0]
    for n in range(1, 16):
        tail = tail + t3[n]
    t4[z] = tail
    tails = [copy(t4.at[z], t4.at[z], along_z[d - 1]) for d in range(1, 8)]
    for c in arriving:
        c.wait_recv()
    total = z_in[0]
    for n in range(1, 8):
        total = total + z_in[n]
    mine = core * 48 + here * 3
    out_ref[pl.ds(mine, 3)] = total
    arriving = [copy(out_ref.at[pl.ds(mine, 3)], out_ref.at[pl.ds(mine, 3)], plane[slot]) for slot in range(15)]
    onward = [copy(out_ref.at[pl.ds(mine, 3)], out_ref.at[pl.ds(mine, 3)], partner)]
    for c in tails:
        c.wait_recv()
    tail = t4[0]
    for n in range(1, 8):
        tail = tail + t4[n]
    tail_ref[0:4, :] = tail
    tail_ref[4:8, :] = tail
    for slot in reversed(range(15)):
        dx, dy = PLANE[slot]
        theirs = core * 48 + (lax.rem(x + 4 - dx, 4) * 4 + lax.rem(y + 4 - dy, 4)) * 3
        arriving[slot].wait_recv()
        onward.append(copy(out_ref.at[pl.ds(theirs, 3)], out_ref.at[pl.ds(theirs, 3)], partner))
    for c in onward:
        c.wait_recv()
    for c in started:
        c.wait_send()


def image_body(
    pairs_hbm, live_hbm, basis_hbm, coords_hbm, lists_hbm, image_ref, sum_ref, tail_ref,
    pairs_ref, live_ref, coords_ref, lists_ref, hist_ref, table_ref, ctab_ref, hot_ref, q_ref, g_ref, blk_ref, rr_ref, it_ref,
    x_ref, y_ref, data, half_in, half, plane_in, z_in, t1, t3, t4, loaded, send, recv, sum_send, sum_recv,
):
    own = 27 * 32
    loads = [
        pltpu.make_async_copy(src, dst, loaded.at[n])
        for n, (src, dst) in enumerate(
            (
                (coords_hbm, coords_ref),
                (basis_hbm, table_ref.at[pl.ds(own, F)]),
                (pairs_hbm, pairs_ref),
                (live_hbm, live_ref),
                (lists_hbm, lists_ref),
            )
        )
    ]
    for c in loads:
        c.start()
    gx, gy, gz = lax.axis_index("gx"), lax.axis_index("gy"), lax.axis_index("gz")
    core = lax.rem(gz, 2)
    far = 2 * core
    partner = {"gz": gz + 1 - 2 * core}
    beyond = {"gz": lax.rem(gz + 7 + 2 * core, 8)}
    up_x, down_x = {"gy": lax.rem(gy + 1, 4)}, {"gy": lax.rem(gy + 3, 4)}
    up_y, down_y = {"gx": lax.rem(gx + 1, 8)}, {"gx": lax.rem(gx + 7, 8)}
    other, plane, along_z = sum_peers()
    barrier = pltpu.get_barrier_semaphore()
    for peer in [partner, beyond, up_x, down_x, up_y, down_y, other] + plane + along_z:
        pl.semaphore_signal(barrier, inc=1, device_id=peer, device_id_type=MESH)

    loads[0].wait()
    flat = coords_ref[...]
    high = flat.astype(jnp.bfloat16).astype(jnp.float32)
    mid = (flat - high).astype(jnp.bfloat16).astype(jnp.float32)
    parts = jnp.concatenate([high, mid, flat - high - mid, jnp.zeros((112, F), jnp.float32)], axis=0)
    ctab_ref[own : own + F, :] = jnp.transpose(parts).astype(jnp.bfloat16)
    ctab_ref[13 * 32 : 14 * 32, :] = ctab_ref[own : own + 32, :]
    loads[1].wait()
    table_ref[13 * 32 : 14 * 32, :] = table_ref[own : own + 32, :]
    pl.semaphore_wait(barrier, 29)

    count = [0]
    started = []

    def copy(src, dst, peer):
        n = count[0]
        count[0] += 1
        c = pltpu.make_async_remote_copy(src_ref=src, dst_ref=dst, send_sem=send.at[n], recv_sem=recv.at[n], device_id=peer, device_id_type=MESH)
        c.start()
        started.append(c)
        return c

    edges, corners = ((1, 0), (1, 2), (0, 1), (2, 1)), ((0, 0), (2, 2), (0, 2), (2, 0))

    class Ghosts:
        def __init__(self, ref):
            self.ref = ref

        def slab(self, a, b, e):
            return self.ref.at[pl.ds(pl.multiple_of((9 * a + 3 * b + e) * 32, 32), 32)]

        def first_hops(self, e):
            return [copy(self.slab(1, 1, e), self.slab(a, b, e), peer) for (a, b), peer in zip(edges, (up_x, down_x, up_y, down_y))]

        def second_hops(self, e):
            return [
                copy(self.slab(a, b, e), self.slab(c, d, e), peer)
                for (a, b), (c, d), peer in zip(edges, corners, (up_y, down_y, down_x, up_x))
            ]

        def forward(self, places):
            return [copy(self.slab(a, b, 1), self.slab(a, b, far), partner) for a, b in places]

        def one(self):
            beyond_copy = copy(self.slab(1, 1, 1), self.slab(1, 1, 2 - far), beyond)
            self.due = [beyond_copy] + self.first_hops(1)
            self.rest = [copy(self.slab(1, 1, 1), self.slab(1, 1, far), partner)]

        def two(self):
            for c in self.due:
                c.wait_recv()
            self.due = self.first_hops(far) + self.second_hops(1)
            self.rest = self.rest + self.forward(edges)

        def three(self):
            for c in self.due:
                c.wait_recv()
            self.rest = self.rest + self.second_hops(far) + self.forward(corners)

        def done(self):
            for c in self.rest:
                c.wait_recv()

    near, rows = Ghosts(ctab_ref), Ghosts(table_ref)
    near.one()
    rows.one()
    chunk = counter(pairs_ref, live_ref, hist_ref)
    loads[2].wait()
    loads[3].wait()
    chunk(0)
    near.two()
    chunk(1)
    near.three()
    rows.two()
    chunk(2)
    chunk(3)
    loads[4].wait()
    for s in range(NB):
        listed = jnp.broadcast_to(lists_ref[s : s + 1, :], (own + F, F))
        hot = lax.broadcasted_iota(jnp.int32, (own + F, F), 0) == listed
        hot_ref[:, s * F : (s + 1) * F] = jnp.where(hot, 1.0, 0.0).astype(jnp.bfloat16)
    rows.three()
    near.done()
    place_partners(ctab_ref, hot_ref, q_ref)
    moments(hist_ref, coords_ref, q_ref, blk_ref, rr_ref)
    rows.done()
    for c in started:
        c.wait_send()
    apply_blocks(table_ref, hot_ref, image_ref, g_ref, blk_ref, it_ref)
    total_grams(
        image_ref, table_ref.at[pl.ds(own, F)], sum_ref, tail_ref, x_ref, y_ref,
        data, half_in, half, plane_in, z_in, t1, t3, t4, sum_send, sum_recv,
    )


def images_and_sums(pairs, live, basis, coords, lists):
    rows = 27 * 32 + F

    def wide(*shape):
        return pltpu.VMEM(shape, jnp.float32)

    def half_wide(*shape):
        return pltpu.VMEM(shape, jnp.bfloat16)

    def semaphores(n):
        return pltpu.SemaphoreType.DMA((n,))

    return pl.pallas_call(
        image_body,
        out_shape=(
            jax.ShapeDtypeStruct((6 * F, K), jnp.float32),
            jax.ShapeDtypeStruct((96, 8, F), jnp.float32),
            jax.ShapeDtypeStruct((8, F), jnp.float32),
        ),
        in_specs=[pl.BlockSpec(memory_space=pltpu.MemorySpace.HBM)] * 5,
        out_specs=(VM, VM, VM),
        scratch_shapes=[
            pltpu.VMEM(pairs.shape, jnp.int32),
            pltpu.VMEM(live.shape, jnp.int32),
            wide(48, F),
            pltpu.VMEM((NB, F), jnp.int32),
            wide(4096, F),
            half_wide(rows, 6 * K),
            half_wide(rows, K),
            half_wide(rows, NB * F),
            wide(768, F),
            wide(6 * K, NB * F),
            wide(576, F),
            wide(112, F),
            wide(6 * K, F),
            half_wide(6 * F, K),
            half_wide(6 * F, K),
            wide(96, 8, F),
            wide(48, 8, F),
            wide(48, 8, F),
            wide(15, 3, 8, F),
            wide(8, 3, 8, F),
            wide(2, 4, F),
            wide(16, 4, F),
            wide(8, 4, F),
            semaphores(5),
            semaphores(52),
            semaphores(52),
            semaphores(80),
            semaphores(80),
        ],
        compiler_params=pltpu.CompilerParams(collective_id=2, has_side_effects=True, vmem_limit_bytes=66_000_000),
        cost_estimate=pl.CostEstimate(flops=16 * 10**9, bytes_accessed=3 * 10**6, transcendentals=0),
        name="images_and_sums",
    )(pairs, live, basis, coords, lists)


def dot32(p, q, dims):
    return lax.dot_general(p, q, (dims, ((), ())), precision=lax.Precision.HIGHEST, preferred_element_type=jnp.float32)


NT = ((1,), (1,))
NN = ((1,), (0,))


def cut(x):
    high = x.astype(jnp.bfloat16)
    rest = x - high.astype(jnp.float32)
    mid = rest.astype(jnp.bfloat16)
    return high, mid, (rest - mid.astype(jnp.float32)).astype(jnp.bfloat16)


def outer(p, q):
    ph, pm, pl_ = cut(p)
    qh, qm, ql = cut(q)
    left = jnp.concatenate([ph, ph, pm, ph, pl_, pm], axis=0)
    right = jnp.concatenate([qh, qm, qh, ql, qh, qm], axis=0)
    return lax.dot_general(left, right, (((0,), (0,)), ((), ())), preferred_element_type=jnp.float32)


def eliminate(mats):
    sub = lax.broadcasted_iota(jnp.int32, (8, F), 0)
    lane = lax.broadcasted_iota(jnp.int32, (8, F), 1)
    tiles = [[m[8 * t : 8 * t + 8, :] for t in range(16)] for m in mats]

    def columns(tile, t):
        return [jnp.broadcast_to(tile[:, 8 * t + k : 8 * t + k + 1], (8, F)) for k in range(8)]

    def spread(tile, r):
        return jnp.broadcast_to(tile[r : r + 1, :], (8, F))

    for t in range(16):
        inside = (lane >= 8 * t) & (lane < 8 * t + 8)
        for rows in tiles:
            top = rows[t]
            c = columns(top, t)
            lead = t + 1 < 16
            if lead:
                after = rows[t + 1]
                ca = columns(after, t)
            scaled = []
            for j in range(8):
                at = lane == 8 * t + j
                pivot = [spread(c[k], j) for k in range(j, 8)]
                inv = 1.0 / pivot[0]
                row = jnp.where(at, 1.0, spread(top, j))
                scaled.append(row * inv)
                if j < 7:
                    f = jnp.where(sub > j, c[j] * inv, 0.0)
                    for k in range(j + 1, 8):
                        c[k] = c[k] - f * pivot[k - j]
                    top = jnp.where(at & (sub > j), 0.0, top) - f * row
                if lead:
                    fa = ca[j] * inv
                    for k in range(j + 1, 8):
                        ca[k] = ca[k] - fa * pivot[k - j]
                    after = jnp.where(at, 0.0, after) - fa * row
            rows[t] = top
            if lead:
                rows[t + 1] = after
            if t + 2 < 16:
                packed = jnp.concatenate([s[0:1, :] for s in scaled], axis=0)
                plain = jnp.where(lane == sub + 8 * t, 1.0, jnp.where(inside & (lane > sub + 8 * t), 0.0, top))
                taken = outer(packed, plain)
                for u in range(t + 2, 16):
                    rows[u] = jnp.where(inside, 0.0, rows[u]) - taken[8 * u : 8 * u + 8, :]
    out = []
    for rows in tiles:
        full = []
        for t in range(16):
            diag = lane == sub + 8 * t
            d = jnp.sum(jnp.where(diag, rows[t], 0.0), axis=1, keepdims=True)
            keep = jnp.where(lane < sub + 8 * t, rows[t], jnp.where(diag, 1.0, 0.0))
            full.append(keep * jnp.broadcast_to(1.0 / jnp.sqrt(d), (8, F)))
        out.append(jnp.concatenate(full, axis=0))
    return out


def solve_body(sum_hbm, tail_hbm, image_hbm, next_ref, ritz_ref, sum_ref, tail_ref, image_ref, mat_ref, inv_ref, loaded, *, total_rows):
    loads = [
        pltpu.make_async_copy(src, dst, loaded.at[n])
        for n, (src, dst) in enumerate(((sum_hbm, sum_ref), (tail_hbm, tail_ref), (image_hbm, image_ref)))
    ]
    for c in loads:
        c.start()
    loads[0].wait()
    loads[1].wait()
    scale = 1.0 / total_rows
    sub = lax.broadcasted_iota(jnp.int32, (F, F), 0)
    lane = lax.broadcasted_iota(jnp.int32, (F, F), 1)

    def unpack(m, half):
        b21 = sum_ref[m * 32 : m * 32 + 16].reshape(F, F) * half
        both = sum_ref[m * 32 + 16 : m * 32 + 32].reshape(F, F) * half
        flip = both.T
        b11 = jnp.where(sub >= lane, both, flip)
        diag = jnp.broadcast_to(tail_ref[m : m + 1, :] * half, (F, F))
        b22 = jnp.where(sub < lane, both, jnp.where(sub == lane, diag, flip))
        return b11, b21, b22

    s11, s21, s22 = unpack(0, scale)
    w11, w21, w22 = unpack(2, scale)
    mat_ref[0] = s11
    mat_ref[1] = w11
    for n, (b21, b22) in enumerate(((s21, s22), (w21, w22))):
        mat_ref[2 + 2 * n] = b21
        mat_ref[3 + 2 * n] = b22

    def half_step(step, carry):
        s, w = eliminate([mat_ref[0], mat_ref[1]])
        for n, top in enumerate((s, w)):
            inv_ref[2 * step + n] = top

        @pl.when(step == 0)
        def _():
            for n, top in enumerate((s, w)):
                left = dot32(mat_ref[2 + 2 * n], top, NT)
                mat_ref[n] = mat_ref[3 + 2 * n] - dot32(left, left, NT)
                mat_ref[2 + 2 * n] = left

        return carry

    lax.fori_loop(0, 2, half_step, 0)

    def whole(n):
        top, low = inv_ref[n], inv_ref[2 + n]
        corner = -dot32(low, dot32(mat_ref[2 + 2 * n], top, NN), NN)
        return jnp.concatenate(
            [jnp.concatenate([top, jnp.zeros((F, F), jnp.float32)], axis=1), jnp.concatenate([corner, low], axis=1)], axis=0
        )

    q11, q21, q22 = unpack(1, 0.5 * scale)
    cross_sum = jnp.concatenate([jnp.concatenate([q11, q21.T], axis=1), jnp.concatenate([q21, q22], axis=1)], axis=0)
    s_inv = whole(0)
    ritz_ref[...] = dot32(dot32(s_inv, cross_sum, NN), s_inv, NT)
    w_inv = whole(1)
    loads[2].wait()
    for j in range(6):
        next_ref[:, j * K : (j + 1) * K] = dot32(image_ref[j * F : (j + 1) * F, :], w_inv, NT)


def solve(sums, tail, image, total_rows):
    return pl.pallas_call(
        functools.partial(solve_body, total_rows=total_rows),
        out_shape=(jax.ShapeDtypeStruct((F, 6 * K), jnp.float32), jax.ShapeDtypeStruct((K, K), jnp.float32)),
        in_specs=[pl.BlockSpec(memory_space=pltpu.MemorySpace.HBM)] * 3,
        out_specs=(VM, VM),
        scratch_shapes=[
            pltpu.VMEM((96, 8, F), jnp.float32),
            pltpu.VMEM((8, F), jnp.float32),
            pltpu.VMEM((6 * F, K), jnp.float32),
            pltpu.VMEM((6, F, F), jnp.float32),
            pltpu.VMEM((4, F, F), jnp.float32),
            pltpu.SemaphoreType.DMA((3,)),
        ],
        compiler_params=pltpu.CompilerParams(vmem_limit_bytes=66_000_000),
        name="solve",
    )(sums, tail, image)


def per_device(coordinates, neighbours, pair_index, pair_live, basis):
    own = coordinates[0, 0, 0].reshape(48, F)
    live = pair_live[0, 0, 0].reshape(1, -1)
    image, sums, tail = images_and_sums(pair_index[0, 0, 0], live, basis[0, 0, 0], own, neighbours[0, 0, 0])
    next_rows, ritz = solve(sums, tail, image, 6.0 * F * 256)
    return next_rows.reshape(1, 1, 1, F, 6 * K), ritz


def solution(mesh):
    cells = [P("gx", "gy", "gz", *([None] * n)) for n in (3, 2, 2, 1, 2)]
    return jax.shard_map(per_device, mesh=mesh, in_specs=tuple(cells), out_specs=(cells[4], P()), check_vma=False)
```

```python
import functools
import jax
import jax.numpy as jnp
from jax import lax
from jax.experimental import pallas as pl
from jax.experimental.pallas import tpu as pltpu
from jax.sharding import PartitionSpec as P

VM = pl.BlockSpec(memory_space=pltpu.VMEM)
F = 128
K = 256
NB = 16
PB = 4096.0
CHUNK = 3840


def counter(pairs_ref, live_ref, hist_ref):
    rows = lax.broadcasted_iota(jnp.int32, (256, CHUNK), 0)
    zero = jnp.zeros((256, CHUNK), jnp.float32)

    def chunk(c):
        at = slice(c * CHUNK, (c + 1) * CHUNK)
        f = pairs_ref[0:1, at]
        s = pairs_ref[1:2, at]
        a = pairs_ref[2:3, at]
        b = pairs_ref[3:4, at]
        live = live_ref[0:1, at]
        value = (live * jnp.where(a >= 8, int(PB), 1)).astype(jnp.float32)
        col = ((a >> 2) & 1) * 128 + f
        right = jnp.where(rows == col, jnp.broadcast_to(value, (256, CHUNK)), zero).astype(jnp.bfloat16)
        hot = rows == (b * 16 + s)
        low = a & 3
        for part in range(4):
            mark = jnp.broadcast_to((low == part).astype(jnp.float32), (256, CHUNK))
            left = jnp.where(hot, mark, zero).astype(jnp.bfloat16)
            got = lax.dot_general(left, right, (((1,), (1,)), ((), ())), preferred_element_type=jnp.float32)
            high = jnp.floor(got * (1.0 / PB))
            lower = got - PB * high
            for mid in range(2):
                lanes = slice(mid * 128, (mid + 1) * 128)
                for top, val in ((0, lower), (1, high)):
                    a = top * 8 + mid * 4 + part
                    here = slice(a * 256, (a + 1) * 256)
                    if c == 0:
                        hist_ref[here, :] = val[:, lanes]
                    else:
                        hist_ref[here, :] = hist_ref[here, :] + val[:, lanes]

    return chunk


def cross(p, q):
    return [
        p[1] * q[2] - p[2] * q[1],
        p[2] * q[0] - p[0] * q[2],
        p[0] * q[1] - p[1] * q[0],
    ]


SYM = ((0, 0), (0, 1), (0, 2), (1, 1), (1, 2), (2, 2))


def symmetric(six):
    return [[six[0], six[1], six[2]], [six[1], six[3], six[4]], [six[2], six[4], six[5]]]


def moments(hist_ref, coords_ref, q_ref, blk_ref, rr_ref):
    blk_ref[...] = jnp.zeros_like(blk_ref)
    rr_ref[...] = jnp.zeros_like(rr_ref)
    own = [jnp.sum(coords_ref[16 * c : 16 * c + 16, :], axis=0, keepdims=True) * (1.0 / 16.0) for c in range(3)]

    def tile(c, b, half):
        return q_ref[(c * 16 + b) * 16 + half * 8 : (c * 16 + b) * 16 + half * 8 + 8, :]

    centres = []
    for half in range(2):
        centre = []
        for c in range(3):
            total = tile(c, 0, half)
            for b in range(1, 16):
                total = total + tile(c, b, half)
            centre.append(total * (1.0 / 16.0))
        centres.append(centre)

    def atom(a, half):
        centre = centres[half]
        r = [jnp.broadcast_to(coords_ref[pl.ds(c * 16 + a, 1), :], (8, F)) for c in range(3)]
        arm = [r[c] - jnp.broadcast_to(own[c], (8, F)) for c in range(3)]
        m = [None] * 6
        n = [[None] * 3 for _ in range(3)]
        for b in range(16):
            q = [tile(c, b, half) for c in range(3)]
            d = [r[c] - q[c] for c in range(3)]
            count = hist_ref[pl.ds(pl.multiple_of(a * 256 + b * 16 + half * 8, 8), 8), :]
            w = (0.01 * count) / jnp.maximum(d[0] * d[0] + d[1] * d[1] + d[2] * d[2], 1.0)
            wd = [w * d[c] for c in range(3)]
            turn = cross([q[c] - centre[c] for c in range(3)], d)
            for k, (j, i) in enumerate(SYM):
                t = wd[j] * d[i]
                m[k] = t if m[k] is None else m[k] + t
            for j in range(3):
                for i in range(3):
                    t = wd[j] * turn[i]
                    n[j][i] = t if n[j][i] is None else n[j][i] + t
        m = symmetric(m)
        rt = [cross(arm, [m[j][i] for j in range(3)]) for i in range(3)]
        rn = [cross(arm, [n[j][i] for j in range(3)]) for i in range(3)]
        for j in range(3):
            for i in range(3):
                for jj, ii, val in ((j, i, m[j][i]), (j, 3 + i, n[j][i]), (3 + j, i, rt[i][j]), (3 + j, 3 + i, rn[i][j])):
                    here = pl.ds((jj * 6 + ii) * 16 + half * 8, 8)
                    blk_ref[here, :] = blk_ref[here, :] - val
        for j in range(3):
            rr = cross(arm, [rt[i][j] for i in range(3)])
            for i in range(3):
                here = pl.ds((j * 3 + i) * 8, 8)
                rr_ref[here, :] = rr_ref[here, :] + rr[i]

    def both(a, carry):
        for half in range(2):
            atom(a, half)
        return carry

    lax.fori_loop(0, 16, both, 0)
    for j in range(3):
        for i in range(3):
            tt = jnp.sum(blk_ref[pl.ds((j * 6 + i) * 16, 16), :], axis=0, keepdims=True)
            rt = jnp.sum(blk_ref[pl.ds(((3 + j) * 6 + i) * 16, 16), :], axis=0, keepdims=True)
            rr = jnp.sum(rr_ref[pl.ds((j * 3 + i) * 8, 8), :], axis=0, keepdims=True)
            for jj, ii, val in ((j, i, -tt), (3 + j, i, -rt), (i, 3 + j, -rt), (3 + j, 3 + i, rr)):
                here = pl.ds((jj * 6 + ii) * 16, 1)
                rr_ref[72 + jj * 6 + ii : 73 + jj * 6 + ii, :] = val
    for ji in range(36):
        here = pl.ds(ji * 16, 1)
        blk_ref[here, :] = blk_ref[here, :] + rr_ref[72 + ji : 73 + ji, :]


KC = 32


def chosen(table_ref, columns, hot_ref):
    return lax.dot_general(table_ref[:, columns], hot_ref[...], (((0,), (0,)), ((), ())), preferred_element_type=jnp.float32)


def place_partners(ctab_ref, hot_ref, q_ref):
    got = chosen(ctab_ref, slice(0, 256), hot_ref)
    pos = got[0:48] + got[48:96] + got[96:144]
    for s in range(NB):
        for t in range(6):
            q_ref[pl.ds(t * 128 + s, 8, stride=16), :] = pos[t * 8 : t * 8 + 8, s * F : (s + 1) * F]


def gather_rows(table_ref, hot_ref, g_ref):
    for part in range(6):
        at = slice(part * K, (part + 1) * K)
        g_ref[at, :] = chosen(table_ref, at, hot_ref)


def apply_blocks(image_ref, g_ref, blk_ref, it_ref):
    def piece(kc, carry):
        start = pl.multiple_of(kc * KC, KC)

        def slot(s, totals):
            totals = list(totals)
            lanes = pl.ds(pl.multiple_of(s * F, F), F)
            for i in range(6):
                g = g_ref[pl.ds(i * K + start, KC), lanes]
                for j in range(6):
                    row = blk_ref[pl.ds((j * 6 + i) * 16 + s, 1), :]
                    totals[j] = totals[j] + jnp.broadcast_to(row, (KC, F)) * g
            return tuple(totals)

        totals = lax.fori_loop(0, NB, slot, tuple(jnp.zeros((KC, F), jnp.float32) for _ in range(6)))
        for j in range(6):
            it_ref[pl.ds(j * K + start, KC), :] = totals[j]
        return carry

    lax.fori_loop(0, K // KC, piece, 0)
    for j in range(6):
        image_ref[j * F : (j + 1) * F, :] = jnp.transpose(it_ref[j * K : (j + 1) * K, :])


MESH = pl.DeviceIdType.MESH


def place():
    gx, gy, gz = lax.axis_index("gx"), lax.axis_index("gy"), lax.axis_index("gz")
    y, z = lax.rem(gx, 4), lax.div(gz, 2) * 2 + lax.div(gx, 4)
    return gy, y, z, lax.rem(gz, 2)


def device(x, y, z, core):
    return {"gx": lax.rem(z, 2) * 4 + y, "gy": x, "gz": lax.div(z, 2) * 2 + core}


PLANE = [(dx, dy) for dx in (2, 1, 3, 0) for dy in (2, 1, 3, 0)][:15]


def sum_peers():
    x, y, z, core = place()
    plane = [device(lax.rem(x + dx, 4), lax.rem(y + dy, 4), z, core) for dx, dy in PLANE]
    along_z = [device(x, y, lax.rem(z + d, 8), core) for d in range(1, 8)]
    return device(x, y, z, 1 - core), plane, along_z


def gram(left, right):
    return lax.dot_general(left[...], right[...], (((0,), (0,)), ((), ())), preferred_element_type=jnp.float32)


def basis_gram(basis_ref, x_ref, data):
    for j in range(6):
        x_ref[j * F : (j + 1) * F, :] = basis_ref[:, j * K : (j + 1) * K]
    both = gram(x_ref, x_ref)
    for n, block in enumerate((both[F:, :F], both[:F, :F], both[F:, F:], jnp.zeros((F, F), jnp.float32))):
        data[n * 16 : n * 16 + 16] = block.reshape(16, 8, F)


def image_grams(image_ref, x_ref, y_ref, data, tail):
    y_ref[...] = image_ref[...].astype(jnp.bfloat16)
    lower = lax.broadcasted_iota(jnp.int32, (F, F), 0) >= lax.broadcasted_iota(jnp.int32, (F, F), 1)
    eye = lax.broadcasted_iota(jnp.int32, (F, F), 0) == lax.broadcasted_iota(jnp.int32, (F, F), 1)
    tail[0] = jnp.zeros((4, F), jnp.float32)
    for m, left in enumerate((x_ref, y_ref)):
        both = gram(left, y_ref)
        b11, b21, b22 = both[:F, :F], both[F:, :F], both[F:, F:]
        if m == 0:
            b11 = b11 + b11.T
            b21 = b21 + both[:F, F:].T
            b22 = b22 + b22.T
        data[m * 32 : m * 32 + 16] = b21.reshape(16, 8, F)
        data[m * 32 + 16 : m * 32 + 32] = jnp.where(lower, b11, b22).reshape(16, 8, F)
        tail[0, m : m + 1, :] = jnp.sum(jnp.where(eye, b22, 0.0), axis=0, keepdims=True)


def summing(data, half_in, half, plane_in, z_in, out_ref, send, recv, tails=None):
    x, y, z, core = place()
    partner, plane, along_z = sum_peers()
    here = x * 4 + y
    count = [0]
    started = []

    def copy(src, dst, peer):
        n = count[0]
        count[0] += 1
        c = pltpu.make_async_remote_copy(src_ref=src, dst_ref=dst, send_sem=send.at[n], recv_sem=recv.at[n], device_id=peer, device_id_type=MESH)
        c.start()
        started.append(c)
        return c

    first = []
    for dx in (2, 1, 3, 0):
        at = lax.rem(x + dx, 4) * 8
        first.append(copy(data.at[pl.ds((1 - core) * 32 + at, 8)], half_in.at[pl.ds(at, 8)], partner))
    if tails:
        t1, t3, t4, tail_ref = tails
        small = copy(t1.at[0], t1.at[1], partner)
    yield
    arriving = []
    for n, dx in enumerate((2, 1, 3, 0)):
        at = lax.rem(x + dx, 4) * 8
        first[n].wait_recv()
        half[pl.ds(at, 8)] = data[pl.ds(core * 32 + at, 8)] + half_in[pl.ds(at, 8)]
        for slot, (px, py) in enumerate(PLANE):
            if px == dx:
                piece = at + lax.rem(y + py, 4) * 2
                arriving.append(copy(half.at[pl.ds(piece, 2)], plane_in.at[slot], plane[slot]))
    if tails:
        small.wait_recv()
        t3[here] = t1[0] + t1[1]
        more = [copy(t3.at[here], t3.at[here], plane[slot]) for slot in range(15)]
    yield
    total = half[pl.ds(here * 2, 2)]
    for slot in range(15):
        arriving[slot].wait_recv()
        total = total + plane_in[slot]
    z_in[z] = total
    arriving = [copy(z_in.at[z], z_in.at[z], along_z[d - 1]) for d in range(1, 8)]
    if tails:
        for c in more:
            c.wait_recv()
        tail = t3[0]
        for n in range(1, 16):
            tail = tail + t3[n]
        t4[z] = tail
        more = [copy(t4.at[z], t4.at[z], along_z[d - 1]) for d in range(1, 8)]
    yield
    for c in arriving:
        c.wait_recv()
    total = z_in[0]
    for n in range(1, 8):
        total = total + z_in[n]
    mine = core * 32 + here * 2
    out_ref[pl.ds(mine, 2)] = total
    arriving = [copy(out_ref.at[pl.ds(mine, 2)], out_ref.at[pl.ds(mine, 2)], plane[slot]) for slot in range(15)]
    onward = [copy(out_ref.at[pl.ds(mine, 2)], out_ref.at[pl.ds(mine, 2)], partner)]
    if tails:
        for c in more:
            c.wait_recv()
        tail = t4[0]
        for n in range(1, 8):
            tail = tail + t4[n]
        tail_ref[0:4, :] = tail
        tail_ref[4:8, :] = tail
    yield
    for slot in reversed(range(15)):
        dx, dy = PLANE[slot]
        theirs = core * 32 + (lax.rem(x + 4 - dx, 4) * 4 + lax.rem(y + 4 - dy, 4)) * 2
        arriving[slot].wait_recv()
        onward.append(copy(out_ref.at[pl.ds(theirs, 2)], out_ref.at[pl.ds(theirs, 2)], partner))
    yield
    for c in onward:
        c.wait_recv()
    for c in started:
        c.wait_send()


def image_body(
    pairs_hbm, live_hbm, basis_hbm, coords_hbm, lists_hbm, image_ref, basis_sum_ref, sum_ref, tail_ref,
    pairs_ref, live_ref, coords_ref, lists_ref, hist_ref, table_ref, ctab_ref, hot_ref, q_ref, g_ref, blk_ref, rr_ref, it_ref,
    x_ref, y_ref, basis_data, basis_half_in, basis_half, basis_plane_in, basis_z_in, data, half_in, half, plane_in, z_in, t1, t3, t4,
    loaded, send, recv, basis_send, basis_recv, sum_send, sum_recv,
):
    own = 27 * 32
    loads = [
        pltpu.make_async_copy(src, dst, loaded.at[n])
        for n, (src, dst) in enumerate(
            (
                (coords_hbm, coords_ref),
                (basis_hbm, table_ref.at[pl.ds(own, F)]),
                (pairs_hbm, pairs_ref),
                (live_hbm, live_ref),
                (lists_hbm, lists_ref),
            )
        )
    ]
    for c in loads:
        c.start()
    gx, gy, gz = lax.axis_index("gx"), lax.axis_index("gy"), lax.axis_index("gz")
    core = lax.rem(gz, 2)
    far = 2 * core
    partner = {"gz": gz + 1 - 2 * core}
    beyond = {"gz": lax.rem(gz + 7 + 2 * core, 8)}
    up_x, down_x = {"gy": lax.rem(gy + 1, 4)}, {"gy": lax.rem(gy + 3, 4)}
    up_y, down_y = {"gx": lax.rem(gx + 1, 8)}, {"gx": lax.rem(gx + 7, 8)}
    other, plane, along_z = sum_peers()
    barrier = pltpu.get_barrier_semaphore()
    for peer in [partner, beyond, up_x, down_x, up_y, down_y, other] + plane + along_z:
        pl.semaphore_signal(barrier, inc=1, device_id=peer, device_id_type=MESH)

    loads[0].wait()
    flat = coords_ref[...]
    high = flat.astype(jnp.bfloat16).astype(jnp.float32)
    mid = (flat - high).astype(jnp.bfloat16).astype(jnp.float32)
    parts = jnp.concatenate([high, mid, flat - high - mid, jnp.zeros((112, F), jnp.float32)], axis=0)
    ctab_ref[own : own + F, :] = jnp.transpose(parts).astype(jnp.bfloat16)
    ctab_ref[13 * 32 : 14 * 32, :] = ctab_ref[own : own + 32, :]
    loads[1].wait()
    table_ref[13 * 32 : 14 * 32, :] = table_ref[own : own + 32, :]
    basis_gram(table_ref.at[pl.ds(own, F)], x_ref, basis_data)
    chunk = counter(pairs_ref, live_ref, hist_ref)
    loads[2].wait()
    loads[3].wait()
    chunk(0)
    pl.semaphore_wait(barrier, 29)

    count = [0]
    started = []

    def copy(src, dst, peer):
        n = count[0]
        count[0] += 1
        c = pltpu.make_async_remote_copy(src_ref=src, dst_ref=dst, send_sem=send.at[n], recv_sem=recv.at[n], device_id=peer, device_id_type=MESH)
        c.start()
        started.append(c)
        return c

    edges, corners = ((1, 0), (1, 2), (0, 1), (2, 1)), ((0, 0), (2, 2), (0, 2), (2, 0))

    class Ghosts:
        def __init__(self, ref):
            self.ref = ref

        def slab(self, a, b, e):
            return self.ref.at[pl.ds(pl.multiple_of((9 * a + 3 * b + e) * 32, 32), 32)]

        def first_hops(self, e):
            return [copy(self.slab(1, 1, e), self.slab(a, b, e), peer) for (a, b), peer in zip(edges, (up_x, down_x, up_y, down_y))]

        def second_hops(self, e):
            return [
                copy(self.slab(a, b, e), self.slab(c, d, e), peer)
                for (a, b), (c, d), peer in zip(edges, corners, (up_y, down_y, down_x, up_x))
            ]

        def forward(self, places):
            return [copy(self.slab(a, b, 1), self.slab(a, b, far), partner) for a, b in places]

        def one(self):
            beyond_copy = copy(self.slab(1, 1, 1), self.slab(1, 1, 2 - far), beyond)
            self.due = [beyond_copy] + self.first_hops(1)
            self.rest = [copy(self.slab(1, 1, 1), self.slab(1, 1, far), partner)]

        def two(self):
            for c in self.due:
                c.wait_recv()
            self.due = self.first_hops(far) + self.second_hops(1)
            self.rest = self.rest + self.forward(edges)

        def three(self):
            for c in self.due:
                c.wait_recv()
            self.rest = self.rest + self.second_hops(far) + self.forward(corners)

        def done(self):
            for c in self.rest:
                c.wait_recv()

    near, rows = Ghosts(ctab_ref), Ghosts(table_ref)
    near.one()
    rows.one()
    basis_sum = summing(
        basis_data, basis_half_in, basis_half, basis_plane_in, basis_z_in, basis_sum_ref, basis_send, basis_recv
    )
    next(basis_sum)
    chunk(1)
    near.two()
    chunk(2)
    near.three()
    rows.two()
    chunk(3)
    loads[4].wait()
    for s in range(NB):
        listed = jnp.broadcast_to(lists_ref[s : s + 1, :], (own + F, F))
        hot = lax.broadcasted_iota(jnp.int32, (own + F, F), 0) == listed
        hot_ref[:, s * F : (s + 1) * F] = jnp.where(hot, 1.0, 0.0).astype(jnp.bfloat16)
    near.done()
    place_partners(ctab_ref, hot_ref, q_ref)
    rows.three()
    next(basis_sum)
    moments(hist_ref, coords_ref, q_ref, blk_ref, rr_ref)
    next(basis_sum)
    rows.done()
    for c in started:
        c.wait_send()
    gather_rows(table_ref, hot_ref, g_ref)
    next(basis_sum)
    apply_blocks(image_ref, g_ref, blk_ref, it_ref)
    image_grams(image_ref, x_ref, y_ref, data, t1)
    sums = summing(data, half_in, half, plane_in, z_in, sum_ref, sum_send, sum_recv, (t1, t3, t4, tail_ref))
    next(sums)
    next(basis_sum)
    for _ in sums:
        pass
    for _ in basis_sum:
        pass


def images_and_sums(pairs, live, basis, coords, lists):
    rows = 27 * 32 + F

    def wide(*shape):
        return pltpu.VMEM(shape, jnp.float32)

    def half_wide(*shape):
        return pltpu.VMEM(shape, jnp.bfloat16)

    def semaphores(n):
        return pltpu.SemaphoreType.DMA((n,))

    return pl.pallas_call(
        image_body,
        out_shape=(
            jax.ShapeDtypeStruct((6 * F, K), jnp.float32),
            jax.ShapeDtypeStruct((64, 8, F), jnp.float32),
            jax.ShapeDtypeStruct((64, 8, F), jnp.float32),
            jax.ShapeDtypeStruct((8, F), jnp.float32),
        ),
        in_specs=[pl.BlockSpec(memory_space=pltpu.MemorySpace.HBM)] * 5,
        out_specs=(VM, VM, VM, VM),
        scratch_shapes=[
            pltpu.VMEM(pairs.shape, jnp.int32),
            pltpu.VMEM(live.shape, jnp.int32),
            wide(48, F),
            pltpu.VMEM((NB, F), jnp.int32),
            wide(4096, F),
            half_wide(rows, 6 * K),
            half_wide(rows, K),
            half_wide(rows, NB * F),
            wide(768, F),
            wide(6 * K, NB * F),
            wide(576, F),
            wide(112, F),
            wide(6 * K, F),
            half_wide(6 * F, K),
            half_wide(6 * F, K),
            *([wide(64, 8, F), wide(32, 8, F), wide(32, 8, F), wide(15, 2, 8, F), wide(8, 2, 8, F)] * 2),
            wide(2, 4, F),
            wide(16, 4, F),
            wide(8, 4, F),
            semaphores(5),
            semaphores(52),
            semaphores(52),
            semaphores(57),
            semaphores(57),
            semaphores(80),
            semaphores(80),
        ],
        compiler_params=pltpu.CompilerParams(collective_id=2, has_side_effects=True, vmem_limit_bytes=66_000_000),
        cost_estimate=pl.CostEstimate(flops=16 * 10**9, bytes_accessed=3 * 10**6, transcendentals=0),
        name="images_and_sums",
    )(pairs, live, basis, coords, lists)


def dot32(p, q, dims):
    return lax.dot_general(p, q, (dims, ((), ())), precision=lax.Precision.HIGHEST, preferred_element_type=jnp.float32)


NT = ((1,), (1,))
NN = ((1,), (0,))


def cut(x):
    high = x.astype(jnp.bfloat16)
    rest = x - high.astype(jnp.float32)
    mid = rest.astype(jnp.bfloat16)
    return high, mid, (rest - mid.astype(jnp.float32)).astype(jnp.bfloat16)


def outer(p, q):
    ph, pm, pl_ = cut(p)
    qh, qm, ql = cut(q)
    left = jnp.concatenate([ph, ph, pm, ph, pl_, pm], axis=0)
    right = jnp.concatenate([qh, qm, qh, ql, qh, qm], axis=0)
    return lax.dot_general(left, right, (((0,), (0,)), ((), ())), preferred_element_type=jnp.float32)


def eliminate(mats):
    sub = lax.broadcasted_iota(jnp.int32, (8, F), 0)
    lane = lax.broadcasted_iota(jnp.int32, (8, F), 1)
    tiles = [[m[8 * t : 8 * t + 8, :] for t in range(16)] for m in mats]

    def columns(tile, t):
        return [jnp.broadcast_to(tile[:, 8 * t + k : 8 * t + k + 1], (8, F)) for k in range(8)]

    def spread(tile, r):
        return jnp.broadcast_to(tile[r : r + 1, :], (8, F))

    for t in range(16):
        inside = (lane >= 8 * t) & (lane < 8 * t + 8)
        for rows in tiles:
            top = rows[t]
            c = columns(top, t)
            lead = t + 1 < 16
            if lead:
                after = rows[t + 1]
                ca = columns(after, t)
            scaled = []
            for j in range(8):
                at = lane == 8 * t + j
                pivot = [spread(c[k], j) for k in range(j, 8)]
                inv = 1.0 / pivot[0]
                row = jnp.where(at, 1.0, spread(top, j))
                scaled.append(row * inv)
                if j < 7:
                    f = jnp.where(sub > j, c[j] * inv, 0.0)
                    for k in range(j + 1, 8):
                        c[k] = c[k] - f * pivot[k - j]
                    top = jnp.where(at & (sub > j), 0.0, top) - f * row
                if lead:
                    fa = ca[j] * inv
                    for k in range(j + 1, 8):
                        ca[k] = ca[k] - fa * pivot[k - j]
                    after = jnp.where(at, 0.0, after) - fa * row
            rows[t] = top
            if lead:
                rows[t + 1] = after
            if t + 2 < 16:
                packed = jnp.concatenate([s[0:1, :] for s in scaled], axis=0)
                plain = jnp.where(lane == sub + 8 * t, 1.0, jnp.where(inside & (lane > sub + 8 * t), 0.0, top))
                taken = outer(packed, plain)
                for u in range(t + 2, 16):
                    rows[u] = jnp.where(inside, 0.0, rows[u]) - taken[8 * u : 8 * u + 8, :]
    out = []
    for rows in tiles:
        full = []
        for t in range(16):
            diag = lane == sub + 8 * t
            d = jnp.sum(jnp.where(diag, rows[t], 0.0), axis=1, keepdims=True)
            keep = jnp.where(lane < sub + 8 * t, rows[t], jnp.where(diag, 1.0, 0.0))
            full.append(keep * jnp.broadcast_to(1.0 / jnp.sqrt(d), (8, F)))
        out.append(jnp.concatenate(full, axis=0))
    return out


def solve_body(basis_hbm, sum_hbm, tail_hbm, image_hbm, next_ref, ritz_ref, basis_ref, sum_ref, tail_ref, image_ref, mat_ref, inv_ref, loaded, *, total_rows):
    loads = [
        pltpu.make_async_copy(src, dst, loaded.at[n])
        for n, (src, dst) in enumerate(
            ((basis_hbm, basis_ref), (sum_hbm, sum_ref), (tail_hbm, tail_ref), (image_hbm, image_ref))
        )
    ]
    for c in loads:
        c.start()
    for c in loads[:3]:
        c.wait()
    scale = 1.0 / total_rows
    sub = lax.broadcasted_iota(jnp.int32, (F, F), 0)
    lane = lax.broadcasted_iota(jnp.int32, (F, F), 1)

    def unpack(m, half):
        b21 = sum_ref[m * 32 : m * 32 + 16].reshape(F, F) * half
        both = sum_ref[m * 32 + 16 : m * 32 + 32].reshape(F, F) * half
        flip = both.T
        b11 = jnp.where(sub >= lane, both, flip)
        diag = jnp.broadcast_to(tail_ref[m : m + 1, :] * half, (F, F))
        b22 = jnp.where(sub < lane, both, jnp.where(sub == lane, diag, flip))
        return b11, b21, b22

    s21, s11, s22 = [basis_ref[n * 16 : n * 16 + 16].reshape(F, F) * scale for n in range(3)]
    w11, w21, w22 = unpack(1, scale)
    mat_ref[0] = s11
    mat_ref[1] = w11
    for n, (b21, b22) in enumerate(((s21, s22), (w21, w22))):
        mat_ref[2 + 2 * n] = b21
        mat_ref[3 + 2 * n] = b22

    def half_step(step, carry):
        s, w = eliminate([mat_ref[0], mat_ref[1]])
        for n, top in enumerate((s, w)):
            inv_ref[2 * step + n] = top

        @pl.when(step == 0)
        def _():
            for n, top in enumerate((s, w)):
                left = dot32(mat_ref[2 + 2 * n], top, NT)
                mat_ref[n] = mat_ref[3 + 2 * n] - dot32(left, left, NT)
                mat_ref[2 + 2 * n] = left

        return carry

    lax.fori_loop(0, 2, half_step, 0)

    def whole(n):
        top, low = inv_ref[n], inv_ref[2 + n]
        corner = -dot32(low, dot32(mat_ref[2 + 2 * n], top, NN), NN)
        return jnp.concatenate(
            [jnp.concatenate([top, jnp.zeros((F, F), jnp.float32)], axis=1), jnp.concatenate([corner, low], axis=1)], axis=0
        )

    q11, q21, q22 = unpack(0, 0.5 * scale)
    cross_sum = jnp.concatenate([jnp.concatenate([q11, q21.T], axis=1), jnp.concatenate([q21, q22], axis=1)], axis=0)
    s_inv = whole(0)
    ritz_ref[...] = dot32(dot32(s_inv, cross_sum, NN), s_inv, NT)
    w_inv = whole(1)
    loads[3].wait()
    for j in range(6):
        next_ref[:, j * K : (j + 1) * K] = dot32(image_ref[j * F : (j + 1) * F, :], w_inv, NT)


def solve(basis_sum, sums, tail, image, total_rows):
    return pl.pallas_call(
        functools.partial(solve_body, total_rows=total_rows),
        out_shape=(jax.ShapeDtypeStruct((F, 6 * K), jnp.float32), jax.ShapeDtypeStruct((K, K), jnp.float32)),
        in_specs=[pl.BlockSpec(memory_space=pltpu.MemorySpace.HBM)] * 4,
        out_specs=(VM, VM),
        scratch_shapes=[
            pltpu.VMEM((64, 8, F), jnp.float32),
            pltpu.VMEM((64, 8, F), jnp.float32),
            pltpu.VMEM((8, F), jnp.float32),
            pltpu.VMEM((6 * F, K), jnp.float32),
            pltpu.VMEM((6, F, F), jnp.float32),
            pltpu.VMEM((4, F, F), jnp.float32),
            pltpu.SemaphoreType.DMA((4,)),
        ],
        compiler_params=pltpu.CompilerParams(vmem_limit_bytes=66_000_000),
        name="solve",
    )(basis_sum, sums, tail, image)


def per_device(coordinates, neighbours, pair_index, pair_live, basis):
    own = coordinates[0, 0, 0].reshape(48, F)
    live = pair_live[0, 0, 0].reshape(1, -1)
    image, basis_sum, sums, tail = images_and_sums(pair_index[0, 0, 0], live, basis[0, 0, 0], own, neighbours[0, 0, 0])
    next_rows, ritz = solve(basis_sum, sums, tail, image, 6.0 * F * 256)
    return next_rows.reshape(1, 1, 1, F, 6 * K), ritz


def solution(mesh):
    cells = [P("gx", "gy", "gz", *([None] * n)) for n in (3, 2, 2, 1, 2)]
    return jax.shard_map(per_device, mesh=mesh, in_specs=tuple(cells), out_specs=(cells[4], P()), check_vma=False)
```

```python
import functools
import jax
import jax.numpy as jnp
from jax import lax
from jax.experimental import pallas as pl
from jax.experimental.pallas import tpu as pltpu
from jax.sharding import PartitionSpec as P

VM = pl.BlockSpec(memory_space=pltpu.VMEM)
F = 128
K = 256
NB = 16
PB = 4096.0
CHUNK = 3840


def counter(pairs_ref, live_ref, hist_ref):
    rows = lax.broadcasted_iota(jnp.int32, (256, CHUNK), 0)
    zero = jnp.zeros((256, CHUNK), jnp.float32)

    def chunk(c):
        at = slice(c * CHUNK, (c + 1) * CHUNK)
        f = pairs_ref[0:1, at]
        s = pairs_ref[1:2, at]
        a = pairs_ref[2:3, at]
        b = pairs_ref[3:4, at]
        live = live_ref[0:1, at]
        value = (live * jnp.where(a >= 8, int(PB), 1)).astype(jnp.float32)
        col = ((a >> 2) & 1) * 128 + f
        right = jnp.where(rows == col, jnp.broadcast_to(value, (256, CHUNK)), zero).astype(jnp.bfloat16)
        hot = rows == (b * 16 + s)
        low = a & 3
        for part in range(4):
            mark = jnp.broadcast_to((low == part).astype(jnp.float32), (256, CHUNK))
            left = jnp.where(hot, mark, zero).astype(jnp.bfloat16)
            got = lax.dot_general(left, right, (((1,), (1,)), ((), ())), preferred_element_type=jnp.float32)
            high = jnp.floor(got * (1.0 / PB))
            lower = got - PB * high
            for mid in range(2):
                lanes = slice(mid * 128, (mid + 1) * 128)
                for top, val in ((0, lower), (1, high)):
                    a = top * 8 + mid * 4 + part
                    here = slice(a * 256, (a + 1) * 256)
                    if c == 0:
                        hist_ref[here, :] = val[:, lanes]
                    else:
                        hist_ref[here, :] = hist_ref[here, :] + val[:, lanes]

    return chunk


def cross(p, q):
    return [
        p[1] * q[2] - p[2] * q[1],
        p[2] * q[0] - p[0] * q[2],
        p[0] * q[1] - p[1] * q[0],
    ]


SYM = ((0, 0), (0, 1), (0, 2), (1, 1), (1, 2), (2, 2))


def symmetric(six):
    return [[six[0], six[1], six[2]], [six[1], six[3], six[4]], [six[2], six[4], six[5]]]


def moments(hist_ref, coords_ref, q_ref, blk_ref, rr_ref):
    blk_ref[...] = jnp.zeros_like(blk_ref)
    rr_ref[...] = jnp.zeros_like(rr_ref)
    own = [jnp.sum(coords_ref[16 * c : 16 * c + 16, :], axis=0, keepdims=True) * (1.0 / 16.0) for c in range(3)]

    def tile(c, b, half):
        return q_ref[(c * 16 + b) * 16 + half * 8 : (c * 16 + b) * 16 + half * 8 + 8, :]

    centres = []
    for half in range(2):
        centre = []
        for c in range(3):
            total = tile(c, 0, half)
            for b in range(1, 16):
                total = total + tile(c, b, half)
            centre.append(total * (1.0 / 16.0))
        centres.append(centre)

    def atom(a, half):
        centre = centres[half]
        r = [jnp.broadcast_to(coords_ref[pl.ds(c * 16 + a, 1), :], (8, F)) for c in range(3)]
        arm = [r[c] - jnp.broadcast_to(own[c], (8, F)) for c in range(3)]
        m = [None] * 6
        n = [[None] * 3 for _ in range(3)]
        for b in range(16):
            q = [tile(c, b, half) for c in range(3)]
            d = [r[c] - q[c] for c in range(3)]
            count = hist_ref[pl.ds(pl.multiple_of(a * 256 + b * 16 + half * 8, 8), 8), :]
            w = (0.01 * count) / jnp.maximum(d[0] * d[0] + d[1] * d[1] + d[2] * d[2], 1.0)
            wd = [w * d[c] for c in range(3)]
            turn = cross([q[c] - centre[c] for c in range(3)], d)
            for k, (j, i) in enumerate(SYM):
                t = wd[j] * d[i]
                m[k] = t if m[k] is None else m[k] + t
            for j in range(3):
                for i in range(3):
                    t = wd[j] * turn[i]
                    n[j][i] = t if n[j][i] is None else n[j][i] + t
        m = symmetric(m)
        rt = [cross(arm, [m[j][i] for j in range(3)]) for i in range(3)]
        rn = [cross(arm, [n[j][i] for j in range(3)]) for i in range(3)]
        for j in range(3):
            for i in range(3):
                for jj, ii, val in ((j, i, m[j][i]), (j, 3 + i, n[j][i]), (3 + j, i, rt[i][j]), (3 + j, 3 + i, rn[i][j])):
                    here = pl.ds((jj * 6 + ii) * 16 + half * 8, 8)
                    blk_ref[here, :] = blk_ref[here, :] - val
        for j in range(3):
            rr = cross(arm, [rt[i][j] for i in range(3)])
            for i in range(3):
                here = pl.ds((j * 3 + i) * 8, 8)
                rr_ref[here, :] = rr_ref[here, :] + rr[i]

    def both(a, carry):
        for half in range(2):
            atom(a, half)
        return carry

    lax.fori_loop(0, 16, both, 0)
    for j in range(3):
        for i in range(3):
            tt = jnp.sum(blk_ref[pl.ds((j * 6 + i) * 16, 16), :], axis=0, keepdims=True)
            rt = jnp.sum(blk_ref[pl.ds(((3 + j) * 6 + i) * 16, 16), :], axis=0, keepdims=True)
            rr = jnp.sum(rr_ref[pl.ds((j * 3 + i) * 8, 8), :], axis=0, keepdims=True)
            for jj, ii, val in ((j, i, -tt), (3 + j, i, -rt), (i, 3 + j, -rt), (3 + j, 3 + i, rr)):
                here = pl.ds((jj * 6 + ii) * 16, 1)
                rr_ref[72 + jj * 6 + ii : 73 + jj * 6 + ii, :] = val
    for ji in range(36):
        here = pl.ds(ji * 16, 1)
        blk_ref[here, :] = blk_ref[here, :] + rr_ref[72 + ji : 73 + ji, :]


KC = 32


def chosen(table_ref, columns, hot_ref):
    return lax.dot_general(table_ref[:, columns], hot_ref[...], (((0,), (0,)), ((), ())), preferred_element_type=jnp.float32)


def place_partners(ctab_ref, hot_ref, q_ref):
    got = chosen(ctab_ref, slice(0, 256), hot_ref)
    pos = got[0:48] + got[48:96] + got[96:144]
    for s in range(NB):
        for t in range(6):
            q_ref[pl.ds(t * 128 + s, 8, stride=16), :] = pos[t * 8 : t * 8 + 8, s * F : (s + 1) * F]


def apply_blocks(table_ref, hot_ref, image_ref, g_ref, blk_ref, it_ref):
    for part in range(6):
        at = slice(part * K, (part + 1) * K)
        g_ref[at, :] = chosen(table_ref, at, hot_ref)

    def piece(kc, carry):
        start = pl.multiple_of(kc * KC, KC)

        def slot(s, totals):
            totals = list(totals)
            lanes = pl.ds(pl.multiple_of(s * F, F), F)
            for i in range(6):
                g = g_ref[pl.ds(i * K + start, KC), lanes]
                for j in range(6):
                    row = blk_ref[pl.ds((j * 6 + i) * 16 + s, 1), :]
                    totals[j] = totals[j] + jnp.broadcast_to(row, (KC, F)) * g
            return tuple(totals)

        totals = lax.fori_loop(0, NB, slot, tuple(jnp.zeros((KC, F), jnp.float32) for _ in range(6)), unroll=2)
        for j in range(6):
            it_ref[pl.ds(j * K + start, KC), :] = totals[j]
        return carry

    lax.fori_loop(0, K // KC, piece, 0)
    for j in range(6):
        image_ref[j * F : (j + 1) * F, :] = jnp.transpose(it_ref[j * K : (j + 1) * K, :])


MESH = pl.DeviceIdType.MESH


def place():
    gx, gy, gz = lax.axis_index("gx"), lax.axis_index("gy"), lax.axis_index("gz")
    y, z = lax.rem(gx, 4), lax.div(gz, 2) * 2 + lax.div(gx, 4)
    return gy, y, z, lax.rem(gz, 2)


def device(x, y, z, core):
    return {"gx": lax.rem(z, 2) * 4 + y, "gy": x, "gz": lax.div(z, 2) * 2 + core}


PLANE = [(dx, dy) for dx in (2, 1, 3, 0) for dy in (2, 1, 3, 0)][:15]


def sum_peers():
    x, y, z, core = place()
    plane = [device(lax.rem(x + dx, 4), lax.rem(y + dy, 4), z, core) for dx, dy in PLANE]
    along_z = [device(x, y, lax.rem(z + d, 8), core) for d in range(1, 8)]
    return device(x, y, z, 1 - core), plane, along_z


def total_grams(image_ref, basis_ref, out_ref, tail_ref, x_ref, y_ref, data, half_in, half, plane_in, z_in, t1, t3, t4, send, recv):
    x, y, z, core = place()
    partner, plane, along_z = sum_peers()
    for j in range(6):
        x_ref[j * F : (j + 1) * F, :] = basis_ref[:, j * K : (j + 1) * K]
    y_ref[...] = image_ref[...].astype(jnp.bfloat16)

    def gram(left, right):
        return lax.dot_general(left[...], right[...], (((0,), (0,)), ((), ())), preferred_element_type=jnp.float32)

    lower = lax.broadcasted_iota(jnp.int32, (F, F), 0) >= lax.broadcasted_iota(jnp.int32, (F, F), 1)
    eye = lax.broadcasted_iota(jnp.int32, (F, F), 0) == lax.broadcasted_iota(jnp.int32, (F, F), 1)
    t1[0] = jnp.zeros((4, F), jnp.float32)
    for m in range(3):
        both = gram(x_ref if m < 2 else y_ref, x_ref if m < 1 else y_ref)
        b11, b21, b22 = both[:F, :F], both[F:, :F], both[F:, F:]
        if m == 1:
            b11 = b11 + b11.T
            b21 = b21 + both[:F, F:].T
            b22 = b22 + b22.T
        data[m * 32 : m * 32 + 16] = b21.reshape(16, 8, F)
        data[m * 32 + 16 : m * 32 + 32] = jnp.where(lower, b11, b22).reshape(16, 8, F)
        t1[0, m : m + 1, :] = jnp.sum(jnp.where(eye, b22, 0.0), axis=0, keepdims=True)
    count = [0]
    started = []

    def copy(src, dst, peer):
        n = count[0]
        count[0] += 1
        c = pltpu.make_async_remote_copy(src_ref=src, dst_ref=dst, send_sem=send.at[n], recv_sem=recv.at[n], device_id=peer, device_id_type=MESH)
        c.start()
        started.append(c)
        return c

    first = []
    for dx in (2, 1, 3, 0):
        at = lax.rem(x + dx, 4) * 12
        first.append(copy(data.at[pl.ds((1 - core) * 48 + at, 12)], half_in.at[pl.ds(at, 12)], partner))
    small = copy(t1.at[0], t1.at[1], partner)
    arriving = []
    for n, dx in enumerate((2, 1, 3, 0)):
        at = lax.rem(x + dx, 4) * 12
        first[n].wait_recv()
        half[pl.ds(at, 12)] = data[pl.ds(core * 48 + at, 12)] + half_in[pl.ds(at, 12)]
        for slot, (px, py) in enumerate(PLANE):
            if px == dx:
                piece = at + lax.rem(y + py, 4) * 3
                arriving.append(copy(half.at[pl.ds(piece, 3)], plane_in.at[slot], plane[slot]))
    small.wait_recv()
    here = x * 4 + y
    t3[here] = t1[0] + t1[1]
    tails = [copy(t3.at[here], t3.at[here], plane[slot]) for slot in range(15)]
    total = half[pl.ds(here * 3, 3)]
    for slot in range(15):
        arriving[slot].wait_recv()
        total = total + plane_in[slot]
    z_in[z] = total
    arriving = [copy(z_in.at[z], z_in.at[z], along_z[d - 1]) for d in range(1, 8)]
    for c in tails:
        c.wait_recv()
    tail = t3[0]
    for n in range(1, 16):
        tail = tail + t3[n]
    t4[z] = tail
    tails = [copy(t4.at[z], t4.at[z], along_z[d - 1]) for d in range(1, 8)]
    for c in arriving:
        c.wait_recv()
    total = z_in[0]
    for n in range(1, 8):
        total = total + z_in[n]
    mine = core * 48 + here * 3
    out_ref[pl.ds(mine, 3)] = total
    arriving = [copy(out_ref.at[pl.ds(mine, 3)], out_ref.at[pl.ds(mine, 3)], plane[slot]) for slot in range(15)]
    onward = [copy(out_ref.at[pl.ds(mine, 3)], out_ref.at[pl.ds(mine, 3)], partner)]
    for c in tails:
        c.wait_recv()
    tail = t4[0]
    for n in range(1, 8):
        tail = tail + t4[n]
    tail_ref[0:4, :] = tail
    tail_ref[4:8, :] = tail
    for slot in reversed(range(15)):
        dx, dy = PLANE[slot]
        theirs = core * 48 + (lax.rem(x + 4 - dx, 4) * 4 + lax.rem(y + 4 - dy, 4)) * 3
        arriving[slot].wait_recv()
        onward.append(copy(out_ref.at[pl.ds(theirs, 3)], out_ref.at[pl.ds(theirs, 3)], partner))
    for c in onward:
        c.wait_recv()
    for c in started:
        c.wait_send()


def image_body(
    pairs_hbm, live_hbm, basis_hbm, coords_hbm, lists_hbm, image_ref, sum_ref, tail_ref,
    pairs_ref, live_ref, coords_ref, lists_ref, hist_ref, table_ref, ctab_ref, hot_ref, q_ref, g_ref, blk_ref, rr_ref, it_ref,
    x_ref, y_ref, data, half_in, half, plane_in, z_in, t1, t3, t4, loaded, send, recv, sum_send, sum_recv,
):
    own = 27 * 32
    loads = [
        pltpu.make_async_copy(src, dst, loaded.at[n])
        for n, (src, dst) in enumerate(
            (
                (coords_hbm, coords_ref),
                (basis_hbm, table_ref.at[pl.ds(own, F)]),
                (pairs_hbm, pairs_ref),
                (live_hbm, live_ref),
                (lists_hbm, lists_ref),
            )
        )
    ]
    for c in loads:
        c.start()
    gx, gy, gz = lax.axis_index("gx"), lax.axis_index("gy"), lax.axis_index("gz")
    core = lax.rem(gz, 2)
    far = 2 * core
    partner = {"gz": gz + 1 - 2 * core}
    beyond = {"gz": lax.rem(gz + 7 + 2 * core, 8)}
    up_x, down_x = {"gy": lax.rem(gy + 1, 4)}, {"gy": lax.rem(gy + 3, 4)}
    up_y, down_y = {"gx": lax.rem(gx + 1, 8)}, {"gx": lax.rem(gx + 7, 8)}
    other, plane, along_z = sum_peers()
    barrier = pltpu.get_barrier_semaphore()
    for peer in [partner, beyond, up_x, down_x, up_y, down_y, other] + plane + along_z:
        pl.semaphore_signal(barrier, inc=1, device_id=peer, device_id_type=MESH)

    loads[0].wait()
    flat = coords_ref[...]
    high = flat.astype(jnp.bfloat16).astype(jnp.float32)
    mid = (flat - high).astype(jnp.bfloat16).astype(jnp.float32)
    parts = jnp.concatenate([high, mid, flat - high - mid, jnp.zeros((112, F), jnp.float32)], axis=0)
    ctab_ref[own : own + F, :] = jnp.transpose(parts).astype(jnp.bfloat16)
    ctab_ref[13 * 32 : 14 * 32, :] = ctab_ref[own : own + 32, :]
    loads[1].wait()
    table_ref[13 * 32 : 14 * 32, :] = table_ref[own : own + 32, :]
    pl.semaphore_wait(barrier, 29)

    count = [0]
    started = []

    def copy(src, dst, peer):
        n = count[0]
        count[0] += 1
        c = pltpu.make_async_remote_copy(src_ref=src, dst_ref=dst, send_sem=send.at[n], recv_sem=recv.at[n], device_id=peer, device_id_type=MESH)
        c.start()
        started.append(c)
        return c

    edges, corners = ((1, 0), (1, 2), (0, 1), (2, 1)), ((0, 0), (2, 2), (0, 2), (2, 0))

    class Ghosts:
        def __init__(self, ref):
            self.ref = ref

        def slab(self, a, b, e):
            return self.ref.at[pl.ds(pl.multiple_of((9 * a + 3 * b + e) * 32, 32), 32)]

        def first_hops(self, e):
            return [copy(self.slab(1, 1, e), self.slab(a, b, e), peer) for (a, b), peer in zip(edges, (up_x, down_x, up_y, down_y))]

        def second_hops(self, e):
            return [
                copy(self.slab(a, b, e), self.slab(c, d, e), peer)
                for (a, b), (c, d), peer in zip(edges, corners, (up_y, down_y, down_x, up_x))
            ]

        def forward(self, places):
            return [copy(self.slab(a, b, 1), self.slab(a, b, far), partner) for a, b in places]

        def one(self):
            beyond_copy = copy(self.slab(1, 1, 1), self.slab(1, 1, 2 - far), beyond)
            self.due = [beyond_copy] + self.first_hops(1)
            self.rest = [copy(self.slab(1, 1, 1), self.slab(1, 1, far), partner)]

        def two(self):
            for c in self.due:
                c.wait_recv()
            self.due = self.first_hops(far) + self.second_hops(1)
            self.rest = self.rest + self.forward(edges)

        def three(self):
            for c in self.due:
                c.wait_recv()
            self.rest = self.rest + self.second_hops(far) + self.forward(corners)

        def done(self):
            for c in self.rest:
                c.wait_recv()

    near, rows = Ghosts(ctab_ref), Ghosts(table_ref)
    near.one()
    rows.one()
    chunk = counter(pairs_ref, live_ref, hist_ref)
    loads[2].wait()
    loads[3].wait()
    chunk(0)
    near.two()
    chunk(1)
    near.three()
    rows.two()
    chunk(2)
    chunk(3)
    loads[4].wait()
    for s in range(NB):
        listed = jnp.broadcast_to(lists_ref[s : s + 1, :], (own + F, F))
        hot = lax.broadcasted_iota(jnp.int32, (own + F, F), 0) == listed
        hot_ref[:, s * F : (s + 1) * F] = jnp.where(hot, 1.0, 0.0).astype(jnp.bfloat16)
    rows.three()
    near.done()
    place_partners(ctab_ref, hot_ref, q_ref)
    moments(hist_ref, coords_ref, q_ref, blk_ref, rr_ref)
    rows.done()
    for c in started:
        c.wait_send()
    apply_blocks(table_ref, hot_ref, image_ref, g_ref, blk_ref, it_ref)
    total_grams(
        image_ref, table_ref.at[pl.ds(own, F)], sum_ref, tail_ref, x_ref, y_ref,
        data, half_in, half, plane_in, z_in, t1, t3, t4, sum_send, sum_recv,
    )


def images_and_sums(pairs, live, basis, coords, lists):
    rows = 27 * 32 + F

    def wide(*shape):
        return pltpu.VMEM(shape, jnp.float32)

    def half_wide(*shape):
        return pltpu.VMEM(shape, jnp.bfloat16)

    def semaphores(n):
        return pltpu.SemaphoreType.DMA((n,))

    return pl.pallas_call(
        image_body,
        out_shape=(
            jax.ShapeDtypeStruct((6 * F, K), jnp.float32),
            jax.ShapeDtypeStruct((96, 8, F), jnp.float32),
            jax.ShapeDtypeStruct((8, F), jnp.float32),
        ),
        in_specs=[pl.BlockSpec(memory_space=pltpu.MemorySpace.HBM)] * 5,
        out_specs=(VM, VM, VM),
        scratch_shapes=[
            pltpu.VMEM(pairs.shape, jnp.int32),
            pltpu.VMEM(live.shape, jnp.int32),
            wide(48, F),
            pltpu.VMEM((NB, F), jnp.int32),
            wide(4096, F),
            half_wide(rows, 6 * K),
            half_wide(rows, K),
            half_wide(rows, NB * F),
            wide(768, F),
            wide(6 * K, NB * F),
            wide(576, F),
            wide(112, F),
            wide(6 * K, F),
            half_wide(6 * F, K),
            half_wide(6 * F, K),
            wide(96, 8, F),
            wide(48, 8, F),
            wide(48, 8, F),
            wide(15, 3, 8, F),
            wide(8, 3, 8, F),
            wide(2, 4, F),
            wide(16, 4, F),
            wide(8, 4, F),
            semaphores(5),
            semaphores(52),
            semaphores(52),
            semaphores(80),
            semaphores(80),
        ],
        compiler_params=pltpu.CompilerParams(collective_id=2, has_side_effects=True, vmem_limit_bytes=66_000_000),
        cost_estimate=pl.CostEstimate(flops=16 * 10**9, bytes_accessed=3 * 10**6, transcendentals=0),
        name="images_and_sums",
    )(pairs, live, basis, coords, lists)


def dot32(p, q, dims):
    return lax.dot_general(p, q, (dims, ((), ())), precision=lax.Precision.HIGHEST, preferred_element_type=jnp.float32)


NT = ((1,), (1,))
NN = ((1,), (0,))


def cut(x):
    high = x.astype(jnp.bfloat16)
    rest = x - high.astype(jnp.float32)
    mid = rest.astype(jnp.bfloat16)
    return high, mid, (rest - mid.astype(jnp.float32)).astype(jnp.bfloat16)


def outer(p, q):
    ph, pm, pl_ = cut(p)
    qh, qm, ql = cut(q)
    left = jnp.concatenate([ph, ph, pm, ph, pl_, pm], axis=0)
    right = jnp.concatenate([qh, qm, qh, ql, qh, qm], axis=0)
    return lax.dot_general(left, right, (((0,), (0,)), ((), ())), preferred_element_type=jnp.float32)


def eliminate(mats):
    sub = lax.broadcasted_iota(jnp.int32, (8, F), 0)
    lane = lax.broadcasted_iota(jnp.int32, (8, F), 1)
    tiles = [[m[8 * t : 8 * t + 8, :] for t in range(16)] for m in mats]

    def columns(tile, t):
        return [jnp.broadcast_to(tile[:, 8 * t + k : 8 * t + k + 1], (8, F)) for k in range(8)]

    def spread(tile, r):
        return jnp.broadcast_to(tile[r : r + 1, :], (8, F))

    for t in range(16):
        inside = (lane >= 8 * t) & (lane < 8 * t + 8)
        for rows in tiles:
            top = rows[t]
            c = columns(top, t)
            lead = t + 1 < 16
            if lead:
                after = rows[t + 1]
                ca = columns(after, t)
            scaled = []
            for j in range(8):
                at = lane == 8 * t + j
                pivot = [spread(c[k], j) for k in range(j, 8)]
                inv = 1.0 / pivot[0]
                row = jnp.where(at, 1.0, spread(top, j))
                scaled.append(row * inv)
                if j < 7:
                    f = jnp.where(sub > j, c[j] * inv, 0.0)
                    for k in range(j + 1, 8):
                        c[k] = c[k] - f * pivot[k - j]
                    top = jnp.where(at & (sub > j), 0.0, top) - f * row
                if lead:
                    fa = ca[j] * inv
                    for k in range(j + 1, 8):
                        ca[k] = ca[k] - fa * pivot[k - j]
                    after = jnp.where(at, 0.0, after) - fa * row
            rows[t] = top
            if lead:
                rows[t + 1] = after
            if t + 2 < 16:
                packed = jnp.concatenate([s[0:1, :] for s in scaled], axis=0)
                plain = jnp.where(lane == sub + 8 * t, 1.0, jnp.where(inside & (lane > sub + 8 * t), 0.0, top))
                taken = outer(packed, plain)
                for u in range(t + 2, 16):
                    rows[u] = jnp.where(inside, 0.0, rows[u]) - taken[8 * u : 8 * u + 8, :]
    out = []
    for rows in tiles:
        full = []
        for t in range(16):
            diag = lane == sub + 8 * t
            d = jnp.sum(jnp.where(diag, rows[t], 0.0), axis=1, keepdims=True)
            keep = jnp.where(lane < sub + 8 * t, rows[t], jnp.where(diag, 1.0, 0.0))
            full.append(keep * jnp.broadcast_to(1.0 / jnp.sqrt(d), (8, F)))
        out.append(jnp.concatenate(full, axis=0))
    return out


def solve_body(sum_hbm, tail_hbm, image_hbm, next_ref, ritz_ref, sum_ref, tail_ref, image_ref, mat_ref, inv_ref, loaded, *, total_rows):
    loads = [
        pltpu.make_async_copy(src, dst, loaded.at[n])
        for n, (src, dst) in enumerate(((sum_hbm, sum_ref), (tail_hbm, tail_ref), (image_hbm, image_ref)))
    ]
    for c in loads:
        c.start()
    loads[0].wait()
    loads[1].wait()
    scale = 1.0 / total_rows
    sub = lax.broadcasted_iota(jnp.int32, (F, F), 0)
    lane = lax.broadcasted_iota(jnp.int32, (F, F), 1)

    def unpack(m, half):
        b21 = sum_ref[m * 32 : m * 32 + 16].reshape(F, F) * half
        both = sum_ref[m * 32 + 16 : m * 32 + 32].reshape(F, F) * half
        flip = both.T
        b11 = jnp.where(sub >= lane, both, flip)
        diag = jnp.broadcast_to(tail_ref[m : m + 1, :] * half, (F, F))
        b22 = jnp.where(sub < lane, both, jnp.where(sub == lane, diag, flip))
        return b11, b21, b22

    s11, s21, s22 = unpack(0, scale)
    w11, w21, w22 = unpack(2, scale)
    mat_ref[0] = s11
    mat_ref[1] = w11
    for n, (b21, b22) in enumerate(((s21, s22), (w21, w22))):
        mat_ref[2 + 2 * n] = b21
        mat_ref[3 + 2 * n] = b22

    def half_step(step, carry):
        s, w = eliminate([mat_ref[0], mat_ref[1]])
        for n, top in enumerate((s, w)):
            inv_ref[2 * step + n] = top

        @pl.when(step == 0)
        def _():
            for n, top in enumerate((s, w)):
                left = dot32(mat_ref[2 + 2 * n], top, NT)
                mat_ref[n] = mat_ref[3 + 2 * n] - dot32(left, left, NT)
                mat_ref[2 + 2 * n] = left

        return carry

    lax.fori_loop(0, 2, half_step, 0)

    def whole(n):
        top, low = inv_ref[n], inv_ref[2 + n]
        corner = -dot32(low, dot32(mat_ref[2 + 2 * n], top, NN), NN)
        return jnp.concatenate(
            [jnp.concatenate([top, jnp.zeros((F, F), jnp.float32)], axis=1), jnp.concatenate([corner, low], axis=1)], axis=0
        )

    q11, q21, q22 = unpack(1, 0.5 * scale)
    cross_sum = jnp.concatenate([jnp.concatenate([q11, q21.T], axis=1), jnp.concatenate([q21, q22], axis=1)], axis=0)
    s_inv = whole(0)
    ritz_ref[...] = dot32(dot32(s_inv, cross_sum, NN), s_inv, NT)
    w_inv = whole(1)
    loads[2].wait()
    for j in range(6):
        next_ref[:, j * K : (j + 1) * K] = dot32(image_ref[j * F : (j + 1) * F, :], w_inv, NT)


def solve(sums, tail, image, total_rows):
    return pl.pallas_call(
        functools.partial(solve_body, total_rows=total_rows),
        out_shape=(jax.ShapeDtypeStruct((F, 6 * K), jnp.float32), jax.ShapeDtypeStruct((K, K), jnp.float32)),
        in_specs=[pl.BlockSpec(memory_space=pltpu.MemorySpace.HBM)] * 3,
        out_specs=(VM, VM),
        scratch_shapes=[
            pltpu.VMEM((96, 8, F), jnp.float32),
            pltpu.VMEM((8, F), jnp.float32),
            pltpu.VMEM((6 * F, K), jnp.float32),
            pltpu.VMEM((6, F, F), jnp.float32),
            pltpu.VMEM((4, F, F), jnp.float32),
            pltpu.SemaphoreType.DMA((3,)),
        ],
        compiler_params=pltpu.CompilerParams(vmem_limit_bytes=66_000_000),
        name="solve",
    )(sums, tail, image)


def per_device(coordinates, neighbours, pair_index, pair_live, basis):
    own = coordinates[0, 0, 0].reshape(48, F)
    live = pair_live[0, 0, 0].reshape(1, -1)
    image, sums, tail = images_and_sums(pair_index[0, 0, 0], live, basis[0, 0, 0], own, neighbours[0, 0, 0])
    next_rows, ritz = solve(sums, tail, image, 6.0 * F * 256)
    return next_rows.reshape(1, 1, 1, F, 6 * K), ritz


def solution(mesh):
    cells = [P("gx", "gy", "gz", *([None] * n)) for n in (3, 2, 2, 1, 2)]
    return jax.shard_map(per_device, mesh=mesh, in_specs=tuple(cells), out_specs=(cells[4], P()), check_vma=False)
```
